32 devices in a mesh: ctx: 8 (over y, x, core), wsh: 4 (over z).
Axes of the slice: x: 2, y: 2, z: 4, core: 2. Of those that a mesh axis runs over, the one named last changes fastest.
Arguments:
- tokens: bfloat16 [4, 2048, 768], P('wsh', 'ctx'), may hold values from -6 to 6
- chars: bfloat16 [4, 8192, 768], P('wsh', 'ctx'), may hold values from -6 to 6
- char_token: int32 [4, 8, 1024], P('wsh', 'ctx'), may hold values from 0 to 255, never falling along the last dimension, each value on 1 to 8 neighbouring positions
- doc_lengths: int32 [4, 8], P('wsh'), may hold values from 1 to 1024, 2048 in all within a row
- gain_attn: bfloat16 [768], P(('ctx', 'wsh')), may hold values from 0.5 to 1.5
- qkv_weight: bfloat16 [768, 2304], P(('ctx', 'wsh')), may hold values from -0.21875 to 0.21875
- out_weight: bfloat16 [768, 768], P(('ctx', 'wsh')), may hold values from -0.21875 to 0.21875
- gain_char: bfloat16 [768], P(('ctx', 'wsh')), may hold values from 0.5 to 1.5
- gru_weight: bfloat16 [768, 1536], P(('ctx', 'wsh')), may hold values from -0.21875 to 0.21875
- conv_weight: bfloat16 [768, 2304], P(('ctx', 'wsh')), may hold values from -0.21875 to 0.21875
- gain_merge: bfloat16 [768], P(('ctx', 'wsh')), may hold values from 0.5 to 1.5
- merge_weight: bfloat16 [768, 768], P(('ctx', 'wsh')), may hold values from -0.21875 to 0.21875
- up_weight: bfloat16 [768, 3072], P(('ctx', 'wsh')), may hold values from -0.21875 to 0.21875
- down_weight: bfloat16 [3072, 768], P(('ctx', 'wsh')), may hold values from -0.109375 to 0.109375
- cot_tokens: bfloat16 [4, 2048, 768], P('wsh', 'ctx'), may hold values from -6 to 6
- cot_chars: bfloat16 [4, 8192, 768], P('wsh', 'ctx'), may hold values from -6 to 6
Outputs:
- out_tokens: bfloat16 [4, 2048, 768], P('wsh', 'ctx')
- out_chars: bfloat16 [4, 8192, 768], P('wsh', 'ctx')
- grad_tokens: bfloat16 [4, 2048, 768], P('wsh', 'ctx')
- grad_chars: bfloat16 [4, 8192, 768], P('wsh', 'ctx')
- grad_gain_attn: float32 [768], P(('ctx', 'wsh'))
- grad_qkv: float32 [768, 2304], P(('ctx', 'wsh'))
- grad_out_proj: float32 [768, 768], P(('ctx', 'wsh'))
- grad_gain_char: float32 [768], P(('ctx', 'wsh'))
- grad_gru: float32 [768, 1536], P(('ctx', 'wsh'))
- grad_conv: float32 [768, 2304], P(('ctx', 'wsh'))
- grad_gain_merge: float32 [768], P(('ctx', 'wsh'))
- grad_merge: float32 [768, 768], P(('ctx', 'wsh'))
- grad_up: float32 [768, 3072], P(('ctx', 'wsh'))
- grad_down: float32 [3072, 768], P(('ctx', 'wsh'))
The draws below stay inside these ranges and needn't reach their ends.
Inputs may be any that keep to these rules, and one draw needn't show every extreme that they name: `char_token`: each block of 1024 characters names its 256 tokens in order, each by 1 to 8 consecutive characters. `doc_lengths`: a sequence's document lengths sum to 2048.
All inputs are finite; a program needn't handle non-finite values.
Results may differ from the reference program's by a relative error of at most 0.02.
Values may be sent and summed in bfloat16 or wider, within the bound.
A program may use at most 320 MiB of HBM per device.

```python
import math
import jax
import jax.numpy as jnp
import numpy as np
from jax import lax

D = 768
HEADS = 12
HEAD_DIM = 64
FF = 3072
TOK_DEV = 256
WORD_MAX = 8
CH_DEV = 1024
SEQ = 2048
CHARS = 8192
DOC_MAX = 1024
NDOCS = 8
BATCH = 4
N_CTX = 8
N_WSH = 4


def token_base(key):
    return jax.random.normal(jax.random.fold_in(key, 101), (BATCH, SEQ, D), jnp.float32)


def token_ramp():
    place = jnp.arange(SEQ, dtype=jnp.float32) / (SEQ - 1)
    return 0.5 + 1.5 * place


def draw_tokens(key, part):
    scaled = token_base(key) * token_ramp()[None, :, None]
    return jnp.clip(scaled, -6.0, 6.0).astype(jnp.bfloat16)


def draw_cot_tokens(key, part):
    noise = jax.random.normal(jax.random.fold_in(key, 202), (BATCH, SEQ, D), jnp.float32)
    return jnp.clip(0.6 * token_base(key) + 0.8 * noise, -6.0, 6.0).astype(jnp.bfloat16)


def shard_levels(own_key, shape, cuts, smallest, largest):
    def one(dim, blocks):
        heights = jax.random.uniform(jax.random.fold_in(jax.random.fold_in(own_key, 6), dim), (blocks,), jnp.float32, smallest / len(cuts), largest / len(cuts))
        return jnp.repeat(jnp.exp(heights), shape[dim] // blocks).reshape((-1,) + (1,) * (len(shape) - dim - 1))

    factor_of = one(*cuts[0])
    for cut in cuts[1:]:
        factor_of = factor_of * one(*cut)
    return factor_of


def profile(count, total, bound, skew):
    weights = [(1 << 20) // math.isqrt(standing ** skew) + 1 for standing in range(2, count + 1)]
    surplus, given = total - bound - (count - 1), [1] * (count - 1)
    while surplus > 0:
        candidates = [i for i in range(count - 1) if given[i] < bound]
        whole, left = sum([weights[i] for i in candidates]), surplus
        for i in candidates:
            more = min(bound - given[i], max(1, left * weights[i] // whole), surplus)
            given[i] = given[i] + more
            surplus = surplus - more
    return np.array([bound] + given)


def uneven(own_key, number_of, total, limit, lean):
    if number_of == 2:
        one = jax.random.randint(own_key, (), max(1, total - limit), min(limit, total - 1) + 1)
        return jnp.stack([one, total - one])
    tallies = jnp.asarray(profile(number_of, total, limit, lean), jnp.int32)
    twos = (number_of - 1) // 2
    donor, receiver = tallies[1:1 + 2 * twos:2], tallies[2:2 + 2 * twos:2]
    room = jnp.minimum(donor - 1, limit - receiver)
    passed = jax.random.randint(jax.random.fold_in(own_key, 1), (twos,), 0, 1 << 20) % (room + 1)
    tallies = tallies.at[1:1 + 2 * twos:2].set(donor - passed).at[2:2 + 2 * twos:2].set(receiver + passed)
    return tallies[jax.random.permutation(jax.random.fold_in(own_key, 2), number_of)]


def normal_values(key, dims, scale, most, cuts=(), held_as=jnp.bfloat16):
    loudness = shard_levels(key, dims, cuts, -0.22, 0.18) if cuts else 1.0
    drawn = jax.random.normal(key, dims, jnp.float32) * scale * loudness
    return jnp.minimum(jnp.maximum(drawn, -most), most).astype(held_as)


def setup_inputs(seed: int = 0) -> dict:
    key_of = jax.random.split(jax.random.key(seed), 17)
    return {
        "tokens": draw_tokens(jax.random.fold_in(key_of[16], 71), 0),
        "chars": normal_values(key_of[1], (BATCH, CHARS, D), 1.0, 6.0, ((0, 4), (1, 8))),
        "char_token": jax.vmap(lambda own: jnp.searchsorted(jnp.cumsum(uneven(own, TOK_DEV, CH_DEV, WORD_MAX, 1)), jnp.arange(CH_DEV), side="right"))(jax.random.split(key_of[2], BATCH * N_CTX)).reshape((BATCH, N_CTX, CH_DEV)).astype(jnp.int32),
        "doc_lengths": jax.vmap(lambda own: uneven(own, NDOCS, SEQ, DOC_MAX, 2))(jax.random.split(key_of[3], BATCH)).reshape((BATCH, NDOCS)).astype(jnp.int32),
        "gain_attn": jnp.clip(1.0 + 0.1 * jax.random.normal(key_of[4], (D,), jnp.float32), 0.5, 1.5).astype(jnp.bfloat16),
        "qkv_weight": normal_values(key_of[5], (D, 3 * D), D ** -0.5, 0.21875, ((0, 32),)),
        "out_weight": normal_values(key_of[6], (D, D), D ** -0.5, 0.21875, ((0, 32),)),
        "gain_char": jnp.clip(1.0 + 0.1 * jax.random.normal(key_of[7], (D,), jnp.float32), 0.5, 1.5).astype(jnp.bfloat16),
        "gru_weight": normal_values(key_of[8], (D, 2 * D), D ** -0.5, 0.21875, ((0, 32),)),
        "conv_weight": normal_values(key_of[9], (D, 3 * D), D ** -0.5, 0.21875, ((0, 32),)),
        "gain_merge": jnp.clip(1.0 + 0.1 * jax.random.normal(key_of[10], (D,), jnp.float32), 0.5, 1.5).astype(jnp.bfloat16),
        "merge_weight": normal_values(key_of[11], (D, D), D ** -0.5, 0.21875, ((0, 32),)),
        "up_weight": normal_values(key_of[12], (D, FF), D ** -0.5, 0.21875, ((0, 32),)),
        "down_weight": normal_values(key_of[13], (FF, D), FF ** -0.5, 0.109375, ((0, 32),)),
        "cot_tokens": draw_cot_tokens(jax.random.fold_in(key_of[16], 71), 0),
        "cot_chars": normal_values(key_of[15], (BATCH, CHARS, D), 1.0, 6.0, ((0, 4), (1, 8))),
    }


@jax.custom_vjp
def low(v):
    return lax.optimization_barrier(v.astype(jnp.bfloat16)).astype(jnp.float32)

@jax.custom_vjp
def low_back(v):
    return v

def low_keep(v):
    return (low(v), None)

def low_pass(kept, grad):
    return (grad,)

def back_keep(v):
    return (v, None)

def back_low(kept, grad):
    return (low(grad),)
low.defvjp(low_keep, low_pass)
low_back.defvjp(back_keep, back_low)

def normed(values, scales):
    average = lax.optimization_barrier(jnp.mean(values, axis=-1, keepdims=True))
    centred = values - average
    spread = lax.optimization_barrier(jnp.mean(centred * centred, axis=-1, keepdims=True))
    return centred * lax.rsqrt(spread + 1e-05) * scales

def matmul(left, right):
    return jnp.dot(left, right, precision=lax.Precision.HIGHEST, preferred_element_type=jnp.float32)

def gelu_exact(values):
    return jax.nn.gelu(values, approximate=False)

def linear_step(former, latter):
    return (former[0] * latter[0], latter[0] * former[1] + latter[1])

def doc_index(positions, starts):
    return lax.optimization_barrier(jnp.sum((starts[None, :] <= positions[:, None]).astype(jnp.int32), axis=1)) - 1

def attend(queries, keys, values, token_docs):
    seq_len = queries.shape[0]
    block = min(seq_len, 512)
    blocks = seq_len // block
    scale = HEAD_DIM ** (-0.5)
    key_heads = keys.reshape(seq_len, HEADS, HEAD_DIM)
    value_heads = values.reshape(seq_len, HEADS, HEAD_DIM)

    def one_block(inputs):
        query_blk, docs_blk = inputs
        scores = jnp.einsum('qhe,khe->hqk', query_blk, key_heads, precision=lax.Precision.HIGHEST) * scale
        scores = low_back(scores)
        allowed = docs_blk[None, :, None] == token_docs[None, None, :]
        masked = jnp.where(allowed, scores, -1e+30)
        peak = lax.optimization_barrier(jnp.max(masked, axis=2, keepdims=True))
        expd = jnp.where(allowed, jnp.exp(masked - peak), 0.0)
        probs = low(expd / lax.optimization_barrier(jnp.sum(expd, axis=2, keepdims=True)))
        result = jnp.einsum('hqk,khe->qhe', probs, value_heads, precision=lax.Precision.HIGHEST)
        return result.reshape(block, HEADS * HEAD_DIM)
    outputs = lax.map(jax.checkpoint(one_block), (queries.reshape(blocks, block, HEADS, HEAD_DIM), token_docs.reshape(blocks, block)))
    return outputs.reshape(seq_len, HEADS * HEAD_DIM)

def sequence_layer(weights, token_in, char_in, token_docs, char_map, keep_fwd, keep_bwd, counts):
    attn_gain, qkv_full, out_full, char_gain, gru_full, conv_full, merge_gain, merge_full, up_full, down_full = weights
    width = token_in.shape[1]
    half_width = width // 2
    seq_len = token_in.shape[0]
    attn_in = low(normed(token_in, attn_gain))
    qkv = low(low_back(matmul(attn_in, qkv_full)))
    attn_f = attend(qkv[:, :width], qkv[:, width:2 * width], qkv[:, 2 * width:], token_docs)
    attn = low(low_back(attn_f))
    proj = low_back(matmul(attn, out_full))
    rms_scale = lax.rsqrt(jnp.mean(proj * proj) + 1e-06)
    stream = token_in + proj * rms_scale
    stream_scale = lax.rsqrt(jnp.mean(stream * stream) + 1e-06)
    resid = stream * stream_scale
    char_low = low(normed(char_in, char_gain))
    gates = low_back(matmul(char_low, gru_full))
    ramp = jnp.arange(half_width, dtype=jnp.float32) / (half_width - 1)
    shift = (1.0 + math.log(CHARS)) * ramp
    lift = jnp.exp(0.5 * shift)
    zeta_f = jax.nn.sigmoid(gates[:, :half_width] - shift)
    cand_f = gates[:, half_width:2 * half_width] * lift
    zeta_b = jax.nn.sigmoid(gates[:, 2 * half_width:3 * half_width] - shift)
    cand_b = gates[:, 3 * half_width:] * lift
    state_f = lax.associative_scan(linear_step, ((1.0 - zeta_f) * keep_fwd[:, None], zeta_f * cand_f))[1]
    state_b = lax.associative_scan(linear_step, ((1.0 - zeta_b) * keep_bwd[:, None], zeta_b * cand_b), reverse=True)[1]
    mixed = low(jnp.concatenate([state_f, state_b], axis=1))
    out_chars = char_in + mixed
    pooled = low(jax.ops.segment_sum(mixed, char_map, num_segments=seq_len) / jnp.sqrt(counts)[:, None])
    padded = jnp.pad(pooled, ((1, 1), (0, 0)))
    conv_out = matmul(padded[0:seq_len], conv_full[:, 0:width])
    conv_out = conv_out + matmul(padded[1:seq_len + 1], conv_full[:, width:2 * width])
    conv_out = conv_out + matmul(padded[2:seq_len + 2], conv_full[:, 2 * width:])
    merge_in = low(normed(resid, merge_gain))
    merge_pre = low_back(matmul(merge_in, merge_full) + conv_out)
    merged = low(gelu_exact(merge_pre))
    up_pre = low_back(matmul(merged, up_full))
    up_act = low(gelu_exact(up_pre))
    out_tokens = resid + matmul(up_act, down_full)
    return (out_tokens, out_chars)

def reference(tokens, chars, char_token, doc_lengths, gain_attn, qkv_weight, out_weight, gain_char, gru_weight, conv_weight, gain_merge, merge_weight, up_weight, down_weight, cot_tokens, cot_chars):
    params = tuple((member.astype(jnp.float32) for member in (gain_attn, qkv_weight, out_weight, gain_char, gru_weight, conv_weight, gain_merge, merge_weight, up_weight, down_weight)))
    positions = jnp.arange(SEQ, dtype=jnp.int32)
    offsets = (jnp.arange(N_CTX, dtype=jnp.int32) * TOK_DEV)[:, None]
    grad_sum = tuple((jnp.zeros_like(member) for member in params))
    token_outs = []
    char_outs = []
    token_grads = []
    char_grads = []
    for batch_index in range(N_WSH):
        lengths = doc_lengths[batch_index]
        starts = jnp.cumsum(lengths) - lengths
        token_docs = doc_index(positions, starts)
        doc_first = jnp.any(starts[None, :] == positions[:, None], axis=1)
        doc_last = jnp.any(starts[None, :] == positions[:, None] + 1, axis=1)
        char_map = (char_token[batch_index] + offsets).reshape(-1).astype(jnp.int32)
        boundary = char_map[1:] != char_map[:-1]
        first_char = jnp.concatenate([jnp.ones((1,), bool), boundary])
        last_char = jnp.concatenate([boundary, jnp.ones((1,), bool)])
        keep_fwd = 1.0 - (first_char & doc_first[char_map]).astype(jnp.float32)
        keep_bwd = 1.0 - (last_char & doc_last[char_map]).astype(jnp.float32)
        counts = jax.ops.segment_sum(jnp.ones(char_map.shape, jnp.float32), char_map, num_segments=SEQ)

        def forward(weights, token_in, char_in):
            return sequence_layer(weights, token_in, char_in, token_docs, char_map, keep_fwd, keep_bwd, counts)
        outputs, pullback = jax.vjp(forward, params, tokens[batch_index].astype(jnp.float32), chars[batch_index].astype(jnp.float32))
        grad_weights, grad_tok, grad_chr = pullback((cot_tokens[batch_index].astype(jnp.float32), cot_chars[batch_index].astype(jnp.float32)))
        grad_sum = tuple((total + extra for total, extra in zip(grad_sum, grad_weights)))
        token_outs.append(outputs[0])
        char_outs.append(outputs[1])
        token_grads.append(grad_tok)
        char_grads.append(grad_chr)
    return (jnp.stack(token_outs).astype(jnp.bfloat16), jnp.stack(char_outs).astype(jnp.bfloat16), jnp.stack(token_grads).astype(jnp.bfloat16), jnp.stack(char_grads).astype(jnp.bfloat16), grad_sum[0], grad_sum[1], grad_sum[2], grad_sum[3], grad_sum[4], grad_sum[5], grad_sum[6], grad_sum[7], grad_sum[8], grad_sum[9])
```

```python
import functools
import math

import jax
import jax.numpy as jnp
from jax import lax
from jax.experimental import pallas as pl
from jax.experimental.pallas import tpu as pltpu
from jax.sharding import PartitionSpec as P

HEADS = 12
HEAD_DIM = 64


masked_score = -1e30


def masks_of(axis):
    return [1 << k for k in range(lax.axis_size(axis).bit_length() - 1)]


def swapped(value, axis, mask):
    count = lax.axis_size(axis)
    return lax.ppermute(value, axis, [(i, i ^ mask) for i in range(count)])


def bit_set(axis, mask):
    return (lax.axis_index(axis) & mask) != 0


def hop_order(axes, upward):
    places, dim = {}, 0
    for axis in axes:
        for mask in reversed(masks_of(axis)):
            places[axis, mask] = dim
            dim = dim + 1
    middle = [("ctx", mask) for mask in masks_of("ctx")[1:]]
    hops = [("wsh", mask) for mask in masks_of("wsh")] if "wsh" in axes else []
    hops = hops + (middle if upward else middle[::-1]) + [("ctx", 1)]
    return [(axis, mask, places[axis, mask]) for axis, mask in hops], dim


def gathered(shard, axes, upward):
    hops, dims = hop_order(axes, upward)
    block = shard.reshape((1,) * dims + shard.shape)
    for axis, mask, dim in hops:
        other = swapped(block, axis, mask)
        high = bit_set(axis, mask)
        block = jnp.concatenate(
            [jnp.where(high, other, block), jnp.where(high, block, other)], axis=dim
        )
    return block.reshape((-1,) + shard.shape[1:])


def scattered(value, axes, upward, last):
    hops, dims = hop_order(axes, upward)
    rows = value.shape[0] >> dims
    block = value.reshape((2,) * dims + (rows,) + value.shape[1:])
    for axis, mask, dim in hops[::-1]:
        high = bit_set(axis, mask).astype(jnp.int32)
        away = lax.dynamic_index_in_dim(block, 1 - high, dim, keepdims=True)
        kept = lax.dynamic_index_in_dim(block, high, dim, keepdims=True)
        other = swapped(away, axis, mask)
        block = kept.astype(jnp.float32) + other.astype(jnp.float32)
        if (axis, mask, dim) != hops[0]:
            block = block.astype(jnp.bfloat16)
    return block.reshape((rows,) + value.shape[1:]).astype(last)


def scan_kernel(forward_first, a_ref, b_ref, local_ref, cum_ref, total_ref, coef_s, term_s):
    rows, width = a_ref.shape
    segments = 8
    length = rows // segments
    lanes = 128
    chunks = width // lanes
    half = chunks // 2
    ahead = [(chunk < half) == forward_first for chunk in range(chunks)]
    for chunk in range(chunks):
        span = pl.ds(chunk * rows, rows)
        coef_s[span, :] = a_ref[:, pl.ds(chunk * lanes, lanes)]
        term_s[span, :] = b_ref[:, pl.ds(chunk * lanes, lanes)]

    def step(j, carry):
        states, prods = carry
        new_states, new_prods = [], []
        for chunk in range(chunks):
            place = j if ahead[chunk] else length - 1 - j
            where = (pl.ds(chunk * rows + place, segments, stride=length), slice(None))
            coef = coef_s[where]
            state = coef * states[chunk] + term_s[where]
            prod = coef * prods[chunk]
            term_s[where] = state
            coef_s[where] = prod
            new_states.append(state)
            new_prods.append(prod)
        return (tuple(new_states), tuple(new_prods))

    zero = jnp.zeros((segments, lanes), jnp.float32)
    one = jnp.ones((segments, lanes), jnp.float32)
    states, prods = lax.fori_loop(
        0, length, step, ((zero,) * chunks, (one,) * chunks), unroll=4
    )
    for chunk in range(chunks):
        cols = pl.ds(chunk * lanes, lanes)
        carry = jnp.zeros((1, lanes), jnp.float32)
        prod = jnp.ones((1, lanes), jnp.float32)
        order = range(segments) if ahead[chunk] else range(segments - 1, -1, -1)
        for segment in order:
            span = (pl.ds(segment * length, length), cols)
            held = pl.ds(chunk * rows + segment * length, length)
            cum = coef_s[held, :]
            local_ref[span] = term_s[held, :] + cum * carry
            cum_ref[span] = cum * prod
            end_prod = prods[chunk][segment : segment + 1]
            carry = end_prod * carry + states[chunk][segment : segment + 1]
            prod = end_prod * prod
        total_ref[0:1, cols] = prod
        total_ref[1:2, cols] = carry


def scan_both(coefs, terms, forward_first):
    rows, width = coefs.shape
    full = jax.ShapeDtypeStruct((rows, width), jnp.float32)
    whole = pl.BlockSpec(memory_space=pltpu.VMEM)
    return pl.pallas_call(
        functools.partial(scan_kernel, forward_first),
        out_shape=(full, full, jax.ShapeDtypeStruct((8, width), jnp.float32)),
        in_specs=[whole, whole],
        out_specs=(whole, whole, whole),
        scratch_shapes=[pltpu.VMEM((rows * width // 128, 128), jnp.float32)] * 2,
        compiler_params=pltpu.CompilerParams(vmem_limit_bytes=32 << 20),
        cost_estimate=pl.CostEstimate(
            flops=8 * rows * width, bytes_accessed=16 * rows * width, transcendentals=0
        ),
        name="scan_both",
    )(coefs, terms)


def carried(totals, forward_first):
    count, mine = lax.axis_size("ctx"), lax.axis_index("ctx")
    pieces = lax.all_gather(totals[:2], "ctx")
    half = totals.shape[1] // 2
    low = jnp.zeros((1, half), jnp.float32)
    high = jnp.zeros((1, half), jnp.float32)
    for position in range(count - 1):
        back = count - 1 - position
        first, second = (position, back) if forward_first else (back, position)
        ahead_ok = (first < mine) if forward_first else (first > mine)
        behind_ok = (second > mine) if forward_first else (second < mine)
        low = jnp.where(
            ahead_ok, pieces[first, 0:1, :half] * low + pieces[first, 1:2, :half], low
        )
        high = jnp.where(
            behind_ok, pieces[second, 0:1, half:] * high + pieces[second, 1:2, half:], high
        )
    return jnp.concatenate([low, high], axis=1)


def padded_2(cells, sides, width):
    for axis, dim in sides:
        count = lax.axis_size(axis)
        ends = count - 1
        head = lax.slice_in_dim(cells, 0, width, axis=dim)
        tail = lax.slice_in_dim(cells, cells.shape[dim] - width, cells.shape[dim], axis=dim)
        cells = jnp.concatenate(
            [
                lax.ppermute(tail, axis, [(i, (i + 1) % count) for i in range(ends)]),
                cells,
                lax.ppermute(head, axis, [((i + 1) % count, i) for i in range(ends)]),
            ],
            axis=dim,
        )
    return cells


def normed(values, scales):
    average = jnp.mean(values, axis=-1, keepdims=True)
    centred = values - average
    spread = jnp.mean(centred * centred, axis=-1, keepdims=True)
    return centred * lax.rsqrt(spread + 1e-05) * scales


def gelu_exact(values):
    return jax.nn.gelu(values, approximate=False)


def doc_index(positions, starts):
    return jnp.sum((starts[None, :] <= positions[:, None]).astype(jnp.int32), axis=1) - 1


def docs_meet(first_docs, second_docs):
    return jnp.logical_and(first_docs[0] <= second_docs[-1], second_docs[0] <= first_docs[-1])


def score_block(query_blk, key_blk, query_docs, key_docs):
    scores = jnp.einsum(
        "qhe,khe->hqk", query_blk, key_blk, preferred_element_type=jnp.float32
    ) * HEAD_DIM ** (-0.5)
    allowed = query_docs[None, :, None] == key_docs[None, None, :]
    return (scores, allowed)


def grad_block(query_blk, key_blk, value_blk, grad_blk, query_docs, key_docs, log_total, row_term):
    scores, allowed = score_block(query_blk, key_blk, query_docs, key_docs)
    probs = jnp.where(allowed, jnp.exp(scores - log_total[:, :, None]), 0.0)
    dprobs = jnp.einsum("qhe,khe->hqk", grad_blk, value_blk, preferred_element_type=jnp.float32)
    dscores = (probs * (dprobs - row_term[:, :, None])).astype(jnp.bfloat16)
    return (probs, dscores)


def body(
    tokens,
    chars,
    char_token,
    doc_lengths,
    gain_attn,
    qkv_weight,
    out_weight,
    gain_char,
    gru_weight,
    conv_weight,
    gain_merge,
    merge_weight,
    up_weight,
    down_weight,
    cot_tokens,
    cot_chars,
):
    f32 = jnp.float32
    bf16 = jnp.bfloat16
    every = ("ctx", "wsh")
    width = tokens.shape[2]
    lane = 128
    gain_block = jnp.stack([gain_attn, gain_char, gain_merge], axis=1)
    gain_block = jnp.pad(gain_block, ((0, 0), (0, lane - 3)))
    gains_and_qkv = gathered(jnp.concatenate([qkv_weight, gain_block], axis=1), every, True)
    qkv_full = gains_and_qkv[:, : 3 * width]
    gains = jnp.transpose(gains_and_qkv[:, 3 * width :].astype(f32))
    attn_gain_f, char_gain_f, merge_gain_f = gains[0], gains[1], gains[2]
    gru_full = gathered(gru_weight, every, False)
    out_merge = gathered(jnp.concatenate([out_weight, merge_weight], axis=1), every, False)
    out_full = out_merge[:, :width]
    merge_full = out_merge[:, width:]
    conv_full = gathered(conv_weight, every, True)
    up_full = gathered(up_weight, every, False)
    down_full = gathered(down_weight, every, True)
    tok_rows = tokens.shape[1]
    char_rows = chars.shape[1]
    half_width = width // 2
    seq_len = tok_rows * lax.axis_size("ctx")
    key_block = min(seq_len, 512)
    key_count = seq_len // key_block
    scale = HEAD_DIM ** (-0.5)
    token_in = tokens[0].astype(f32)
    char_in = chars[0].astype(f32)
    char_map = char_token[0, 0]
    lengths = doc_lengths[0]
    starts = jnp.cumsum(lengths) - lengths
    positions = lax.axis_index("ctx") * tok_rows + jnp.arange(tok_rows, dtype=jnp.int32)
    query_docs = doc_index(positions, starts)
    doc_first = jnp.any(starts[None, :] == positions[:, None], axis=1)
    doc_last = jnp.any(starts[None, :] == positions[:, None] + 1, axis=1)
    onehot = char_map[None, :] == jnp.arange(tok_rows, dtype=jnp.int32)[:, None]
    onehot_low = onehot.astype(bf16)
    counts = jnp.sum(onehot.astype(f32), axis=1)
    root_counts = jnp.sqrt(counts)
    boundary = char_map[1:] != char_map[:-1]
    first_char = jnp.concatenate([jnp.ones((1,), bool), boundary])
    last_char = jnp.concatenate([boundary, jnp.ones((1,), bool)])
    opens_doc = jnp.any(onehot & doc_first[:, None], axis=0)
    closes_doc = jnp.any(onehot & doc_last[:, None], axis=0)
    keep_fwd = 1.0 - (first_char & opens_doc).astype(f32)
    keep_bwd = 1.0 - (last_char & closes_doc).astype(f32)
    attn_in = normed(token_in, attn_gain_f).astype(bf16)
    qkv = jnp.dot(attn_in, qkv_full, preferred_element_type=f32).astype(bf16)
    queries = qkv[:, :width]
    keys = qkv[:, width : 2 * width]
    values = qkv[:, 2 * width :]
    keys_all = gathered(keys, ("ctx",), True)
    values_all = gathered(values, ("ctx",), False)
    query_heads = queries.reshape(tok_rows, HEADS, HEAD_DIM)
    key_blocks = keys_all.reshape(key_count, key_block, HEADS, HEAD_DIM)
    value_blocks = values_all.reshape(key_count, key_block, HEADS, HEAD_DIM)
    key_docs = doc_index(jnp.arange(seq_len, dtype=jnp.int32), starts).reshape(key_count, key_block)

    def forward_block(carry, inputs):
        key_blk, value_blk, docs_blk = inputs

        def forward_used(state):
            run_max, run_total, run_acc = state
            scores, allowed = score_block(query_heads, key_blk, query_docs, docs_blk)
            scores = jnp.where(allowed, scores, masked_score)
            new_max = jnp.maximum(run_max, jnp.max(scores, axis=2))
            factor = jnp.exp(run_max - new_max)
            weights = jnp.where(allowed, jnp.exp(scores - new_max[:, :, None]), 0.0)
            run_total = run_total * factor + jnp.sum(weights, axis=2)
            run_acc = run_acc * factor[:, :, None] + jnp.einsum(
                "hqk,khe->hqe", weights.astype(bf16), value_blk, preferred_element_type=f32
            )
            return (new_max, run_total, run_acc)

        def forward_skipped(state):
            return state

        return (
            lax.cond(docs_meet(query_docs, docs_blk), forward_used, forward_skipped, carry),
            None,
        )

    start_carry = (
        jnp.full((HEADS, tok_rows), masked_score, f32),
        jnp.zeros((HEADS, tok_rows), f32),
        jnp.zeros((HEADS, tok_rows, HEAD_DIM), f32),
    )
    (run_max, run_total, run_acc), _ = lax.scan(
        forward_block, start_carry, (key_blocks, value_blocks, key_docs)
    )
    log_total = run_max + jnp.log(run_total)
    attn_heads = jnp.transpose(run_acc / run_total[:, :, None], (1, 0, 2))
    attn_out = attn_heads.reshape(tok_rows, width).astype(bf16)
    proj = jnp.dot(attn_out, out_full, preferred_element_type=f32)
    sq_proj, cross_sum, sq_tok = lax.psum(
        (jnp.sum(proj * proj), jnp.sum(token_in * proj), jnp.sum(token_in * token_in)), "ctx"
    )
    elements = seq_len * width
    rms_scale = lax.rsqrt(sq_proj / elements + 1e-06)
    stream_sq = (sq_tok + 2.0 * rms_scale * cross_sum + rms_scale * rms_scale * sq_proj) / elements
    stream_scale = lax.rsqrt(stream_sq + 1e-06)
    stream = token_in + proj * rms_scale
    resid = stream * stream_scale
    char_low = normed(char_in, char_gain_f).astype(bf16)
    gates = jnp.dot(char_low, gru_full, preferred_element_type=f32)
    ramp = jnp.arange(half_width, dtype=f32) / (half_width - 1)
    shift = (1.0 + math.log(char_rows * lax.axis_size("ctx"))) * ramp
    lift = jnp.exp(0.5 * shift)
    zeta_f = jax.nn.sigmoid(gates[:, :half_width] - shift)
    cand_f = gates[:, half_width : 2 * half_width] * lift
    zeta_b = jax.nn.sigmoid(gates[:, 2 * half_width : 3 * half_width] - shift)
    cand_b = gates[:, 3 * half_width :] * lift
    coef_f = (1.0 - zeta_f) * keep_fwd[:, None]
    coef_b = (1.0 - zeta_b) * keep_bwd[:, None]
    coefs = jnp.concatenate([coef_f, coef_b], axis=1)
    terms = jnp.concatenate([zeta_f * cand_f, zeta_b * cand_b], axis=1)
    local_state, cum_state, totals = scan_both(coefs, terms, True)
    carry_in = carried(totals, True)
    states = local_state + cum_state * carry_in
    state_f = states[:, :half_width]
    state_b = states[:, half_width:]
    carry_in_f = carry_in[0, :half_width]
    carry_in_b = carry_in[0, half_width:]
    mixed = states.astype(bf16)
    out_chars = (char_in + mixed.astype(f32)).astype(bf16)
    pooled = (jnp.dot(onehot_low, mixed, preferred_element_type=f32) / root_counts[:, None]).astype(
        bf16
    )
    padded = padded_2(pooled, (("ctx", 0),), 1)
    conv_out = jnp.zeros((tok_rows, width), f32)
    for kernel in range(3):
        conv_out = conv_out + jnp.dot(
            padded[kernel : kernel + tok_rows],
            conv_full[:, kernel * width : (kernel + 1) * width],
            preferred_element_type=f32,
        )
    merge_in = normed(resid, merge_gain_f).astype(bf16)
    merge_pre = jnp.dot(merge_in, merge_full, preferred_element_type=f32) + conv_out
    merged = gelu_exact(merge_pre).astype(bf16)
    up_pre = jnp.dot(merged, up_full, preferred_element_type=f32)
    up_act = gelu_exact(up_pre).astype(bf16)
    out_tok = (resid + jnp.dot(up_act, down_full, preferred_element_type=f32)).astype(bf16)
    cot_tok = cot_tokens[0]
    cot_tok_f = cot_tok.astype(f32)
    cot_chr_f = cot_chars[0].astype(f32)
    grad_down = jnp.einsum("tf,td->fd", up_act, cot_tok, preferred_element_type=f32)
    grad_act = jnp.einsum("td,fd->tf", cot_tok, down_full, preferred_element_type=f32)
    _, gelu_up_back = jax.vjp(gelu_exact, up_pre)
    grad_up_pre = gelu_up_back(grad_act)[0].astype(bf16)
    grad_up = jnp.einsum("tc,tf->cf", merged, grad_up_pre, preferred_element_type=f32)
    grad_merged = jnp.einsum("tf,cf->tc", grad_up_pre, up_full, preferred_element_type=f32)
    _, gelu_merge_back = jax.vjp(gelu_exact, merge_pre)
    grad_pre = gelu_merge_back(grad_merged)[0].astype(bf16)
    grad_merge = jnp.einsum("tc,te->ce", merge_in, grad_pre, preferred_element_type=f32)
    grad_merge_in = jnp.einsum("te,ce->tc", grad_pre, merge_full, preferred_element_type=f32)
    grad_conv = jnp.concatenate(
        [
            jnp.einsum(
                "tc,te->ce",
                padded[kernel : kernel + tok_rows],
                grad_pre,
                preferred_element_type=f32,
            )
            for kernel in range(3)
        ],
        axis=1,
    )
    grad_padded = padded_2(grad_pre, (("ctx", 0),), 1)
    grad_pooled = jnp.zeros((tok_rows, width), f32)
    for kernel in range(3):
        grad_pooled = grad_pooled + jnp.einsum(
            "te,ce->tc",
            grad_padded[2 - kernel : 2 - kernel + tok_rows],
            conv_full[:, kernel * width : (kernel + 1) * width],
            preferred_element_type=f32,
        )
    _, merge_norm_back = jax.vjp(normed, resid, merge_gain_f)
    grad_resid_norm, grad_merge_gain = merge_norm_back(grad_merge_in)
    grad_resid = cot_tok_f + grad_resid_norm
    grad_mixed = cot_chr_f + jnp.take(grad_pooled / root_counts[:, None], char_map, axis=0)
    shifted_f = jnp.concatenate([coef_f[1:], jnp.ones((1, half_width), f32)], axis=0)
    shifted_b = jnp.concatenate([jnp.ones((1, half_width), f32), coef_b[:-1]], axis=0)
    local_lam, cum_lam, lam_totals = scan_both(
        jnp.concatenate([shifted_f, shifted_b], axis=1), grad_mixed, False
    )
    edge = jnp.concatenate([coef_f[0], coef_b[-1]])[None, :]
    lams = local_lam + cum_lam * carried(lam_totals[:2] * edge, False)
    lam_f = lams[:, :half_width]
    lam_b = lams[:, half_width:]
    prev_f = jnp.concatenate([carry_in_f[None, :], state_f[:-1]], axis=0)
    grad_zeta_f = lam_f * (cand_f - keep_fwd[:, None] * prev_f) * zeta_f * (1.0 - zeta_f)
    grad_cand_f = lam_f * zeta_f * lift
    next_b = jnp.concatenate([state_b[1:], carry_in_b[None, :]], axis=0)
    grad_zeta_b = lam_b * (cand_b - keep_bwd[:, None] * next_b) * zeta_b * (1.0 - zeta_b)
    grad_cand_b = lam_b * zeta_b * lift
    grad_gates = jnp.concatenate(
        [grad_zeta_f, grad_cand_f, grad_zeta_b, grad_cand_b], axis=1
    ).astype(bf16)
    grad_gru = jnp.einsum("tc,tg->cg", char_low, grad_gates, preferred_element_type=f32)
    grad_char_norm = jnp.einsum("tg,cg->tc", grad_gates, gru_full, preferred_element_type=f32)
    _, char_norm_back = jax.vjp(normed, char_in, char_gain_f)
    grad_char_in, grad_char_gain = char_norm_back(grad_char_norm)
    grad_chars_out = (cot_chr_f + grad_char_in).astype(bf16)
    dot_stream, dot_proj = lax.psum(
        (jnp.sum(grad_resid * stream), jnp.sum(grad_resid * proj)), "ctx"
    )
    mean_gs = dot_stream / elements
    mean_gp = dot_proj / elements
    mean_sp = (cross_sum + rms_scale * sq_proj) / elements
    grad_stream = stream_scale * grad_resid - stream_scale**3 * mean_gs * stream
    mean_gsp = stream_scale * mean_gp - stream_scale**3 * mean_gs * mean_sp
    grad_proj = (rms_scale * grad_stream - rms_scale**3 * mean_gsp * proj).astype(bf16)
    grad_out_proj = jnp.einsum("tc,te->ce", attn_out, grad_proj, preferred_element_type=f32)
    grad_attn = jnp.einsum("te,ce->tc", grad_proj, out_full, preferred_element_type=f32).astype(
        bf16
    )
    grad_heads = grad_attn.reshape(tok_rows, HEADS, HEAD_DIM)
    row_term = jnp.einsum("qhe,qhe->hq", grad_heads.astype(f32), attn_heads)

    def step_block(dq_acc, inputs):
        key_blk, value_blk, docs_blk = inputs

        def step_used(acc):
            probs, dscores = grad_block(
                query_heads,
                key_blk,
                value_blk,
                grad_heads,
                query_docs,
                docs_blk,
                log_total,
                row_term,
            )
            acc = (
                acc
                + jnp.einsum("hqk,khe->qhe", dscores, key_blk, preferred_element_type=f32) * scale
            )
            dk_blk = (
                jnp.einsum("hqk,qhe->khe", dscores, query_heads, preferred_element_type=f32) * scale
            )
            dv_blk = jnp.einsum(
                "hqk,qhe->khe", probs.astype(bf16), grad_heads, preferred_element_type=f32
            )
            return (acc, (dk_blk, dv_blk))

        def step_skipped(acc):
            zero_blk = jnp.zeros((key_blk.shape[0], HEADS, HEAD_DIM), f32)
            return (acc, (zero_blk, zero_blk))

        return lax.cond(docs_meet(query_docs, docs_blk), step_used, step_skipped, dq_acc)

    dq_heads, key_terms = lax.scan(
        step_block,
        jnp.zeros((tok_rows, HEADS, HEAD_DIM), f32),
        (key_blocks, value_blocks, key_docs),
    )
    dk_local = scattered(key_terms[0].reshape(seq_len, width).astype(bf16), ("ctx",), True, bf16)
    dv_local = scattered(key_terms[1].reshape(seq_len, width).astype(bf16), ("ctx",), False, bf16)
    grad_qkv_low = jnp.concatenate(
        [
            dq_heads.reshape(tok_rows, width).astype(bf16),
            dk_local,
            dv_local,
        ],
        axis=1,
    )
    grad_qkv = jnp.einsum("tc,tg->cg", attn_in, grad_qkv_low, preferred_element_type=f32)
    grad_attn_in = jnp.einsum("tg,cg->tc", grad_qkv_low, qkv_full, preferred_element_type=f32)
    _, attn_norm_back = jax.vjp(normed, token_in, attn_gain_f)
    grad_token_in, grad_attn_gain = attn_norm_back(grad_attn_in)
    grad_tokens_out = (grad_stream + grad_token_in).astype(bf16)
    gain_grads = jnp.stack([grad_attn_gain, grad_char_gain, grad_merge_gain], axis=1)
    gain_grads = jnp.pad(gain_grads, ((0, 0), (0, lane - 3)))
    down_shard = scattered(grad_down.astype(bf16), every, True, f32)
    up_shard = scattered(grad_up.astype(bf16), every, False, f32)
    merge_conv = jnp.concatenate([grad_merge.astype(bf16), grad_conv.astype(bf16)], axis=1)
    merge_conv = scattered(merge_conv, every, True, f32)
    gru_out = jnp.concatenate([grad_gru.astype(bf16), grad_out_proj.astype(bf16)], axis=1)
    gru_out = scattered(gru_out, every, False, f32)
    qkv_shard = scattered(grad_qkv.astype(bf16), every, True, f32)
    gain_shard = scattered(gain_grads.astype(bf16), every, False, f32)
    shards = (
        gain_shard[:, 0],
        qkv_shard,
        gru_out[:, 2 * width :],
        gain_shard[:, 1],
        gru_out[:, : 2 * width],
        merge_conv[:, width:],
        gain_shard[:, 2],
        merge_conv[:, :width],
        up_shard,
        down_shard,
    )
    return (
        out_tok[None],
        out_chars[None],
        grad_tokens_out[None],
        grad_chars_out[None],
        shards[0],
        shards[1],
        shards[2],
        shards[3],
        shards[4],
        shards[5],
        shards[6],
        shards[7],
        shards[8],
        shards[9],
    )


def solution(mesh):
    in_specs = (
        P("wsh", "ctx", None),
        P("wsh", "ctx", None),
        P("wsh", "ctx", None),
        P("wsh", None),
        P(("ctx", "wsh")),
        P(("ctx", "wsh"), None),
        P(("ctx", "wsh"), None),
        P(("ctx", "wsh")),
        P(("ctx", "wsh"), None),
        P(("ctx", "wsh"), None),
        P(("ctx", "wsh")),
        P(("ctx", "wsh"), None),
        P(("ctx", "wsh"), None),
        P(("ctx", "wsh"), None),
        P("wsh", "ctx", None),
        P("wsh", "ctx", None),
    )
    out_specs = (
        P("wsh", "ctx", None),
        P("wsh", "ctx", None),
        P("wsh", "ctx", None),
        P("wsh", "ctx", None),
        P(("ctx", "wsh")),
        P(("ctx", "wsh"), None),
        P(("ctx", "wsh"), None),
        P(("ctx", "wsh")),
        P(("ctx", "wsh"), None),
        P(("ctx", "wsh"), None),
        P(("ctx", "wsh")),
        P(("ctx", "wsh"), None),
        P(("ctx", "wsh"), None),
        P(("ctx", "wsh"), None),
    )
    return jax.shard_map(body, mesh=mesh, in_specs=in_specs, out_specs=out_specs, check_vma=False)
```

```python
import functools
import math

import jax
import jax.numpy as jnp
from jax import lax
from jax.experimental import pallas as pl
from jax.experimental.pallas import tpu as pltpu
from jax.sharding import PartitionSpec as P

HEADS = 12
HEAD_DIM = 64


masked_score = -1e30


def masks_of(axis):
    return [1 << k for k in range(lax.axis_size(axis).bit_length() - 1)]


def place_of(axis, partner):
    here = {"ctx": lax.axis_index("ctx"), "wsh": lax.axis_index("wsh")}
    here[axis] = partner
    return (here["ctx"], here["wsh"])


def greet(over_wsh):
    barrier = pltpu.get_barrier_semaphore()
    partners = [
        place_of("ctx", lax.bitwise_xor(lax.axis_index("ctx"), mask)) for mask in masks_of("ctx")
    ]
    if over_wsh:
        partners = partners + [
            place_of("wsh", lax.bitwise_xor(lax.axis_index("wsh"), gap))
            for gap in range(1, lax.axis_size("wsh"))
        ]
    for partner in partners:
        pl.semaphore_signal(
            barrier, inc=1, device_id=partner, device_id_type=pl.DeviceIdType.MESH
        )
    pl.semaphore_wait(barrier, len(partners))


def ctx_bits(upward):
    masks = masks_of("ctx")
    middle = masks[1:]
    return (middle if upward else middle[::-1]) + masks[:1]


def ctx_bit(mask):
    return lax.rem(lax.div(lax.axis_index("ctx"), mask), 2)


def ctx_index(fixed):
    return tuple(
        fixed[mask] if mask in fixed else slice(None) for mask in reversed(masks_of("ctx"))
    )


def remote(src, dst, sems, number, partner):
    return pltpu.make_async_remote_copy(
        src_ref=src,
        dst_ref=dst,
        send_sem=sems[0].at[number],
        recv_sem=sems[1].at[number],
        device_id=partner,
        device_id_type=pl.DeviceIdType.MESH,
    )


def gather_kernel(slots, count, over_wsh, *refs):
    shards, outs = refs[:count], refs[count : 2 * count]
    sems, local_sems = refs[2 * count : 2 * count + 2], refs[2 * count + 2]
    width_w = lax.axis_size("wsh") if over_wsh else 1
    mine_w = lax.axis_index("wsh") if over_wsh else 0
    bits = len(masks_of("ctx"))
    per_stream = width_w - 1 + bits
    greet(over_wsh)
    streams = [stream for slot in slots for stream in slot]
    number_of = {stream: position for position, stream in enumerate(streams)}
    started = {}

    def start(stream, step):
        array, first, cols, upward = stream
        base = number_of[stream] * per_stream
        span = pl.ds(first, cols)
        out = outs[array]
        every = {mask: ctx_bit(mask) for mask in masks_of("ctx")}
        copies = []
        if step == 0:
            own = ctx_index(every) + (mine_w, slice(None), span)
            copy = pltpu.make_async_copy(
                shards[array].at[:, span], out.at[own], local_sems.at[number_of[stream]]
            )
            copies.append(copy)
            for gap in range(1, width_w):
                copies.append(
                    remote(
                        shards[array].at[:, span],
                        out.at[own],
                        sems,
                        base + gap - 1,
                        place_of("wsh", lax.bitwise_xor(mine_w, gap)),
                    )
                )
        else:
            order = ctx_bits(upward)
            held = {mask: every[mask] for mask in order[step - 1 :]}
            part = ctx_index(held) + (slice(None), slice(None), span)
            partner = place_of("ctx", lax.bitwise_xor(lax.axis_index("ctx"), order[step - 1]))
            copies.append(
                remote(out.at[part], out.at[part], sems, base + width_w - 1 + step - 1, partner)
            )
        for copy in copies:
            copy.start()
        started[stream, step] = copies

    def finish(stream, step):
        for position, copy in enumerate(started[stream, step]):
            if step == 0 and position == 0:
                copy.wait()
            else:
                copy.wait_recv()

    for tick in range(len(slots) + bits + 1):
        for number, slot in reversed(list(enumerate(slots))):
            step = tick - number
            for stream in slot:
                if 1 <= step <= bits + 1:
                    finish(stream, step - 1)
                if 0 <= step <= bits:
                    start(stream, step)
    for (stream, step), copies in started.items():
        for copy in copies[1:] if step == 0 else copies:
            copy.wait_send()


def gather_all(arrays, slots, over_wsh, collective):
    bits = len(masks_of("ctx"))
    width_w = lax.axis_size("wsh") if over_wsh else 1
    count = len(arrays)
    streams = sum(len(slot) for slot in slots)
    copies = streams * (width_w - 1 + bits)
    hbm = pl.BlockSpec(memory_space=pl.ANY)
    outs = pl.pallas_call(
        functools.partial(gather_kernel, slots, count, over_wsh),
        out_shape=tuple(
            jax.ShapeDtypeStruct((2,) * bits + (width_w,) + array.shape, array.dtype)
            for array in arrays
        ),
        in_specs=[hbm] * count,
        out_specs=(hbm,) * count,
        scratch_shapes=[
            pltpu.SemaphoreType.DMA((copies,)),
            pltpu.SemaphoreType.DMA((copies,)),
            pltpu.SemaphoreType.DMA((streams,)),
        ],
        compiler_params=pltpu.CompilerParams(
            collective_id=collective, has_side_effects=True, vmem_limit_bytes=4 << 20
        ),
        name="gather_all",
    )(*arrays)
    return [out.reshape((-1, out.shape[-1])) for out in outs]


def add_into(total_ref, extra_ref, fixed_total, fixed_extra, shape, rows, block_rows, span):
    steps = math.prod(shape) * (rows // block_rows)

    def step(position, carry):
        rest = position
        chunk = lax.rem(rest, rows // block_rows)
        rest = lax.div(rest, rows // block_rows)
        free = []
        for size in reversed(shape):
            free.append(lax.rem(rest, size))
            rest = lax.div(rest, size)
        free = free[::-1]
        take = iter(free)
        into = tuple(next(take) if entry is None else entry for entry in fixed_total)
        take = iter(free)
        source = tuple(next(take) if entry is None else entry for entry in fixed_extra)
        down = pl.ds(pl.multiple_of(chunk * block_rows, block_rows), block_rows)
        total_ref[into + (down, span)] = (
            total_ref[into + (down, span)] + extra_ref[source + (down, slice(None))]
        )
        return carry

    lax.fori_loop(0, steps, step, 0)


def scatter_kernel(slots, count, over_wsh, *refs):
    streams = [stream for slot in slots for stream in slot]
    grads, outs = refs[:count], refs[count : 2 * count]
    bits = len(masks_of("ctx"))
    held = refs[2 * count : 3 * count]
    rest = refs[3 * count :]
    per_stream_bufs = bits + (1 if over_wsh else 0)
    landing = {}
    for number, stream in enumerate(streams):
        landing[stream] = rest[number * per_stream_bufs : (number + 1) * per_stream_bufs]
    sems = rest[len(streams) * per_stream_bufs : len(streams) * per_stream_bufs + 2]
    local_sems = rest[len(streams) * per_stream_bufs + 2]
    width_w = lax.axis_size("wsh") if over_wsh else 1
    mine_w = lax.axis_index("wsh") if over_wsh else 0
    per_stream = width_w - 1 + bits
    number_of = {stream: position for position, stream in enumerate(streams)}
    every = {mask: ctx_bit(mask) for mask in masks_of("ctx")}
    low = masks_of("ctx")[0]
    started = {}
    greet(over_wsh)

    def start(stream, step):
        array, first, cols, upward = stream
        base = number_of[stream] * per_stream
        span = pl.ds(first, cols)
        order = ctx_bits(upward)[::-1]
        copies = []
        if step == 0:
            kept = ctx_index({low: every[low]}) + (slice(None), slice(None), span)
            copies.append(
                pltpu.make_async_copy(
                    grads[array].at[kept],
                    held[array].at[(slice(None),) * bits + (slice(None), span)],
                    local_sems.at[number_of[stream]],
                )
            )
            away = ctx_index({low: 1 - every[low]}) + (slice(None), slice(None), span)
            copies.append(
                remote(
                    grads[array].at[away],
                    landing[stream][0],
                    sems,
                    base,
                    place_of("ctx", lax.bitwise_xor(lax.axis_index("ctx"), low)),
                )
            )
        elif step < bits:
            fixed = {mask: every[mask] for mask in order[:step]}
            fixed[order[step]] = 1 - every[order[step]]
            away = ctx_index(fixed)[:-1] + (slice(None), slice(None), span)
            copies.append(
                remote(
                    held[array].at[away],
                    landing[stream][step],
                    sems,
                    base + step,
                    place_of("ctx", lax.bitwise_xor(lax.axis_index("ctx"), order[step])),
                )
            )
        elif over_wsh:
            here = ctx_index(every)[:-1]
            for gap in range(1, width_w):
                other = lax.bitwise_xor(mine_w, gap)
                copies.append(
                    remote(
                        held[array].at[here + (other, slice(None), span)],
                        landing[stream][bits].at[gap - 1],
                        sems,
                        base + bits + gap - 1,
                        place_of("wsh", other),
                    )
                )
        for copy in copies:
            copy.start()
        started[stream, step] = copies

    def finish(stream, step):
        array, first, cols, upward = stream
        span = pl.ds(first, cols)
        order = ctx_bits(upward)[::-1]
        for position, copy in enumerate(started[stream, step]):
            if step == 0 and position == 0:
                copy.wait()
            else:
                copy.wait_recv()
        rows = held[array].shape[-2]
        block_rows = rows if rows <= 24 else 32
        if step < bits:
            fixed = {mask: every[mask] for mask in order[: step + 1]}
            lead = ctx_index(fixed)[:-1]
            into = tuple(None if isinstance(entry, slice) else entry for entry in lead) + (None,)
            free = (2,) * (bits - 1 - step)
            add_into(
                held[array],
                landing[stream][step],
                into,
                (None,) * (len(free) + 1),
                free + (width_w,),
                rows,
                block_rows,
                span,
            )
        if step == bits or (step == bits - 1 and not over_wsh):
            here = ctx_index(every)[:-1] + (mine_w,)
            for chunk in range(0, rows, block_rows):
                down = pl.ds(chunk, block_rows)
                total = held[array][here + (down, span)].astype(jnp.float32)
                for gap in range(1, width_w):
                    total = total + landing[stream][bits][gap - 1, down, :].astype(jnp.float32)
                outs[array][down, span] = total.astype(outs[array].dtype)

    steps = bits + (1 if over_wsh else 0)
    for tick in range(len(slots) + steps):
        for number, slot in reversed(list(enumerate(slots))):
            step = tick - number
            for stream in slot:
                if 1 <= step <= steps:
                    finish(stream, step - 1)
                if 0 <= step < steps:
                    start(stream, step)
    for (stream, step), copies in started.items():
        for copy in copies[1:] if step == 0 else copies:
            copy.wait_send()


def scatter_sums(arrays, slots, over_wsh, collective, dtype):
    bits = len(masks_of("ctx"))
    width_w = lax.axis_size("wsh") if over_wsh else 1
    count = len(arrays)
    parts = width_w << bits
    rows = [array.shape[0] // parts for array in arrays]
    shaped = [
        array.reshape((2,) * bits + (width_w, row, array.shape[1]))
        for array, row in zip(arrays, rows)
    ]
    streams = [stream for slot in slots for stream in slot]
    copies = len(streams) * (width_w - 1 + bits)
    buffers = [
        pltpu.VMEM((2,) * (bits - 1) + (width_w, row, array.shape[1]), array.dtype)
        for array, row in zip(arrays, rows)
    ]
    for array, first, cols, upward in streams:
        kind = arrays[array].dtype
        for step in range(bits):
            buffers.append(
                pltpu.VMEM((2,) * (bits - 1 - step) + (width_w, rows[array], cols), kind)
            )
        if over_wsh:
            buffers.append(pltpu.VMEM((width_w - 1, rows[array], cols), kind))
    return pl.pallas_call(
        functools.partial(scatter_kernel, slots, count, over_wsh),
        out_shape=tuple(
            jax.ShapeDtypeStruct((row, array.shape[1]), dtype) for array, row in zip(arrays, rows)
        ),
        in_specs=[pl.BlockSpec(memory_space=pl.ANY)] * count,
        out_specs=(pl.BlockSpec(memory_space=pltpu.VMEM),) * count,
        scratch_shapes=buffers
        + [
            pltpu.SemaphoreType.DMA((copies,)),
            pltpu.SemaphoreType.DMA((copies,)),
            pltpu.SemaphoreType.DMA((len(streams),)),
        ],
        compiler_params=pltpu.CompilerParams(
            collective_id=collective, has_side_effects=True, vmem_limit_bytes=56 << 20
        ),
        name="scatter_sums",
    )(*shaped)


def halves(number, cols):
    pieces = 2 if cols < 2304 else 4
    cuts = [cols * piece // pieces // 128 * 128 for piece in range(pieces)] + [cols]
    streams = [
        (number, cuts[piece], cuts[piece + 1] - cuts[piece], piece % 2 == 0)
        for piece in range(pieces)
    ]
    return [tuple(streams[piece : piece + 2]) for piece in range(0, pieces, 2)]


def slots_of(arrays):
    return [
        slot for number, part in enumerate(arrays) for slot in halves(number, part.shape[1])
    ]


def scan_kernel(forward_first, a_ref, b_ref, local_ref, cum_ref, total_ref, coef_s, term_s):
    rows, width = a_ref.shape
    segments = 8
    length = rows // segments
    lanes = 128
    chunks = width // lanes
    half = chunks // 2
    ahead = [(chunk < half) == forward_first for chunk in range(chunks)]
    for chunk in range(chunks):
        span = pl.ds(chunk * rows, rows)
        coef_s[span, :] = a_ref[:, pl.ds(chunk * lanes, lanes)]
        term_s[span, :] = b_ref[:, pl.ds(chunk * lanes, lanes)]

    def step(j, carry):
        states, prods = carry
        new_states, new_prods = [], []
        for chunk in range(chunks):
            place = j if ahead[chunk] else length - 1 - j
            where = (pl.ds(chunk * rows + place, segments, stride=length), slice(None))
            coef = coef_s[where]
            state = coef * states[chunk] + term_s[where]
            prod = coef * prods[chunk]
            term_s[where] = state
            coef_s[where] = prod
            new_states.append(state)
            new_prods.append(prod)
        return (tuple(new_states), tuple(new_prods))

    zero = jnp.zeros((segments, lanes), jnp.float32)
    one = jnp.ones((segments, lanes), jnp.float32)
    states, prods = lax.fori_loop(
        0, length, step, ((zero,) * chunks, (one,) * chunks), unroll=4
    )
    for chunk in range(chunks):
        cols = pl.ds(chunk * lanes, lanes)
        carry = jnp.zeros((1, lanes), jnp.float32)
        prod = jnp.ones((1, lanes), jnp.float32)
        order = range(segments) if ahead[chunk] else range(segments - 1, -1, -1)
        for segment in order:
            span = (pl.ds(segment * length, length), cols)
            held = pl.ds(chunk * rows + segment * length, length)
            cum = coef_s[held, :]
            local_ref[span] = term_s[held, :] + cum * carry
            cum_ref[span] = cum * prod
            end_prod = prods[chunk][segment : segment + 1]
            carry = end_prod * carry + states[chunk][segment : segment + 1]
            prod = end_prod * prod
        total_ref[0:1, cols] = prod
        total_ref[1:2, cols] = carry


def scan_both(coefs, terms, forward_first):
    rows, width = coefs.shape
    full = jax.ShapeDtypeStruct((rows, width), jnp.float32)
    whole = pl.BlockSpec(memory_space=pltpu.VMEM)
    return pl.pallas_call(
        functools.partial(scan_kernel, forward_first),
        out_shape=(full, full, jax.ShapeDtypeStruct((8, width), jnp.float32)),
        in_specs=[whole, whole],
        out_specs=(whole, whole, whole),
        scratch_shapes=[pltpu.VMEM((rows * width // 128, 128), jnp.float32)] * 2,
        compiler_params=pltpu.CompilerParams(vmem_limit_bytes=32 << 20),
        cost_estimate=pl.CostEstimate(
            flops=8 * rows * width, bytes_accessed=16 * rows * width, transcendentals=0
        ),
        name="scan_both",
    )(coefs, terms)


def carried(totals, forward_first):
    count, mine = lax.axis_size("ctx"), lax.axis_index("ctx")
    pieces = lax.all_gather(totals[:2], "ctx")
    half = totals.shape[1] // 2
    low = jnp.zeros((1, half), jnp.float32)
    high = jnp.zeros((1, half), jnp.float32)
    for position in range(count - 1):
        back = count - 1 - position
        first, second = (position, back) if forward_first else (back, position)
        ahead_ok = (first < mine) if forward_first else (first > mine)
        behind_ok = (second > mine) if forward_first else (second < mine)
        low = jnp.where(
            ahead_ok, pieces[first, 0:1, :half] * low + pieces[first, 1:2, :half], low
        )
        high = jnp.where(
            behind_ok, pieces[second, 0:1, half:] * high + pieces[second, 1:2, half:], high
        )
    return jnp.concatenate([low, high], axis=1)


def padded_2(cells, sides, width):
    for axis, dim in sides:
        count = lax.axis_size(axis)
        ends = count - 1
        head = lax.slice_in_dim(cells, 0, width, axis=dim)
        tail = lax.slice_in_dim(cells, cells.shape[dim] - width, cells.shape[dim], axis=dim)
        cells = jnp.concatenate(
            [
                lax.ppermute(tail, axis, [(i, (i + 1) % count) for i in range(ends)]),
                cells,
                lax.ppermute(head, axis, [((i + 1) % count, i) for i in range(ends)]),
            ],
            axis=dim,
        )
    return cells


def normed(values, scales):
    average = jnp.mean(values, axis=-1, keepdims=True)
    centred = values - average
    spread = jnp.mean(centred * centred, axis=-1, keepdims=True)
    return centred * lax.rsqrt(spread + 1e-05) * scales


def gelu_exact(values):
    return jax.nn.gelu(values, approximate=False)


def doc_index(positions, starts):
    return jnp.sum((starts[None, :] <= positions[:, None]).astype(jnp.int32), axis=1) - 1


def docs_meet(first_docs, second_docs):
    return jnp.logical_and(first_docs[0] <= second_docs[-1], second_docs[0] <= first_docs[-1])


def score_block(query_blk, key_blk, query_docs, key_docs):
    scores = jnp.einsum(
        "qhe,khe->hqk", query_blk, key_blk, preferred_element_type=jnp.float32
    ) * HEAD_DIM ** (-0.5)
    allowed = query_docs[None, :, None] == key_docs[None, None, :]
    return (scores, allowed)


def grad_block(query_blk, key_blk, value_blk, grad_blk, query_docs, key_docs, log_total, row_term):
    scores, allowed = score_block(query_blk, key_blk, query_docs, key_docs)
    probs = jnp.where(allowed, jnp.exp(scores - log_total[:, :, None]), 0.0)
    dprobs = jnp.einsum("qhe,khe->hqk", grad_blk, value_blk, preferred_element_type=jnp.float32)
    dscores = (probs * (dprobs - row_term[:, :, None])).astype(jnp.bfloat16)
    return (probs, dscores)


def body(
    tokens,
    chars,
    char_token,
    doc_lengths,
    gain_attn,
    qkv_weight,
    out_weight,
    gain_char,
    gru_weight,
    conv_weight,
    gain_merge,
    merge_weight,
    up_weight,
    down_weight,
    cot_tokens,
    cot_chars,
):
    f32 = jnp.float32
    bf16 = jnp.bfloat16
    every = ("ctx", "wsh")
    width = tokens.shape[2]
    lane = 128
    gain_block = jnp.stack([gain_attn, gain_char, gain_merge], axis=1)
    gain_block = jnp.pad(gain_block, ((0, 0), (0, lane - 3)))
    first_needed = [gru_weight, jnp.concatenate([qkv_weight, gain_block], axis=1)]
    gru_full, gains_and_qkv = gather_all(
        first_needed,
        slots_of(first_needed),
        True,
        0,
    )
    qkv_full = gains_and_qkv[:, : 3 * width]
    gains = jnp.transpose(gains_and_qkv[:, 3 * width :].astype(f32))
    attn_gain_f, char_gain_f, merge_gain_f = gains[0], gains[1], gains[2]
    later = [conv_weight, out_weight, merge_weight, up_weight, down_weight]
    conv_full, out_full, merge_full, up_full, down_full = gather_all(
        later,
        slots_of(later),
        True,
        1,
    )
    tok_rows = tokens.shape[1]
    char_rows = chars.shape[1]
    half_width = width // 2
    seq_len = tok_rows * lax.axis_size("ctx")
    key_block = min(seq_len, 512)
    key_count = seq_len // key_block
    scale = HEAD_DIM ** (-0.5)
    token_in = tokens[0].astype(f32)
    char_in = chars[0].astype(f32)
    char_map = char_token[0, 0]
    lengths = doc_lengths[0]
    starts = jnp.cumsum(lengths) - lengths
    positions = lax.axis_index("ctx") * tok_rows + jnp.arange(tok_rows, dtype=jnp.int32)
    query_docs = doc_index(positions, starts)
    doc_first = jnp.any(starts[None, :] == positions[:, None], axis=1)
    doc_last = jnp.any(starts[None, :] == positions[:, None] + 1, axis=1)
    onehot = char_map[None, :] == jnp.arange(tok_rows, dtype=jnp.int32)[:, None]
    onehot_low = onehot.astype(bf16)
    counts = jnp.sum(onehot.astype(f32), axis=1)
    root_counts = jnp.sqrt(counts)
    boundary = char_map[1:] != char_map[:-1]
    first_char = jnp.concatenate([jnp.ones((1,), bool), boundary])
    last_char = jnp.concatenate([boundary, jnp.ones((1,), bool)])
    opens_doc = jnp.any(onehot & doc_first[:, None], axis=0)
    closes_doc = jnp.any(onehot & doc_last[:, None], axis=0)
    keep_fwd = 1.0 - (first_char & opens_doc).astype(f32)
    keep_bwd = 1.0 - (last_char & closes_doc).astype(f32)
    attn_in = normed(token_in, attn_gain_f).astype(bf16)
    qkv = jnp.dot(attn_in, qkv_full, preferred_element_type=f32).astype(bf16)
    queries = qkv[:, :width]
    keys = qkv[:, width : 2 * width]
    values = qkv[:, 2 * width :]
    keys_all, values_all = gather_all(
        [keys, values], [((0, 0, width, True), (1, 0, width, False))], False, 2
    )
    query_heads = queries.reshape(tok_rows, HEADS, HEAD_DIM)
    key_blocks = keys_all.reshape(key_count, key_block, HEADS, HEAD_DIM)
    value_blocks = values_all.reshape(key_count, key_block, HEADS, HEAD_DIM)
    key_docs = doc_index(jnp.arange(seq_len, dtype=jnp.int32), starts).reshape(key_count, key_block)

    def forward_block(carry, inputs):
        key_blk, value_blk, docs_blk = inputs

        def forward_used(state):
            run_max, run_total, run_acc = state
            scores, allowed = score_block(query_heads, key_blk, query_docs, docs_blk)
            scores = jnp.where(allowed, scores, masked_score)
            new_max = jnp.maximum(run_max, jnp.max(scores, axis=2))
            factor = jnp.exp(run_max - new_max)
            weights = jnp.where(allowed, jnp.exp(scores - new_max[:, :, None]), 0.0)
            run_total = run_total * factor + jnp.sum(weights, axis=2)
            run_acc = run_acc * factor[:, :, None] + jnp.einsum(
                "hqk,khe->hqe", weights.astype(bf16), value_blk, preferred_element_type=f32
            )
            return (new_max, run_total, run_acc)

        def forward_skipped(state):
            return state

        return (
            lax.cond(docs_meet(query_docs, docs_blk), forward_used, forward_skipped, carry),
            None,
        )

    start_carry = (
        jnp.full((HEADS, tok_rows), masked_score, f32),
        jnp.zeros((HEADS, tok_rows), f32),
        jnp.zeros((HEADS, tok_rows, HEAD_DIM), f32),
    )
    (run_max, run_total, run_acc), _ = lax.scan(
        forward_block, start_carry, (key_blocks, value_blocks, key_docs)
    )
    log_total = run_max + jnp.log(run_total)
    attn_heads = jnp.transpose(run_acc / run_total[:, :, None], (1, 0, 2))
    attn_out = attn_heads.reshape(tok_rows, width).astype(bf16)
    proj = jnp.dot(attn_out, out_full, preferred_element_type=f32)
    sq_proj, cross_sum, sq_tok = lax.psum(
        (jnp.sum(proj * proj), jnp.sum(token_in * proj), jnp.sum(token_in * token_in)), "ctx"
    )
    elements = seq_len * width
    rms_scale = lax.rsqrt(sq_proj / elements + 1e-06)
    stream_sq = (sq_tok + 2.0 * rms_scale * cross_sum + rms_scale * rms_scale * sq_proj) / elements
    stream_scale = lax.rsqrt(stream_sq + 1e-06)
    stream = token_in + proj * rms_scale
    resid = stream * stream_scale
    char_low = normed(char_in, char_gain_f).astype(bf16)
    gates = jnp.dot(char_low, gru_full, preferred_element_type=f32)
    ramp = jnp.arange(half_width, dtype=f32) / (half_width - 1)
    shift = (1.0 + math.log(char_rows * lax.axis_size("ctx"))) * ramp
    lift = jnp.exp(0.5 * shift)
    zeta_f = jax.nn.sigmoid(gates[:, :half_width] - shift)
    cand_f = gates[:, half_width : 2 * half_width] * lift
    zeta_b = jax.nn.sigmoid(gates[:, 2 * half_width : 3 * half_width] - shift)
    cand_b = gates[:, 3 * half_width :] * lift
    coef_f = (1.0 - zeta_f) * keep_fwd[:, None]
    coef_b = (1.0 - zeta_b) * keep_bwd[:, None]
    coefs = jnp.concatenate([coef_f, coef_b], axis=1)
    terms = jnp.concatenate([zeta_f * cand_f, zeta_b * cand_b], axis=1)
    local_state, cum_state, totals = scan_both(coefs, terms, True)
    carry_in = carried(totals, True)
    states = local_state + cum_state * carry_in
    state_f = states[:, :half_width]
    state_b = states[:, half_width:]
    carry_in_f = carry_in[0, :half_width]
    carry_in_b = carry_in[0, half_width:]
    mixed = states.astype(bf16)
    out_chars = (char_in + mixed.astype(f32)).astype(bf16)
    pooled = (jnp.dot(onehot_low, mixed, preferred_element_type=f32) / root_counts[:, None]).astype(
        bf16
    )
    padded = padded_2(pooled, (("ctx", 0),), 1)
    conv_out = jnp.zeros((tok_rows, width), f32)
    for kernel in range(3):
        conv_out = conv_out + jnp.dot(
            padded[kernel : kernel + tok_rows],
            conv_full[:, kernel * width : (kernel + 1) * width],
            preferred_element_type=f32,
        )
    merge_in = normed(resid, merge_gain_f).astype(bf16)
    merge_pre = jnp.dot(merge_in, merge_full, preferred_element_type=f32) + conv_out
    merged = gelu_exact(merge_pre).astype(bf16)
    up_pre = jnp.dot(merged, up_full, preferred_element_type=f32)
    up_act = gelu_exact(up_pre).astype(bf16)
    out_tok = (resid + jnp.dot(up_act, down_full, preferred_element_type=f32)).astype(bf16)
    cot_tok = cot_tokens[0]
    cot_tok_f = cot_tok.astype(f32)
    cot_chr_f = cot_chars[0].astype(f32)
    grad_down = jnp.einsum("tf,td->fd", up_act, cot_tok, preferred_element_type=f32)
    grad_act = jnp.einsum("td,fd->tf", cot_tok, down_full, preferred_element_type=f32)
    _, gelu_up_back = jax.vjp(gelu_exact, up_pre)
    grad_up_pre = gelu_up_back(grad_act)[0].astype(bf16)
    grad_up = jnp.einsum("tc,tf->cf", merged, grad_up_pre, preferred_element_type=f32)
    grad_merged = jnp.einsum("tf,cf->tc", grad_up_pre, up_full, preferred_element_type=f32)
    _, gelu_merge_back = jax.vjp(gelu_exact, merge_pre)
    grad_pre = gelu_merge_back(grad_merged)[0].astype(bf16)
    grad_merge = jnp.einsum("tc,te->ce", merge_in, grad_pre, preferred_element_type=f32)
    grad_merge_in = jnp.einsum("te,ce->tc", grad_pre, merge_full, preferred_element_type=f32)
    grad_conv = jnp.concatenate(
        [
            jnp.einsum(
                "tc,te->ce",
                padded[kernel : kernel + tok_rows],
                grad_pre,
                preferred_element_type=f32,
            )
            for kernel in range(3)
        ],
        axis=1,
    )
    grad_padded = padded_2(grad_pre, (("ctx", 0),), 1)
    grad_pooled = jnp.zeros((tok_rows, width), f32)
    for kernel in range(3):
        grad_pooled = grad_pooled + jnp.einsum(
            "te,ce->tc",
            grad_padded[2 - kernel : 2 - kernel + tok_rows],
            conv_full[:, kernel * width : (kernel + 1) * width],
            preferred_element_type=f32,
        )
    _, merge_norm_back = jax.vjp(normed, resid, merge_gain_f)
    grad_resid_norm, grad_merge_gain = merge_norm_back(grad_merge_in)
    grad_resid = cot_tok_f + grad_resid_norm
    grad_mixed = cot_chr_f + jnp.take(grad_pooled / root_counts[:, None], char_map, axis=0)
    shifted_f = jnp.concatenate([coef_f[1:], jnp.ones((1, half_width), f32)], axis=0)
    shifted_b = jnp.concatenate([jnp.ones((1, half_width), f32), coef_b[:-1]], axis=0)
    local_lam, cum_lam, lam_totals = scan_both(
        jnp.concatenate([shifted_f, shifted_b], axis=1), grad_mixed, False
    )
    edge = jnp.concatenate([coef_f[0], coef_b[-1]])[None, :]
    lams = local_lam + cum_lam * carried(lam_totals[:2] * edge, False)
    lam_f = lams[:, :half_width]
    lam_b = lams[:, half_width:]
    prev_f = jnp.concatenate([carry_in_f[None, :], state_f[:-1]], axis=0)
    grad_zeta_f = lam_f * (cand_f - keep_fwd[:, None] * prev_f) * zeta_f * (1.0 - zeta_f)
    grad_cand_f = lam_f * zeta_f * lift
    next_b = jnp.concatenate([state_b[1:], carry_in_b[None, :]], axis=0)
    grad_zeta_b = lam_b * (cand_b - keep_bwd[:, None] * next_b) * zeta_b * (1.0 - zeta_b)
    grad_cand_b = lam_b * zeta_b * lift
    grad_gates = jnp.concatenate(
        [grad_zeta_f, grad_cand_f, grad_zeta_b, grad_cand_b], axis=1
    ).astype(bf16)
    grad_gru = jnp.einsum("tc,tg->cg", char_low, grad_gates, preferred_element_type=f32)
    grad_char_norm = jnp.einsum("tg,cg->tc", grad_gates, gru_full, preferred_element_type=f32)
    _, char_norm_back = jax.vjp(normed, char_in, char_gain_f)
    grad_char_in, grad_char_gain = char_norm_back(grad_char_norm)
    grad_chars_out = (cot_chr_f + grad_char_in).astype(bf16)
    dot_stream, dot_proj = lax.psum(
        (jnp.sum(grad_resid * stream), jnp.sum(grad_resid * proj)), "ctx"
    )
    mean_gs = dot_stream / elements
    mean_gp = dot_proj / elements
    mean_sp = (cross_sum + rms_scale * sq_proj) / elements
    grad_stream = stream_scale * grad_resid - stream_scale**3 * mean_gs * stream
    mean_gsp = stream_scale * mean_gp - stream_scale**3 * mean_gs * mean_sp
    grad_proj = (rms_scale * grad_stream - rms_scale**3 * mean_gsp * proj).astype(bf16)
    grad_out_proj = jnp.einsum("tc,te->ce", attn_out, grad_proj, preferred_element_type=f32)
    grad_attn = jnp.einsum("te,ce->tc", grad_proj, out_full, preferred_element_type=f32).astype(
        bf16
    )
    grad_heads = grad_attn.reshape(tok_rows, HEADS, HEAD_DIM)
    row_term = jnp.einsum("qhe,qhe->hq", grad_heads.astype(f32), attn_heads)

    def step_block(dq_acc, inputs):
        key_blk, value_blk, docs_blk = inputs

        def step_used(acc):
            probs, dscores = grad_block(
                query_heads,
                key_blk,
                value_blk,
                grad_heads,
                query_docs,
                docs_blk,
                log_total,
                row_term,
            )
            acc = (
                acc
                + jnp.einsum("hqk,khe->qhe", dscores, key_blk, preferred_element_type=f32) * scale
            )
            dk_blk = (
                jnp.einsum("hqk,qhe->khe", dscores, query_heads, preferred_element_type=f32) * scale
            )
            dv_blk = jnp.einsum(
                "hqk,qhe->khe", probs.astype(bf16), grad_heads, preferred_element_type=f32
            )
            return (acc, (dk_blk, dv_blk))

        def step_skipped(acc):
            zero_blk = jnp.zeros((key_blk.shape[0], HEADS, HEAD_DIM), f32)
            return (acc, (zero_blk, zero_blk))

        return lax.cond(docs_meet(query_docs, docs_blk), step_used, step_skipped, dq_acc)

    dq_heads, key_terms = lax.scan(
        step_block,
        jnp.zeros((tok_rows, HEADS, HEAD_DIM), f32),
        (key_blocks, value_blocks, key_docs),
    )
    dk_local, dv_local = scatter_sums(
        [term.reshape(seq_len, width).astype(bf16) for term in key_terms],
        [((0, 0, width, True), (1, 0, width, False))],
        False,
        3,
        bf16,
    )
    grad_qkv_low = jnp.concatenate(
        [
            dq_heads.reshape(tok_rows, width).astype(bf16),
            dk_local,
            dv_local,
        ],
        axis=1,
    )
    grad_qkv = jnp.einsum("tc,tg->cg", attn_in, grad_qkv_low, preferred_element_type=f32)
    grad_attn_in = jnp.einsum("tg,cg->tc", grad_qkv_low, qkv_full, preferred_element_type=f32)
    _, attn_norm_back = jax.vjp(normed, token_in, attn_gain_f)
    grad_token_in, grad_attn_gain = attn_norm_back(grad_attn_in)
    grad_tokens_out = (grad_stream + grad_token_in).astype(bf16)
    gain_grads = jnp.stack([grad_attn_gain, grad_char_gain, grad_merge_gain], axis=1)
    gain_grads = jnp.pad(gain_grads, ((0, 0), (0, lane - 3)))
    early = [grad_down, grad_up, grad_merge, grad_conv]
    early = [part.astype(bf16) for part in early]
    down_shard, up_shard, merge_shard, conv_shard = scatter_sums(
        early,
        slots_of(early),
        True,
        4,
        f32,
    )
    late = [grad_gru, grad_out_proj, jnp.concatenate([grad_qkv, gain_grads], axis=1)]
    late = [part.astype(bf16) for part in late]
    gru_shard, out_shard, qkv_shard = scatter_sums(
        late,
        slots_of(late),
        True,
        5,
        f32,
    )
    gain_shard = qkv_shard[:, 3 * width :]
    shards = (
        gain_shard[:, 0],
        qkv_shard[:, : 3 * width],
        out_shard,
        gain_shard[:, 1],
        gru_shard,
        conv_shard,
        gain_shard[:, 2],
        merge_shard,
        up_shard,
        down_shard,
    )
    return (
        out_tok[None],
        out_chars[None],
        grad_tokens_out[None],
        grad_chars_out[None],
        shards[0],
        shards[1],
        shards[2],
        shards[3],
        shards[4],
        shards[5],
        shards[6],
        shards[7],
        shards[8],
        shards[9],
    )


def solution(mesh):
    in_specs = (
        P("wsh", "ctx", None),
        P("wsh", "ctx", None),
        P("wsh", "ctx", None),
        P("wsh", None),
        P(("ctx", "wsh")),
        P(("ctx", "wsh"), None),
        P(("ctx", "wsh"), None),
        P(("ctx", "wsh")),
        P(("ctx", "wsh"), None),
        P(("ctx", "wsh"), None),
        P(("ctx", "wsh")),
        P(("ctx", "wsh"), None),
        P(("ctx", "wsh"), None),
        P(("ctx", "wsh"), None),
        P("wsh", "ctx", None),
        P("wsh", "ctx", None),
    )
    out_specs = (
        P("wsh", "ctx", None),
        P("wsh", "ctx", None),
        P("wsh", "ctx", None),
        P("wsh", "ctx", None),
        P(("ctx", "wsh")),
        P(("ctx", "wsh"), None),
        P(("ctx", "wsh"), None),
        P(("ctx", "wsh")),
        P(("ctx", "wsh"), None),
        P(("ctx", "wsh"), None),
        P(("ctx", "wsh")),
        P(("ctx", "wsh"), None),
        P(("ctx", "wsh"), None),
        P(("ctx", "wsh"), None),
    )
    return jax.shard_map(body, mesh=mesh, in_specs=in_specs, out_specs=out_specs, check_vma=False)
```

```python
import functools
import math

import jax
import jax.numpy as jnp
from jax import lax
from jax.experimental import pallas as pl
from jax.experimental.pallas import tpu as pltpu
from jax.sharding import PartitionSpec as P

HEADS = 12
HEAD_DIM = 64


masked_score = -1e30


def masks_of(axis):
    return [1 << k for k in range(lax.axis_size(axis).bit_length() - 1)]


def place_of(axis, partner):
    here = {"ctx": lax.axis_index("ctx"), "wsh": lax.axis_index("wsh")}
    here[axis] = partner
    return (here["ctx"], here["wsh"])


def greet(over_wsh):
    barrier = pltpu.get_barrier_semaphore()
    partners = [
        place_of("ctx", lax.bitwise_xor(lax.axis_index("ctx"), mask)) for mask in masks_of("ctx")
    ]
    if over_wsh:
        partners = partners + [
            place_of("wsh", lax.bitwise_xor(lax.axis_index("wsh"), gap))
            for gap in range(1, lax.axis_size("wsh"))
        ]
    for partner in partners:
        pl.semaphore_signal(
            barrier, inc=1, device_id=partner, device_id_type=pl.DeviceIdType.MESH
        )
    pl.semaphore_wait(barrier, len(partners))


def ctx_bits(upward):
    masks = masks_of("ctx")
    middle = masks[1:]
    return (middle if upward else middle[::-1]) + masks[:1]


def ctx_bit(mask):
    return lax.rem(lax.div(lax.axis_index("ctx"), mask), 2)


def ctx_index(fixed):
    return tuple(
        fixed[mask] if mask in fixed else slice(None) for mask in reversed(masks_of("ctx"))
    )


def remote(src, dst, sems, number, partner):
    return pltpu.make_async_remote_copy(
        src_ref=src,
        dst_ref=dst,
        send_sem=sems[0].at[number],
        recv_sem=sems[1].at[number],
        device_id=partner,
        device_id_type=pl.DeviceIdType.MESH,
    )


def gather_kernel(slots, count, over_wsh, *refs):
    shards, outs = refs[:count], refs[count : 2 * count]
    sems, local_sems = refs[2 * count : 2 * count + 2], refs[2 * count + 2]
    width_w = lax.axis_size("wsh") if over_wsh else 1
    mine_w = lax.axis_index("wsh") if over_wsh else 0
    bits = len(masks_of("ctx"))
    per_stream = width_w - 1 + bits
    greet(over_wsh)
    streams = [stream for slot in slots for stream in slot]
    number_of = {stream: position for position, stream in enumerate(streams)}
    started = {}

    def start(stream, step):
        array, first, cols, upward = stream
        base = number_of[stream] * per_stream
        span = pl.ds(first, cols)
        out = outs[array]
        every = {mask: ctx_bit(mask) for mask in masks_of("ctx")}
        copies = []
        if step == 0:
            own = ctx_index(every) + (mine_w, slice(None), span)
            copy = pltpu.make_async_copy(
                shards[array].at[:, span], out.at[own], local_sems.at[number_of[stream]]
            )
            copies.append(copy)
            for gap in range(1, width_w):
                copies.append(
                    remote(
                        shards[array].at[:, span],
                        out.at[own],
                        sems,
                        base + gap - 1,
                        place_of("wsh", lax.bitwise_xor(mine_w, gap)),
                    )
                )
        else:
            order = ctx_bits(upward)
            held = {mask: every[mask] for mask in order[step - 1 :]}
            part = ctx_index(held) + (slice(None), slice(None), span)
            partner = place_of("ctx", lax.bitwise_xor(lax.axis_index("ctx"), order[step - 1]))
            copies.append(
                remote(out.at[part], out.at[part], sems, base + width_w - 1 + step - 1, partner)
            )
        for copy in copies:
            copy.start()
        started[stream, step] = copies

    def finish(stream, step):
        for position, copy in enumerate(started[stream, step]):
            if step == 0 and position == 0:
                copy.wait()
            else:
                copy.wait_recv()

    for tick in range(len(slots) + bits + 1):
        for number, slot in reversed(list(enumerate(slots))):
            step = tick - number
            for stream in slot:
                if 1 <= step <= bits + 1:
                    finish(stream, step - 1)
                if 0 <= step <= bits:
                    start(stream, step)
    for (stream, step), copies in started.items():
        for copy in copies[1:] if step == 0 else copies:
            copy.wait_send()


def gather_all(arrays, slots, over_wsh, collective):
    bits = len(masks_of("ctx"))
    width_w = lax.axis_size("wsh") if over_wsh else 1
    count = len(arrays)
    streams = sum(len(slot) for slot in slots)
    copies = streams * (width_w - 1 + bits)
    hbm = pl.BlockSpec(memory_space=pl.ANY)
    outs = pl.pallas_call(
        functools.partial(gather_kernel, slots, count, over_wsh),
        out_shape=tuple(
            jax.ShapeDtypeStruct((2,) * bits + (width_w,) + array.shape, array.dtype)
            for array in arrays
        ),
        in_specs=[hbm] * count,
        out_specs=(hbm,) * count,
        scratch_shapes=[
            pltpu.SemaphoreType.DMA((copies,)),
            pltpu.SemaphoreType.DMA((copies,)),
            pltpu.SemaphoreType.DMA((streams,)),
        ],
        compiler_params=pltpu.CompilerParams(
            collective_id=collective, has_side_effects=True, vmem_limit_bytes=4 << 20
        ),
        name="gather_all",
    )(*arrays)
    return [out.reshape((-1, out.shape[-1])) for out in outs]


def add_into(total_ref, extra_ref, fixed_total, fixed_extra, shape, rows, block_rows, span):
    steps = math.prod(shape) * (rows // block_rows)

    def step(position, carry):
        rest = position
        chunk = lax.rem(rest, rows // block_rows)
        rest = lax.div(rest, rows // block_rows)
        free = []
        for size in reversed(shape):
            free.append(lax.rem(rest, size))
            rest = lax.div(rest, size)
        free = free[::-1]
        take = iter(free)
        into = tuple(next(take) if entry is None else entry for entry in fixed_total)
        take = iter(free)
        source = tuple(next(take) if entry is None else entry for entry in fixed_extra)
        down = pl.ds(pl.multiple_of(chunk * block_rows, block_rows), block_rows)
        total_ref[into + (down, span)] = (
            total_ref[into + (down, span)] + extra_ref[source + (down, slice(None))]
        )
        return carry

    lax.fori_loop(0, steps, step, 0)


def scatter_kernel(slots, count, over_wsh, *refs):
    streams = [stream for slot in slots for stream in slot]
    grads, outs = refs[:count], refs[count : 2 * count]
    bits = len(masks_of("ctx"))
    held = refs[2 * count : 3 * count]
    rest = refs[3 * count :]
    per_stream_bufs = bits + (1 if over_wsh else 0)
    landing = {}
    for number, stream in enumerate(streams):
        landing[stream] = rest[number * per_stream_bufs : (number + 1) * per_stream_bufs]
    sems = rest[len(streams) * per_stream_bufs : len(streams) * per_stream_bufs + 2]
    local_sems = rest[len(streams) * per_stream_bufs + 2]
    width_w = lax.axis_size("wsh") if over_wsh else 1
    mine_w = lax.axis_index("wsh") if over_wsh else 0
    per_stream = width_w - 1 + bits
    number_of = {stream: position for position, stream in enumerate(streams)}
    every = {mask: ctx_bit(mask) for mask in masks_of("ctx")}
    low = masks_of("ctx")[0]
    started = {}
    greet(over_wsh)

    def start(stream, step):
        array, first, cols, upward = stream
        base = number_of[stream] * per_stream
        span = pl.ds(first, cols)
        order = ctx_bits(upward)[::-1]
        copies = []
        if step == 0:
            kept = ctx_index({low: every[low]}) + (slice(None), slice(None), span)
            copies.append(
                pltpu.make_async_copy(
                    grads[array].at[kept],
                    held[array].at[(slice(None),) * bits + (slice(None), span)],
                    local_sems.at[number_of[stream]],
                )
            )
            away = ctx_index({low: 1 - every[low]}) + (slice(None), slice(None), span)
            copies.append(
                remote(
                    grads[array].at[away],
                    landing[stream][0],
                    sems,
                    base,
                    place_of("ctx", lax.bitwise_xor(lax.axis_index("ctx"), low)),
                )
            )
        elif step < bits:
            fixed = {mask: every[mask] for mask in order[:step]}
            fixed[order[step]] = 1 - every[order[step]]
            away = ctx_index(fixed)[:-1] + (slice(None), slice(None), span)
            copies.append(
                remote(
                    held[array].at[away],
                    landing[stream][step],
                    sems,
                    base + step,
                    place_of("ctx", lax.bitwise_xor(lax.axis_index("ctx"), order[step])),
                )
            )
        elif over_wsh:
            here = ctx_index(every)[:-1]
            for gap in range(1, width_w):
                other = lax.bitwise_xor(mine_w, gap)
                copies.append(
                    remote(
                        held[array].at[here + (other, slice(None), span)],
                        landing[stream][bits].at[gap - 1],
                        sems,
                        base + bits + gap - 1,
                        place_of("wsh", other),
                    )
                )
        for copy in copies:
            copy.start()
        started[stream, step] = copies

    def finish(stream, step):
        array, first, cols, upward = stream
        span = pl.ds(first, cols)
        order = ctx_bits(upward)[::-1]
        for position, copy in enumerate(started[stream, step]):
            if step == 0 and position == 0:
                copy.wait()
            else:
                copy.wait_recv()
        rows = held[array].shape[-2]
        block_rows = rows if rows <= 24 else 32
        if step < bits:
            fixed = {mask: every[mask] for mask in order[: step + 1]}
            lead = ctx_index(fixed)[:-1]
            into = tuple(None if isinstance(entry, slice) else entry for entry in lead) + (None,)
            free = (2,) * (bits - 1 - step)
            add_into(
                held[array],
                landing[stream][step],
                into,
                (None,) * (len(free) + 1),
                free + (width_w,),
                rows,
                block_rows,
                span,
            )
        if step == bits or (step == bits - 1 and not over_wsh):
            here = ctx_index(every)[:-1] + (mine_w,)
            for chunk in range(0, rows, block_rows):
                down = pl.ds(chunk, block_rows)
                total = held[array][here + (down, span)].astype(jnp.float32)
                for gap in range(1, width_w):
                    total = total + landing[stream][bits][gap - 1, down, :].astype(jnp.float32)
                outs[array][down, span] = total.astype(outs[array].dtype)

    steps = bits + (1 if over_wsh else 0)
    for tick in range(len(slots) + steps):
        for number, slot in reversed(list(enumerate(slots))):
            step = tick - number
            for stream in slot:
                if 1 <= step <= steps:
                    finish(stream, step - 1)
                if 0 <= step < steps:
                    start(stream, step)
    for (stream, step), copies in started.items():
        for copy in copies[1:] if step == 0 else copies:
            copy.wait_send()


def scatter_sums(arrays, slots, over_wsh, collective, dtype):
    bits = len(masks_of("ctx"))
    width_w = lax.axis_size("wsh") if over_wsh else 1
    count = len(arrays)
    parts = width_w << bits
    rows = [array.shape[0] // parts for array in arrays]
    shaped = [
        array.reshape((2,) * bits + (width_w, row, array.shape[1]))
        for array, row in zip(arrays, rows)
    ]
    streams = [stream for slot in slots for stream in slot]
    copies = len(streams) * (width_w - 1 + bits)
    buffers = [
        pltpu.VMEM((2,) * (bits - 1) + (width_w, row, array.shape[1]), array.dtype)
        for array, row in zip(arrays, rows)
    ]
    for array, first, cols, upward in streams:
        kind = arrays[array].dtype
        for step in range(bits):
            buffers.append(
                pltpu.VMEM((2,) * (bits - 1 - step) + (width_w, rows[array], cols), kind)
            )
        if over_wsh:
            buffers.append(pltpu.VMEM((width_w - 1, rows[array], cols), kind))
    return pl.pallas_call(
        functools.partial(scatter_kernel, slots, count, over_wsh),
        out_shape=tuple(
            jax.ShapeDtypeStruct((row, array.shape[1]), dtype) for array, row in zip(arrays, rows)
        ),
        in_specs=[pl.BlockSpec(memory_space=pl.ANY)] * count,
        out_specs=(pl.BlockSpec(memory_space=pltpu.VMEM),) * count,
        scratch_shapes=buffers
        + [
            pltpu.SemaphoreType.DMA((copies,)),
            pltpu.SemaphoreType.DMA((copies,)),
            pltpu.SemaphoreType.DMA((len(streams),)),
        ],
        compiler_params=pltpu.CompilerParams(
            collective_id=collective, has_side_effects=True, vmem_limit_bytes=56 << 20
        ),
        name="scatter_sums",
    )(*shaped)


def halves(number, cols):
    pieces = 2 if cols < 2304 else 4
    cuts = [cols * piece // pieces // 128 * 128 for piece in range(pieces)] + [cols]
    streams = [
        (number, cuts[piece], cuts[piece + 1] - cuts[piece], piece % 2 == 0)
        for piece in range(pieces)
    ]
    return [tuple(streams[piece : piece + 2]) for piece in range(0, pieces, 2)]


def slots_of(arrays):
    return [
        slot for number, part in enumerate(arrays) for slot in halves(number, part.shape[1])
    ]


HEAD_GROUPS = 4


def groups():
    apart = lax.axis_size("ctx") // HEAD_GROUPS
    mine = lax.axis_index("ctx")
    return apart, lax.div(mine, apart), lax.rem(mine, apart)


def ctx_partner(gap):
    return place_of("ctx", lax.bitwise_xor(lax.axis_index("ctx"), gap))


def greet_ctx(gaps):
    barrier = pltpu.get_barrier_semaphore()
    for gap in gaps:
        pl.semaphore_signal(
            barrier, inc=1, device_id=ctx_partner(gap), device_id_type=pl.DeviceIdType.MESH
        )
    pl.semaphore_wait(barrier, len(gaps))


def spread_kernel(qkv_ref, q_out, kv_out, send_q, send_kv, send_sem, recv_sem, local_sem):
    apart, group, inner = groups()
    width = qkv_ref.shape[1] // 3
    cols = width // HEAD_GROUPS
    mine = lax.axis_index("ctx")
    sems = (send_sem, recv_sem)
    gaps = [gap * apart for gap in range(1, HEAD_GROUPS)] + list(range(1, apart))
    for other in range(HEAD_GROUPS):
        send_q[other] = qkv_ref[:, other * cols : (other + 1) * cols]
        for part in range(2):
            first = (part + 1) * width + other * cols
            send_kv[other, :, part * cols : (part + 1) * cols] = qkv_ref[:, first : first + cols]
    greet_ctx(gaps)
    kv_copies, q_copies = [], []
    for gap in range(1, HEAD_GROUPS):
        other = lax.bitwise_xor(group, gap)
        partner = ctx_partner(gap * apart)
        copy = remote(send_kv.at[other], kv_out.at[mine], sems, gap - 1, partner)
        copy.start()
        kv_copies.append(copy)
    for gap in range(1, HEAD_GROUPS):
        other = lax.bitwise_xor(group, gap)
        partner = ctx_partner(gap * apart)
        copy = remote(send_q.at[other], q_out.at[group], sems, HEAD_GROUPS - 2 + gap, partner)
        copy.start()
        q_copies.append(copy)
    own = [
        pltpu.make_async_copy(send_kv.at[group], kv_out.at[mine], local_sem.at[0]),
        pltpu.make_async_copy(send_q.at[group], q_out.at[group], local_sem.at[1]),
    ]
    for copy in own:
        copy.start()
    own[0].wait()
    number = 2 * (HEAD_GROUPS - 1)
    passed = []
    for gap in range(HEAD_GROUPS):
        if gap:
            kv_copies[gap - 1].wait_recv()
        slot = lax.bitwise_xor(mine, gap * apart)
        for near in range(1, apart):
            copy = remote(kv_out.at[slot], kv_out.at[slot], sems, number, ctx_partner(near))
            copy.start()
            passed.append(copy)
            number = number + 1
    own[1].wait()
    for copy in q_copies:
        copy.wait_recv()
    for copy in passed:
        copy.wait_recv()
    for copy in kv_copies + q_copies + passed:
        copy.wait_send()


def spread_heads(qkv, collective):
    rows = qkv.shape[0]
    count = lax.axis_size("ctx")
    apart = count // HEAD_GROUPS
    cols = qkv.shape[1] // 3 // HEAD_GROUPS
    copies = 2 * (HEAD_GROUPS - 1) + HEAD_GROUPS * (apart - 1)
    hbm = pl.BlockSpec(memory_space=pl.ANY)
    return pl.pallas_call(
        spread_kernel,
        out_shape=(
            jax.ShapeDtypeStruct((HEAD_GROUPS, rows, cols), qkv.dtype),
            jax.ShapeDtypeStruct((count, rows, 2 * cols), qkv.dtype),
        ),
        in_specs=[pl.BlockSpec(memory_space=pltpu.VMEM)],
        out_specs=(hbm, hbm),
        scratch_shapes=[
            pltpu.VMEM((HEAD_GROUPS, rows, cols), qkv.dtype),
            pltpu.VMEM((HEAD_GROUPS, rows, 2 * cols), qkv.dtype),
            pltpu.SemaphoreType.DMA((copies,)),
            pltpu.SemaphoreType.DMA((copies,)),
            pltpu.SemaphoreType.DMA((2,)),
        ],
        compiler_params=pltpu.CompilerParams(
            collective_id=collective, has_side_effects=True, vmem_limit_bytes=16 << 20
        ),
        name="spread_heads",
    )(qkv)


def head_rows(value, head):
    rows = lax.broadcasted_iota(jnp.int32, value.shape, 0)
    inside = (rows >= head * HEAD_DIM) & (rows < (head + 1) * HEAD_DIM)
    return jnp.where(inside, value, jnp.zeros_like(value))


def head_cols(value, head):
    cols = lax.broadcasted_iota(jnp.int32, value.shape, 1)
    inside = (cols >= head * HEAD_DIM) & (cols < (head + 1) * HEAD_DIM)
    return jnp.where(inside, value, jnp.zeros_like(value))


def turned(value):
    return jnp.transpose(value.astype(jnp.float32))


def dot32(left, right):
    return jnp.dot(left, right, preferred_element_type=jnp.float32)


def key_mask(key_block, size, spans_ref, slot):
    keys = key_block * size + lax.broadcasted_iota(jnp.int32, (size, size), 0)
    return (keys >= spans_ref[slot, 0:1, :]) & (keys < spans_ref[slot, 1:2, :])


def attend_kernel(bounds, q_ref, kv_ref, spans_ref, o_ref, exact_ref, log_ref, vt_s, qt_s, ot_s, stat_s):
    blocks, size, both = kv_ref.shape
    cols = both // 2
    heads = cols // HEAD_DIM

    def turn_values(block, carry):
        vt_s[block] = turned(kv_ref[block, :, cols:]).astype(jnp.bfloat16)
        return carry

    lax.fori_loop(0, blocks, turn_values, 0)

    def query_block(slot, carry):
        qt = (turned(q_ref[slot]) * HEAD_DIM ** (-0.5)).astype(jnp.bfloat16)
        for head in range(heads):
            qt_s[head] = head_rows(qt, head)
        ot_s[...] = jnp.zeros_like(ot_s)
        stat_s[0] = jnp.full_like(stat_s[0], masked_score)
        stat_s[1] = jnp.zeros_like(stat_s[1])

        def key_step(block, carry):
            allowed = key_mask(block, size, spans_ref, slot)
            keys = kv_ref[block, :, :cols]
            for head in range(heads):
                row = slice(head, head + 1)
                part = slice(head * HEAD_DIM, (head + 1) * HEAD_DIM)
                scores = jnp.where(allowed, dot32(keys, qt_s[head]), masked_score)
                old = stat_s[0, row, :]
                top = jnp.maximum(old, jnp.max(scores, axis=0, keepdims=True))
                factor = jnp.exp(old - top)
                weights = jnp.exp(scores - top)
                stat_s[0, row, :] = top
                stat_s[1, row, :] = stat_s[1, row, :] * factor + jnp.sum(
                    weights, axis=0, keepdims=True
                )
                ot_s[part, :] = ot_s[part, :] * factor + dot32(
                    vt_s[block, part, :], weights.astype(jnp.bfloat16)
                )
            return carry

        lax.fori_loop(bounds[slot, 0], bounds[slot, 1], key_step, 0)
        for head in range(heads):
            row = slice(head, head + 1)
            part = slice(head * HEAD_DIM, (head + 1) * HEAD_DIM)
            ot_s[part, :] = ot_s[part, :] / stat_s[1, row, :]
            log_ref[slot, row, :] = stat_s[0, row, :] + jnp.log(stat_s[1, row, :])
        exact = jnp.transpose(ot_s[...])
        exact_ref[slot] = exact
        o_ref[slot] = exact.astype(jnp.bfloat16)
        return carry

    lax.fori_loop(0, q_ref.shape[0], query_block, 0)


def attend_back_kernel(
    bounds, q_ref, kv_ref, g_ref, exact_ref, log_ref, spans_ref, dq_ref, dkv_ref, v_s, kt_s, qt_s, gt_s,
    qn_s, gn_s, dqt_s, row_s, dk_s, dv_s
):
    blocks, size, both = kv_ref.shape
    cols = both // 2
    heads = cols // HEAD_DIM
    scale = HEAD_DIM ** (-0.5)
    bf16 = jnp.bfloat16

    def turn_keys(block, carry):
        kt_s[block] = turned(kv_ref[block, :, :cols]).astype(bf16)
        v_s[block] = kv_ref[block, :, cols:]
        dk_s[block] = jnp.zeros(dk_s.shape[1:], jnp.float32)
        dv_s[block] = jnp.zeros(dv_s.shape[1:], jnp.float32)
        return carry

    lax.fori_loop(0, blocks, turn_keys, 0)

    def query_block(slot, carry):
        qn = (q_ref[slot].astype(jnp.float32) * scale).astype(bf16)
        gn = g_ref[slot]
        qt = turned(qn).astype(bf16)
        gt32 = turned(gn)
        products = gt32 * jnp.transpose(exact_ref[slot])
        gt = gt32.astype(bf16)
        for head in range(heads):
            part = slice(head * HEAD_DIM, (head + 1) * HEAD_DIM)
            qt_s[head] = head_rows(qt, head)
            gt_s[head] = head_rows(gt, head)
            qn_s[head] = head_cols(qn, head)
            gn_s[head] = head_cols(gn, head)
            row_s[head : head + 1, :] = jnp.sum(products[part], axis=0, keepdims=True)
        dqt_s[...] = jnp.zeros_like(dqt_s)

        def key_step(block, carry):
            allowed = key_mask(block, size, spans_ref, slot)
            keys = kv_ref[block, :, :cols]
            values = v_s[block]
            dk = jnp.zeros(dk_s.shape[1:], jnp.float32)
            dv = jnp.zeros(dv_s.shape[1:], jnp.float32)
            for head in range(heads):
                row = slice(head, head + 1)
                part = slice(head * HEAD_DIM, (head + 1) * HEAD_DIM)
                scores = jnp.where(allowed, dot32(keys, qt_s[head]), masked_score)
                weights = jnp.exp(scores - log_ref[slot, row, :])
                slopes = dot32(values, gt_s[head])
                ds = (weights * (slopes - row_s[row, :])).astype(bf16)
                dqt_s[part, :] = dqt_s[part, :] + dot32(kt_s[block, part, :], ds)
                dk = dk + dot32(ds, qn_s[head])
                dv = dv + dot32(weights.astype(bf16), gn_s[head])
            dk_s[block] = dk_s[block] + dk
            dv_s[block] = dv_s[block] + dv
            return carry

        lax.fori_loop(bounds[slot, 0], bounds[slot, 1], key_step, 0)
        dq_ref[slot] = (jnp.transpose(dqt_s[...]) * scale).astype(bf16)
        return carry

    lax.fori_loop(0, q_ref.shape[0], query_block, 0)

    def write(block, carry):
        dkv_ref[block, :, :cols] = dk_s[block].astype(bf16)
        dkv_ref[block, :, cols:] = dv_s[block].astype(bf16)
        return carry

    lax.fori_loop(0, blocks, write, 0)


def attend(bounds, q, kv, spans):
    slots, size, cols = q.shape
    blocks = kv.shape[0]
    heads = cols // HEAD_DIM
    whole = pl.BlockSpec(memory_space=pltpu.VMEM)
    f32, bf16 = jnp.float32, jnp.bfloat16
    return pl.pallas_call(
        attend_kernel,
        out_shape=(
            jax.ShapeDtypeStruct(q.shape, bf16),
            jax.ShapeDtypeStruct(q.shape, f32),
            jax.ShapeDtypeStruct((slots, 8, size), f32),
        ),
        in_specs=[pl.BlockSpec(memory_space=pltpu.SMEM), whole, whole, whole],
        out_specs=(whole, whole, whole),
        scratch_shapes=[
            pltpu.VMEM((blocks, cols, size), bf16),
            pltpu.VMEM((heads, cols, size), bf16),
            pltpu.VMEM((cols, size), f32),
            pltpu.VMEM((2, 8, size), f32),
        ],
        compiler_params=pltpu.CompilerParams(vmem_limit_bytes=32 << 20),
        name="attend",
    )(bounds, q, kv, spans)


def attend_back(bounds, q, kv, g, exact, log, spans):
    slots, size, cols = q.shape
    blocks = kv.shape[0]
    heads = cols // HEAD_DIM
    whole = pl.BlockSpec(memory_space=pltpu.VMEM)
    f32, bf16 = jnp.float32, jnp.bfloat16
    return pl.pallas_call(
        attend_back_kernel,
        out_shape=(
            jax.ShapeDtypeStruct(q.shape, bf16),
            jax.ShapeDtypeStruct(kv.shape, bf16),
        ),
        in_specs=[pl.BlockSpec(memory_space=pltpu.SMEM)] + [whole] * 6,
        out_specs=(whole, whole),
        scratch_shapes=[
            pltpu.VMEM((blocks, size, cols), bf16),
            pltpu.VMEM((blocks, cols, size), bf16),
            pltpu.VMEM((heads, cols, size), bf16),
            pltpu.VMEM((heads, cols, size), bf16),
            pltpu.VMEM((heads, size, cols), bf16),
            pltpu.VMEM((heads, size, cols), bf16),
            pltpu.VMEM((cols, size), f32),
            pltpu.VMEM((8, size), f32),
            pltpu.VMEM((blocks, size, cols), f32),
            pltpu.VMEM((blocks, size, cols), f32),
        ],
        compiler_params=pltpu.CompilerParams(vmem_limit_bytes=48 << 20),
        name="attend_back",
    )(bounds, q, kv, g, exact, log, spans)


def exchange_sums(sums_ref, sems, base):
    mine = lax.axis_index("ctx")
    copies = []
    for gap in range(1, lax.axis_size("ctx")):
        copy = remote(sums_ref.at[mine], sums_ref.at[mine], sems, base + gap - 1, ctx_partner(gap))
        copy.start()
        copies.append(copy)
    return copies


def total_of(sums_ref):
    total = sums_ref[0]
    for slot in range(1, sums_ref.shape[0]):
        total = total + sums_ref[slot]
    return total


def summed(value):
    return jnp.sum(jnp.sum(value, axis=0, keepdims=True), axis=1, keepdims=True)


def join_kernel(
    elements, o_ref, tokens_ref, weight_ref, attn_ref, proj_ref, resid_ref, stat_ref, land, sums, send_sem,
    recv_sem, local_sem
):
    apart, group, inner = groups()
    cols = o_ref.shape[2]
    sems = (send_sem, recv_sem)
    greet_ctx(list(range(1, lax.axis_size("ctx"))))
    copies = []
    for gap in range(1, HEAD_GROUPS):
        other = lax.bitwise_xor(group, gap)
        copy = remote(o_ref.at[other], land.at[group], sems, gap - 1, ctx_partner(gap * apart))
        copy.start()
        copies.append(copy)
    own = pltpu.make_async_copy(o_ref.at[group], land.at[group], local_sem.at[0])
    own.start()
    tokens = tokens_ref[...].astype(jnp.float32)
    square = summed(tokens * tokens)
    own.wait()
    for copy in copies:
        copy.wait_recv()
    proj = jnp.zeros(proj_ref.shape, jnp.float32)
    for other in range(HEAD_GROUPS):
        part = land[other]
        attn_ref[:, other * cols : (other + 1) * cols] = part
        proj = proj + dot32(part, weight_ref[other * cols : (other + 1) * cols, :])
    proj_ref[...] = proj
    row = lax.broadcasted_iota(jnp.int32, sums.shape[1:], 0)
    mine = lax.axis_index("ctx")
    sums[mine] = jnp.where(
        row == 0,
        summed(proj * proj),
        jnp.where(row == 1, summed(tokens * proj), jnp.where(row == 2, square, 0.0)),
    )
    small = exchange_sums(sums, sems, HEAD_GROUPS - 1)
    for copy in small:
        copy.wait_recv()
    total = total_of(sums)
    stat_ref[...] = total
    sq_proj, cross, sq_tok = total[0:1, 0:1], total[1:2, 0:1], total[2:3, 0:1]
    rms_scale = lax.rsqrt(sq_proj / elements + 1e-06)
    stream_sq = (sq_tok + 2.0 * rms_scale * cross + rms_scale * rms_scale * sq_proj) / elements
    stream_scale = lax.rsqrt(stream_sq + 1e-06)
    resid_ref[...] = (tokens + proj_ref[...] * rms_scale) * stream_scale
    for copy in copies + small:
        copy.wait_send()


def join_heads(o, tokens, weight, elements, collective):
    rows, width = tokens.shape
    count = lax.axis_size("ctx")
    copies = HEAD_GROUPS - 1 + count - 1
    whole = pl.BlockSpec(memory_space=pltpu.VMEM)
    f32, bf16 = jnp.float32, jnp.bfloat16
    return pl.pallas_call(
        functools.partial(join_kernel, elements),
        out_shape=(
            jax.ShapeDtypeStruct((rows, width), bf16),
            jax.ShapeDtypeStruct((rows, width), f32),
            jax.ShapeDtypeStruct((rows, width), f32),
            jax.ShapeDtypeStruct((8, 128), f32),
        ),
        in_specs=[whole] * 3,
        out_specs=(whole,) * 4,
        scratch_shapes=[
            pltpu.VMEM(o.shape, bf16),
            pltpu.VMEM((count, 8, 128), f32),
            pltpu.SemaphoreType.DMA((copies,)),
            pltpu.SemaphoreType.DMA((copies,)),
            pltpu.SemaphoreType.DMA((1,)),
        ],
        compiler_params=pltpu.CompilerParams(
            collective_id=collective, has_side_effects=True, vmem_limit_bytes=24 << 20
        ),
        name="join_heads",
    )(o, tokens, weight)


def part_kernel(
    elements, resid_grad_ref, proj_ref, tokens_ref, weight_ref, stat_ref, stream_grad_ref, proj_grad_ref,
    g_out, send, sums, send_sem, recv_sem, local_sem
):
    apart, group, inner = groups()
    cols = g_out.shape[2]
    sems = (send_sem, recv_sem)
    greet_ctx(list(range(1, lax.axis_size("ctx"))))
    mine = lax.axis_index("ctx")
    sq_proj, cross, sq_tok = stat_ref[0:1, 0:1], stat_ref[1:2, 0:1], stat_ref[2:3, 0:1]
    rms_scale = lax.rsqrt(sq_proj / elements + 1e-06)
    stream_sq = (sq_tok + 2.0 * rms_scale * cross + rms_scale * rms_scale * sq_proj) / elements
    stream_scale = lax.rsqrt(stream_sq + 1e-06)
    stream = tokens_ref[...].astype(jnp.float32) + proj_ref[...] * rms_scale
    row = lax.broadcasted_iota(jnp.int32, sums.shape[1:], 0)
    sums[mine] = jnp.where(
        row == 0,
        summed(resid_grad_ref[...] * stream),
        jnp.where(row == 1, summed(resid_grad_ref[...] * proj_ref[...]), 0.0),
    )
    small = exchange_sums(sums, sems, HEAD_GROUPS - 1)
    for copy in small:
        copy.wait_recv()
    total = total_of(sums)
    mean_gs = total[0:1, 0:1] / elements
    mean_gp = total[1:2, 0:1] / elements
    mean_sp = (cross + rms_scale * sq_proj) / elements
    cubed = stream_scale * stream_scale * stream_scale
    stream_grad = stream_scale * resid_grad_ref[...] - cubed * mean_gs * stream
    stream_grad_ref[...] = stream_grad
    mean_gsp = stream_scale * mean_gp - cubed * mean_gs * mean_sp
    proj_grad = (
        rms_scale * stream_grad - rms_scale * rms_scale * rms_scale * mean_gsp * proj_ref[...]
    ).astype(jnp.bfloat16)
    proj_grad_ref[...] = proj_grad
    for other in range(HEAD_GROUPS):
        send[other] = lax.dot_general(
            proj_grad,
            weight_ref[other * cols : (other + 1) * cols, :],
            (((1,), (1,)), ((), ())),
            preferred_element_type=jnp.float32,
        ).astype(jnp.bfloat16)
    copies = []
    for gap in range(1, HEAD_GROUPS):
        other = lax.bitwise_xor(group, gap)
        copy = remote(send.at[other], g_out.at[group], sems, gap - 1, ctx_partner(gap * apart))
        copy.start()
        copies.append(copy)
    own = pltpu.make_async_copy(send.at[group], g_out.at[group], local_sem.at[0])
    own.start()
    own.wait()
    for copy in copies:
        copy.wait_recv()
    for copy in copies + small:
        copy.wait_send()


def part_heads(resid_grad, proj, tokens, weight, stat, elements, collective):
    rows, width = tokens.shape
    count = lax.axis_size("ctx")
    copies = HEAD_GROUPS - 1 + count - 1
    cols = width // HEAD_GROUPS
    whole = pl.BlockSpec(memory_space=pltpu.VMEM)
    f32, bf16 = jnp.float32, jnp.bfloat16
    return pl.pallas_call(
        functools.partial(part_kernel, elements),
        out_shape=(
            jax.ShapeDtypeStruct((rows, width), f32),
            jax.ShapeDtypeStruct((rows, width), bf16),
            jax.ShapeDtypeStruct((HEAD_GROUPS, rows, cols), bf16),
        ),
        in_specs=[whole] * 5,
        out_specs=(whole, whole, pl.BlockSpec(memory_space=pl.ANY)),
        scratch_shapes=[
            pltpu.VMEM((HEAD_GROUPS, rows, cols), bf16),
            pltpu.VMEM((count, 8, 128), f32),
            pltpu.SemaphoreType.DMA((copies,)),
            pltpu.SemaphoreType.DMA((copies,)),
            pltpu.SemaphoreType.DMA((1,)),
        ],
        compiler_params=pltpu.CompilerParams(
            collective_id=collective, has_side_effects=True, vmem_limit_bytes=24 << 20
        ),
        name="part_heads",
    )(resid_grad, proj, tokens, weight, stat)


def collect_kernel(dq_ref, dkv_ref, out_ref, near_land, own_s, q_land, kv_land, send_sem, recv_sem, local_sem):
    apart, group, inner = groups()
    cols = dq_ref.shape[2]
    rows = dq_ref.shape[1]
    width = cols * HEAD_GROUPS
    sems = (send_sem, recv_sem)
    gaps = [gap * apart for gap in range(1, HEAD_GROUPS)] + list(range(1, apart))
    greet_ctx(gaps)
    number = 0
    near = []
    for gap in range(1, apart):
        other = lax.bitwise_xor(inner, gap)
        copy = remote(dkv_ref.at[:, other], near_land.at[gap - 1], sems, number, ctx_partner(gap))
        copy.start()
        near.append(copy)
        number = number + 1
    own = pltpu.make_async_copy(dkv_ref.at[:, inner], own_s, local_sem.at[0])
    own.start()
    own_q = pltpu.make_async_copy(dq_ref.at[group], q_land.at[group], local_sem.at[1])
    own_q.start()
    far_q = []
    for gap in range(1, HEAD_GROUPS):
        other = lax.bitwise_xor(group, gap)
        copy = remote(dq_ref.at[other], q_land.at[group], sems, number, ctx_partner(gap * apart))
        copy.start()
        far_q.append(copy)
        number = number + 1
    own.wait()
    for copy in near:
        copy.wait_recv()
    chunk = 32

    def add(position, carry):
        slot = lax.div(position, rows // chunk)
        down = pl.ds(pl.multiple_of(lax.rem(position, rows // chunk) * chunk, chunk), chunk)
        total = own_s[slot, down, :].astype(jnp.float32)
        for gap in range(1, apart):
            total = total + near_land[gap - 1, slot, down, :].astype(jnp.float32)
        own_s[slot, down, :] = total.astype(own_s.dtype)
        return carry

    lax.fori_loop(0, HEAD_GROUPS * (rows // chunk), add, 0)
    own_kv = pltpu.make_async_copy(own_s.at[group], kv_land.at[group], local_sem.at[2])
    own_kv.start()
    far_kv = []
    for gap in range(1, HEAD_GROUPS):
        other = lax.bitwise_xor(group, gap)
        copy = remote(own_s.at[other], kv_land.at[group], sems, number, ctx_partner(gap * apart))
        copy.start()
        far_kv.append(copy)
        number = number + 1
    own_q.wait()
    for copy in far_q:
        copy.wait_recv()
    for other in range(HEAD_GROUPS):
        out_ref[:, other * cols : (other + 1) * cols] = q_land[other]
    own_kv.wait()
    for copy in far_kv:
        copy.wait_recv()
    for other in range(HEAD_GROUPS):
        for part in range(2):
            first = (part + 1) * width + other * cols
            out_ref[:, first : first + cols] = kv_land[other, :, part * cols : (part + 1) * cols]
    for copy in near + far_q + far_kv:
        copy.wait_send()


def collect_heads(dq, dkv, collective):
    slots, rows, cols = dq.shape
    count = lax.axis_size("ctx")
    apart = count // HEAD_GROUPS
    copies = apart - 1 + 2 * (HEAD_GROUPS - 1)
    hbm = pl.BlockSpec(memory_space=pl.ANY)
    bf16 = jnp.bfloat16
    return pl.pallas_call(
        collect_kernel,
        out_shape=jax.ShapeDtypeStruct((rows, 3 * cols * HEAD_GROUPS), bf16),
        in_specs=[hbm, hbm],
        out_specs=pl.BlockSpec(memory_space=pltpu.VMEM),
        scratch_shapes=[
            pltpu.VMEM((max(apart - 1, 1), HEAD_GROUPS, rows, 2 * cols), bf16),
            pltpu.VMEM((HEAD_GROUPS, rows, 2 * cols), bf16),
            pltpu.VMEM((HEAD_GROUPS, rows, cols), bf16),
            pltpu.VMEM((HEAD_GROUPS, rows, 2 * cols), bf16),
            pltpu.SemaphoreType.DMA((copies,)),
            pltpu.SemaphoreType.DMA((copies,)),
            pltpu.SemaphoreType.DMA((3,)),
        ],
        compiler_params=pltpu.CompilerParams(
            collective_id=collective, has_side_effects=True, vmem_limit_bytes=24 << 20
        ),
        name="collect_heads",
    )(dq, dkv.reshape(HEAD_GROUPS, apart, rows, 2 * cols))


def scan_kernel(forward_first, a_ref, b_ref, local_ref, cum_ref, total_ref, coef_s, term_s):
    rows, width = a_ref.shape
    segments = 8
    length = rows // segments
    lanes = 128
    chunks = width // lanes
    half = chunks // 2
    ahead = [(chunk < half) == forward_first for chunk in range(chunks)]
    for chunk in range(chunks):
        span = pl.ds(chunk * rows, rows)
        coef_s[span, :] = a_ref[:, pl.ds(chunk * lanes, lanes)]
        term_s[span, :] = b_ref[:, pl.ds(chunk * lanes, lanes)]

    def step(j, carry):
        states, prods = carry
        new_states, new_prods = [], []
        for chunk in range(chunks):
            place = j if ahead[chunk] else length - 1 - j
            where = (pl.ds(chunk * rows + place, segments, stride=length), slice(None))
            coef = coef_s[where]
            state = coef * states[chunk] + term_s[where]
            prod = coef * prods[chunk]
            term_s[where] = state
            coef_s[where] = prod
            new_states.append(state)
            new_prods.append(prod)
        return (tuple(new_states), tuple(new_prods))

    zero = jnp.zeros((segments, lanes), jnp.float32)
    one = jnp.ones((segments, lanes), jnp.float32)
    states, prods = lax.fori_loop(
        0, length, step, ((zero,) * chunks, (one,) * chunks), unroll=4
    )
    for chunk in range(chunks):
        cols = pl.ds(chunk * lanes, lanes)
        carry = jnp.zeros((1, lanes), jnp.float32)
        prod = jnp.ones((1, lanes), jnp.float32)
        order = range(segments) if ahead[chunk] else range(segments - 1, -1, -1)
        for segment in order:
            span = (pl.ds(segment * length, length), cols)
            held = pl.ds(chunk * rows + segment * length, length)
            cum = coef_s[held, :]
            local_ref[span] = term_s[held, :] + cum * carry
            cum_ref[span] = cum * prod
            end_prod = prods[chunk][segment : segment + 1]
            carry = end_prod * carry + states[chunk][segment : segment + 1]
            prod = end_prod * prod
        total_ref[0:1, cols] = prod
        total_ref[1:2, cols] = carry


def scan_both(coefs, terms, forward_first):
    rows, width = coefs.shape
    full = jax.ShapeDtypeStruct((rows, width), jnp.float32)
    whole = pl.BlockSpec(memory_space=pltpu.VMEM)
    return pl.pallas_call(
        functools.partial(scan_kernel, forward_first),
        out_shape=(full, full, jax.ShapeDtypeStruct((8, width), jnp.float32)),
        in_specs=[whole, whole],
        out_specs=(whole, whole, whole),
        scratch_shapes=[pltpu.VMEM((rows * width // 128, 128), jnp.float32)] * 2,
        compiler_params=pltpu.CompilerParams(vmem_limit_bytes=32 << 20),
        cost_estimate=pl.CostEstimate(
            flops=8 * rows * width, bytes_accessed=16 * rows * width, transcendentals=0
        ),
        name="scan_both",
    )(coefs, terms)


def carried(totals, forward_first):
    count, mine = lax.axis_size("ctx"), lax.axis_index("ctx")
    pieces = lax.all_gather(totals[:2], "ctx")
    half = totals.shape[1] // 2
    low = jnp.zeros((1, half), jnp.float32)
    high = jnp.zeros((1, half), jnp.float32)
    for position in range(count - 1):
        back = count - 1 - position
        first, second = (position, back) if forward_first else (back, position)
        ahead_ok = (first < mine) if forward_first else (first > mine)
        behind_ok = (second > mine) if forward_first else (second < mine)
        low = jnp.where(
            ahead_ok, pieces[first, 0:1, :half] * low + pieces[first, 1:2, :half], low
        )
        high = jnp.where(
            behind_ok, pieces[second, 0:1, half:] * high + pieces[second, 1:2, half:], high
        )
    return jnp.concatenate([low, high], axis=1)


def padded_2(cells, sides, width):
    for axis, dim in sides:
        count = lax.axis_size(axis)
        ends = count - 1
        head = lax.slice_in_dim(cells, 0, width, axis=dim)
        tail = lax.slice_in_dim(cells, cells.shape[dim] - width, cells.shape[dim], axis=dim)
        cells = jnp.concatenate(
            [
                lax.ppermute(tail, axis, [(i, (i + 1) % count) for i in range(ends)]),
                cells,
                lax.ppermute(head, axis, [((i + 1) % count, i) for i in range(ends)]),
            ],
            axis=dim,
        )
    return cells


def normed(values, scales):
    average = jnp.mean(values, axis=-1, keepdims=True)
    centred = values - average
    spread = jnp.mean(centred * centred, axis=-1, keepdims=True)
    return centred * lax.rsqrt(spread + 1e-05) * scales


def gelu_exact(values):
    return jax.nn.gelu(values, approximate=False)


def body(
    tokens,
    chars,
    char_token,
    doc_lengths,
    gain_attn,
    qkv_weight,
    out_weight,
    gain_char,
    gru_weight,
    conv_weight,
    gain_merge,
    merge_weight,
    up_weight,
    down_weight,
    cot_tokens,
    cot_chars,
):
    f32 = jnp.float32
    bf16 = jnp.bfloat16
    every = ("ctx", "wsh")
    width = tokens.shape[2]
    lane = 128
    gain_block = jnp.stack([gain_attn, gain_char, gain_merge], axis=1)
    gain_block = jnp.pad(gain_block, ((0, 0), (0, lane - 3)))
    first_needed = [gru_weight, jnp.concatenate([qkv_weight, gain_block], axis=1)]
    gru_full, gains_and_qkv = gather_all(
        first_needed,
        slots_of(first_needed),
        True,
        0,
    )
    qkv_full = gains_and_qkv[:, : 3 * width]
    gains = jnp.transpose(gains_and_qkv[:, 3 * width :].astype(f32))
    attn_gain_f, char_gain_f, merge_gain_f = gains[0], gains[1], gains[2]
    later = [conv_weight, out_weight, merge_weight, up_weight, down_weight]
    conv_full, out_full, merge_full, up_full, down_full = gather_all(
        later,
        slots_of(later),
        True,
        1,
    )
    tok_rows = tokens.shape[1]
    char_rows = chars.shape[1]
    half_width = width // 2
    seq_len = tok_rows * lax.axis_size("ctx")
    token_in = tokens[0].astype(f32)
    char_in = chars[0].astype(f32)
    char_map = char_token[0, 0]
    lengths = doc_lengths[0]
    starts = jnp.cumsum(lengths) - lengths
    positions = lax.axis_index("ctx") * tok_rows + jnp.arange(tok_rows, dtype=jnp.int32)
    doc_first = jnp.any(starts[None, :] == positions[:, None], axis=1)
    doc_last = jnp.any(starts[None, :] == positions[:, None] + 1, axis=1)
    onehot = char_map[None, :] == jnp.arange(tok_rows, dtype=jnp.int32)[:, None]
    onehot_low = onehot.astype(bf16)
    counts = jnp.sum(onehot.astype(f32), axis=1)
    root_counts = jnp.sqrt(counts)
    boundary = char_map[1:] != char_map[:-1]
    first_char = jnp.concatenate([jnp.ones((1,), bool), boundary])
    last_char = jnp.concatenate([boundary, jnp.ones((1,), bool)])
    opens_doc = jnp.any(onehot & doc_first[:, None], axis=0)
    closes_doc = jnp.any(onehot & doc_last[:, None], axis=0)
    keep_fwd = 1.0 - (first_char & opens_doc).astype(f32)
    keep_bwd = 1.0 - (last_char & closes_doc).astype(f32)
    attn_in = normed(token_in, attn_gain_f).astype(bf16)
    qkv = jnp.dot(attn_in, qkv_full, preferred_element_type=f32).astype(bf16)
    elements = seq_len * width
    apart = lax.axis_size("ctx") // HEAD_GROUPS
    slot_blocks = jnp.arange(HEAD_GROUPS, dtype=jnp.int32) * apart + lax.rem(
        lax.axis_index("ctx"), apart
    )
    slot_positions = slot_blocks[:, None] * tok_rows + jnp.arange(tok_rows, dtype=jnp.int32)[None]
    before = starts[None, None, :] <= slot_positions[:, :, None]
    doc_begin = jnp.max(jnp.where(before, starts, 0), axis=2)
    doc_end = jnp.min(jnp.where(before, seq_len, starts), axis=2)
    spans = jnp.concatenate(
        [
            doc_begin[:, None, :],
            doc_end[:, None, :],
            jnp.zeros((HEAD_GROUPS, 6, tok_rows), jnp.int32),
        ],
        axis=1,
    )
    bounds = jnp.stack(
        [doc_begin[:, 0] // tok_rows, (doc_end[:, -1] + tok_rows - 1) // tok_rows], axis=1
    )
    q_heads, kv_heads = spread_heads(qkv, 2)
    o_heads, exact_heads, log_heads = attend(bounds, q_heads, kv_heads, spans)
    attn_out, proj, resid, sums = join_heads(o_heads, tokens[0], out_full, elements, 6)
    char_low = normed(char_in, char_gain_f).astype(bf16)
    gates = jnp.dot(char_low, gru_full, preferred_element_type=f32)
    ramp = jnp.arange(half_width, dtype=f32) / (half_width - 1)
    shift = (1.0 + math.log(char_rows * lax.axis_size("ctx"))) * ramp
    lift = jnp.exp(0.5 * shift)
    zeta_f = jax.nn.sigmoid(gates[:, :half_width] - shift)
    cand_f = gates[:, half_width : 2 * half_width] * lift
    zeta_b = jax.nn.sigmoid(gates[:, 2 * half_width : 3 * half_width] - shift)
    cand_b = gates[:, 3 * half_width :] * lift
    coef_f = (1.0 - zeta_f) * keep_fwd[:, None]
    coef_b = (1.0 - zeta_b) * keep_bwd[:, None]
    coefs = jnp.concatenate([coef_f, coef_b], axis=1)
    terms = jnp.concatenate([zeta_f * cand_f, zeta_b * cand_b], axis=1)
    local_state, cum_state, totals = scan_both(coefs, terms, True)
    carry_in = carried(totals, True)
    states = local_state + cum_state * carry_in
    state_f = states[:, :half_width]
    state_b = states[:, half_width:]
    carry_in_f = carry_in[0, :half_width]
    carry_in_b = carry_in[0, half_width:]
    mixed = states.astype(bf16)
    out_chars = (char_in + mixed.astype(f32)).astype(bf16)
    pooled = (jnp.dot(onehot_low, mixed, preferred_element_type=f32) / root_counts[:, None]).astype(
        bf16
    )
    padded = padded_2(pooled, (("ctx", 0),), 1)
    conv_out = jnp.zeros((tok_rows, width), f32)
    for kernel in range(3):
        conv_out = conv_out + jnp.dot(
            padded[kernel : kernel + tok_rows],
            conv_full[:, kernel * width : (kernel + 1) * width],
            preferred_element_type=f32,
        )
    merge_in = normed(resid, merge_gain_f).astype(bf16)
    merge_pre = jnp.dot(merge_in, merge_full, preferred_element_type=f32) + conv_out
    merged = gelu_exact(merge_pre).astype(bf16)
    up_pre = jnp.dot(merged, up_full, preferred_element_type=f32)
    up_act = gelu_exact(up_pre).astype(bf16)
    out_tok = (resid + jnp.dot(up_act, down_full, preferred_element_type=f32)).astype(bf16)
    cot_tok = cot_tokens[0]
    cot_tok_f = cot_tok.astype(f32)
    cot_chr_f = cot_chars[0].astype(f32)
    grad_down = jnp.einsum("tf,td->fd", up_act, cot_tok, preferred_element_type=f32)
    grad_act = jnp.einsum("td,fd->tf", cot_tok, down_full, preferred_element_type=f32)
    _, gelu_up_back = jax.vjp(gelu_exact, up_pre)
    grad_up_pre = gelu_up_back(grad_act)[0].astype(bf16)
    grad_up = jnp.einsum("tc,tf->cf", merged, grad_up_pre, preferred_element_type=f32)
    grad_merged = jnp.einsum("tf,cf->tc", grad_up_pre, up_full, preferred_element_type=f32)
    _, gelu_merge_back = jax.vjp(gelu_exact, merge_pre)
    grad_pre = gelu_merge_back(grad_merged)[0].astype(bf16)
    grad_merge = jnp.einsum("tc,te->ce", merge_in, grad_pre, preferred_element_type=f32)
    grad_merge_in = jnp.einsum("te,ce->tc", grad_pre, merge_full, preferred_element_type=f32)
    grad_conv = jnp.concatenate(
        [
            jnp.einsum(
                "tc,te->ce",
                padded[kernel : kernel + tok_rows],
                grad_pre,
                preferred_element_type=f32,
            )
            for kernel in range(3)
        ],
        axis=1,
    )
    grad_padded = padded_2(grad_pre, (("ctx", 0),), 1)
    grad_pooled = jnp.zeros((tok_rows, width), f32)
    for kernel in range(3):
        grad_pooled = grad_pooled + jnp.einsum(
            "te,ce->tc",
            grad_padded[2 - kernel : 2 - kernel + tok_rows],
            conv_full[:, kernel * width : (kernel + 1) * width],
            preferred_element_type=f32,
        )
    _, merge_norm_back = jax.vjp(normed, resid, merge_gain_f)
    grad_resid_norm, grad_merge_gain = merge_norm_back(grad_merge_in)
    grad_resid = cot_tok_f + grad_resid_norm
    grad_mixed = cot_chr_f + jnp.take(grad_pooled / root_counts[:, None], char_map, axis=0)
    shifted_f = jnp.concatenate([coef_f[1:], jnp.ones((1, half_width), f32)], axis=0)
    shifted_b = jnp.concatenate([jnp.ones((1, half_width), f32), coef_b[:-1]], axis=0)
    local_lam, cum_lam, lam_totals = scan_both(
        jnp.concatenate([shifted_f, shifted_b], axis=1), grad_mixed, False
    )
    edge = jnp.concatenate([coef_f[0], coef_b[-1]])[None, :]
    lams = local_lam + cum_lam * carried(lam_totals[:2] * edge, False)
    lam_f = lams[:, :half_width]
    lam_b = lams[:, half_width:]
    prev_f = jnp.concatenate([carry_in_f[None, :], state_f[:-1]], axis=0)
    grad_zeta_f = lam_f * (cand_f - keep_fwd[:, None] * prev_f) * zeta_f * (1.0 - zeta_f)
    grad_cand_f = lam_f * zeta_f * lift
    next_b = jnp.concatenate([state_b[1:], carry_in_b[None, :]], axis=0)
    grad_zeta_b = lam_b * (cand_b - keep_bwd[:, None] * next_b) * zeta_b * (1.0 - zeta_b)
    grad_cand_b = lam_b * zeta_b * lift
    grad_gates = jnp.concatenate(
        [grad_zeta_f, grad_cand_f, grad_zeta_b, grad_cand_b], axis=1
    ).astype(bf16)
    grad_gru = jnp.einsum("tc,tg->cg", char_low, grad_gates, preferred_element_type=f32)
    grad_char_norm = jnp.einsum("tg,cg->tc", grad_gates, gru_full, preferred_element_type=f32)
    _, char_norm_back = jax.vjp(normed, char_in, char_gain_f)
    grad_char_in, grad_char_gain = char_norm_back(grad_char_norm)
    grad_chars_out = (cot_chr_f + grad_char_in).astype(bf16)
    grad_stream, grad_proj, g_heads = part_heads(
        grad_resid, proj, tokens[0], out_full, sums, elements, 7
    )
    grad_out_proj = jnp.einsum("tc,te->ce", attn_out, grad_proj, preferred_element_type=f32)
    dq_heads, dkv_heads = attend_back(
        bounds, q_heads, kv_heads, g_heads, exact_heads, log_heads, spans
    )
    grad_qkv_low = collect_heads(dq_heads, dkv_heads, 3)
    grad_qkv = jnp.einsum("tc,tg->cg", attn_in, grad_qkv_low, preferred_element_type=f32)
    grad_attn_in = jnp.einsum("tg,cg->tc", grad_qkv_low, qkv_full, preferred_element_type=f32)
    _, attn_norm_back = jax.vjp(normed, token_in, attn_gain_f)
    grad_token_in, grad_attn_gain = attn_norm_back(grad_attn_in)
    grad_tokens_out = (grad_stream + grad_token_in).astype(bf16)
    gain_grads = jnp.stack([grad_attn_gain, grad_char_gain, grad_merge_gain], axis=1)
    gain_grads = jnp.pad(gain_grads, ((0, 0), (0, lane - 3)))
    early = [grad_down, grad_up, grad_merge, grad_conv]
    early = [part.astype(bf16) for part in early]
    down_shard, up_shard, merge_shard, conv_shard = scatter_sums(
        early,
        slots_of(early),
        True,
        4,
        f32,
    )
    late = [grad_gru, grad_out_proj, jnp.concatenate([grad_qkv, gain_grads], axis=1)]
    late = [part.astype(bf16) for part in late]
    gru_shard, out_shard, qkv_shard = scatter_sums(
        late,
        slots_of(late),
        True,
        5,
        f32,
    )
    gain_shard = qkv_shard[:, 3 * width :]
    shards = (
        gain_shard[:, 0],
        qkv_shard[:, : 3 * width],
        out_shard,
        gain_shard[:, 1],
        gru_shard,
        conv_shard,
        gain_shard[:, 2],
        merge_shard,
        up_shard,
        down_shard,
    )
    return (
        out_tok[None],
        out_chars[None],
        grad_tokens_out[None],
        grad_chars_out[None],
        shards[0],
        shards[1],
        shards[2],
        shards[3],
        shards[4],
        shards[5],
        shards[6],
        shards[7],
        shards[8],
        shards[9],
    )


def solution(mesh):
    in_specs = (
        P("wsh", "ctx", None),
        P("wsh", "ctx", None),
        P("wsh", "ctx", None),
        P("wsh", None),
        P(("ctx", "wsh")),
        P(("ctx", "wsh"), None),
        P(("ctx", "wsh"), None),
        P(("ctx", "wsh")),
        P(("ctx", "wsh"), None),
        P(("ctx", "wsh"), None),
        P(("ctx", "wsh")),
        P(("ctx", "wsh"), None),
        P(("ctx", "wsh"), None),
        P(("ctx", "wsh"), None),
        P("wsh", "ctx", None),
        P("wsh", "ctx", None),
    )
    out_specs = (
        P("wsh", "ctx", None),
        P("wsh", "ctx", None),
        P("wsh", "ctx", None),
        P("wsh", "ctx", None),
        P(("ctx", "wsh")),
        P(("ctx", "wsh"), None),
        P(("ctx", "wsh"), None),
        P(("ctx", "wsh")),
        P(("ctx", "wsh"), None),
        P(("ctx", "wsh"), None),
        P(("ctx", "wsh")),
        P(("ctx", "wsh"), None),
        P(("ctx", "wsh"), None),
        P(("ctx", "wsh"), None),
    )
    return jax.shard_map(body, mesh=mesh, in_specs=in_specs, out_specs=out_specs, check_vma=False)
```

```python
import functools
import math

import jax
import jax.numpy as jnp
from jax import lax
from jax.experimental import pallas as pl
from jax.experimental.pallas import tpu as pltpu
from jax.sharding import PartitionSpec as P

HEADS = 12
HEAD_DIM = 64


masked_score = -1e30


def masks_of(axis):
    return [1 << k for k in range(lax.axis_size(axis).bit_length() - 1)]


def place_of(axis, partner):
    here = {"ctx": lax.axis_index("ctx"), "wsh": lax.axis_index("wsh")}
    here[axis] = partner
    return (here["ctx"], here["wsh"])


def greet(over_wsh):
    barrier = pltpu.get_barrier_semaphore()
    partners = [
        place_of("ctx", lax.bitwise_xor(lax.axis_index("ctx"), mask)) for mask in masks_of("ctx")
    ]
    if over_wsh:
        partners = partners + [
            place_of("wsh", lax.bitwise_xor(lax.axis_index("wsh"), gap))
            for gap in range(1, lax.axis_size("wsh"))
        ]
    for partner in partners:
        pl.semaphore_signal(
            barrier, inc=1, device_id=partner, device_id_type=pl.DeviceIdType.MESH
        )
    pl.semaphore_wait(barrier, len(partners))


def ctx_bits(upward):
    masks = masks_of("ctx")
    middle = masks[1:]
    return (middle if upward else middle[::-1]) + masks[:1]


def ctx_bit(mask):
    return lax.rem(lax.div(lax.axis_index("ctx"), mask), 2)


def ctx_index(fixed):
    return tuple(
        fixed[mask] if mask in fixed else slice(None) for mask in reversed(masks_of("ctx"))
    )


def remote(src, dst, sems, number, partner):
    return pltpu.make_async_remote_copy(
        src_ref=src,
        dst_ref=dst,
        send_sem=sems[0].at[number],
        recv_sem=sems[1].at[number],
        device_id=partner,
        device_id_type=pl.DeviceIdType.MESH,
    )


LAG = 2
FRONT_SHARE = 0.75
BACK_SHARE = 0.85
SLOT_ELEMENTS = 24 * 512


def wavefront(slots, steps, move):
    moves = []
    for tick in range(1, len(slots) + steps * LAG):
        for number in range(len(slots) - 1, -1, -1):
            step, off = divmod(tick - number - 1, LAG)
            if off == 0 and 0 <= step < steps:
                moves.append(functools.partial(move, slots[number], step + 1))
    return moves


def weave(ticks, pieces, share):
    ticks = list(ticks)
    total = len(ticks)
    ticks.pop(0)()
    for number, piece in enumerate(pieces):
        piece()
        while total - len(ticks) < share * total * (number + 1) / len(pieces) and ticks:
            ticks.pop(0)()
    for tick in ticks:
        tick()


def gather_ticks(slots, shards, outs, sems, local_sems, over_wsh):
    width_w = lax.axis_size("wsh") if over_wsh else 1
    mine_w = lax.axis_index("wsh") if over_wsh else 0
    bits = len(masks_of("ctx"))
    per_stream = width_w - 1 + bits
    streams = [stream for slot in slots for stream in slot]
    number_of = {stream: position for position, stream in enumerate(streams)}
    started = {}

    def start(stream, step):
        array, first, cols, upward = stream
        base = number_of[stream] * per_stream
        span = pl.ds(first, cols)
        out = outs[array]
        every = {mask: ctx_bit(mask) for mask in masks_of("ctx")}
        copies = []
        if step == 0:
            own = ctx_index(every) + (mine_w, slice(None), span)
            copy = pltpu.make_async_copy(
                shards[array].at[:, span], out.at[own], local_sems.at[number_of[stream]]
            )
            copies.append(copy)
            for gap in range(1, width_w):
                copies.append(
                    remote(
                        shards[array].at[:, span],
                        out.at[own],
                        sems,
                        base + gap - 1,
                        place_of("wsh", lax.bitwise_xor(mine_w, gap)),
                    )
                )
        else:
            order = ctx_bits(upward)
            held = {mask: every[mask] for mask in order[step - 1 :]}
            part = ctx_index(held) + (slice(None), slice(None), span)
            partner = place_of("ctx", lax.bitwise_xor(lax.axis_index("ctx"), order[step - 1]))
            copies.append(
                remote(out.at[part], out.at[part], sems, base + width_w - 1 + step - 1, partner)
            )
        for copy in copies:
            copy.start()
        started[stream, step] = copies

    def finish(stream, step):
        for position, copy in enumerate(started[stream, step]):
            if step == 0 and position == 0:
                copy.wait()
            else:
                copy.wait_recv()

    def first():
        for stream in streams:
            start(stream, 0)

    def move(slot, step):
        for stream in slot:
            finish(stream, step - 1)
            if step <= bits:
                start(stream, step)

    def drain():
        for (stream, step), copies in started.items():
            for copy in copies[1:] if step == 0 else copies:
                copy.wait_send()

    return [first] + wavefront(slots, bits + 1, move) + [drain]


def gather_sems(slots, over_wsh):
    bits = len(masks_of("ctx"))
    width_w = lax.axis_size("wsh") if over_wsh else 1
    streams = sum(len(slot) for slot in slots)
    copies = streams * (width_w - 1 + bits)
    return [
        pltpu.SemaphoreType.DMA((copies,)),
        pltpu.SemaphoreType.DMA((copies,)),
        pltpu.SemaphoreType.DMA((streams,)),
    ]


def gather_shapes(arrays, over_wsh):
    bits = len(masks_of("ctx"))
    width_w = lax.axis_size("wsh") if over_wsh else 1
    return tuple(
        jax.ShapeDtypeStruct((2,) * bits + (width_w,) + array.shape, array.dtype)
        for array in arrays
    )


def gather_kernel(slots, count, over_wsh, *refs):
    greet(over_wsh)
    shards, outs, sems = refs[:count], refs[count : 2 * count], refs[2 * count :]
    for tick in gather_ticks(slots, shards, outs, sems[:2], sems[2], over_wsh):
        tick()


def gather_all(arrays, slots, over_wsh, collective):
    count = len(arrays)
    hbm = pl.BlockSpec(memory_space=pl.ANY)
    outs = pl.pallas_call(
        functools.partial(gather_kernel, slots, count, over_wsh),
        out_shape=gather_shapes(arrays, over_wsh),
        in_specs=[hbm] * count,
        out_specs=(hbm,) * count,
        scratch_shapes=gather_sems(slots, over_wsh),
        compiler_params=pltpu.CompilerParams(
            collective_id=collective, has_side_effects=True, vmem_limit_bytes=4 << 20
        ),
        name="gather_all",
    )(*arrays)
    return [out.reshape((-1, out.shape[-1])) for out in outs]


def add_into(total_ref, extra_ref, fixed_total, fixed_extra, shape, rows, block_rows, span):
    steps = math.prod(shape) * (rows // block_rows)

    def step(position, carry):
        rest = position
        chunk = lax.rem(rest, rows // block_rows)
        rest = lax.div(rest, rows // block_rows)
        free = []
        for size in reversed(shape):
            free.append(lax.rem(rest, size))
            rest = lax.div(rest, size)
        free = free[::-1]
        take = iter(free)
        into = tuple(next(take) if entry is None else entry for entry in fixed_total)
        take = iter(free)
        source = tuple(next(take) if entry is None else entry for entry in fixed_extra)
        down = pl.ds(pl.multiple_of(chunk * block_rows, block_rows), block_rows)
        total_ref[into + (down, span)] = (
            total_ref[into + (down, span)] + extra_ref[source + (down, slice(None))]
        )
        return carry

    lax.fori_loop(0, steps, step, 0)


def scatter_ticks(slots, grads, outs, scratch, over_wsh):
    streams = [stream for slot in slots for stream in slot]
    bits = len(masks_of("ctx"))
    held, rest = scratch[: len(grads)], scratch[len(grads) :]
    per_stream_bufs = bits + (1 if over_wsh else 0)
    landing = {}
    for number, stream in enumerate(streams):
        landing[stream] = rest[number * per_stream_bufs : (number + 1) * per_stream_bufs]
    sems = rest[len(streams) * per_stream_bufs : len(streams) * per_stream_bufs + 2]
    local_sems = rest[len(streams) * per_stream_bufs + 2]
    width_w = lax.axis_size("wsh") if over_wsh else 1
    mine_w = lax.axis_index("wsh") if over_wsh else 0
    per_stream = width_w - 1 + bits
    number_of = {stream: position for position, stream in enumerate(streams)}
    every = {mask: ctx_bit(mask) for mask in masks_of("ctx")}
    low = masks_of("ctx")[0]
    started = {}

    def start(stream, step):
        array, first, cols, upward = stream
        base = number_of[stream] * per_stream
        span = pl.ds(first, cols)
        order = ctx_bits(upward)[::-1]
        copies = []
        if step == 0:
            kept = ctx_index({low: every[low]}) + (slice(None), slice(None), span)
            copies.append(
                pltpu.make_async_copy(
                    grads[array].at[kept],
                    held[array].at[(slice(None),) * bits + (slice(None), span)],
                    local_sems.at[number_of[stream]],
                )
            )
            away = ctx_index({low: 1 - every[low]}) + (slice(None), slice(None), span)
            copies.append(
                remote(
                    grads[array].at[away],
                    landing[stream][0],
                    sems,
                    base,
                    place_of("ctx", lax.bitwise_xor(lax.axis_index("ctx"), low)),
                )
            )
        elif step < bits:
            fixed = {mask: every[mask] for mask in order[:step]}
            fixed[order[step]] = 1 - every[order[step]]
            away = ctx_index(fixed)[:-1] + (slice(None), slice(None), span)
            copies.append(
                remote(
                    held[array].at[away],
                    landing[stream][step],
                    sems,
                    base + step,
                    place_of("ctx", lax.bitwise_xor(lax.axis_index("ctx"), order[step])),
                )
            )
        elif over_wsh:
            here = ctx_index(every)[:-1]
            for gap in range(1, width_w):
                other = lax.bitwise_xor(mine_w, gap)
                copies.append(
                    remote(
                        held[array].at[here + (other, slice(None), span)],
                        landing[stream][bits].at[gap - 1],
                        sems,
                        base + bits + gap - 1,
                        place_of("wsh", other),
                    )
                )
        for copy in copies:
            copy.start()
        started[stream, step] = copies

    def finish(stream, step):
        array, first, cols, upward = stream
        span = pl.ds(first, cols)
        order = ctx_bits(upward)[::-1]
        for position, copy in enumerate(started[stream, step]):
            if step == 0 and position == 0:
                copy.wait()
            else:
                copy.wait_recv()
        rows = held[array].shape[-2]
        block_rows = rows if rows <= 24 else 32
        if step < bits:
            fixed = {mask: every[mask] for mask in order[: step + 1]}
            lead = ctx_index(fixed)[:-1]
            into = tuple(None if isinstance(entry, slice) else entry for entry in lead) + (None,)
            free = (2,) * (bits - 1 - step)
            add_into(
                held[array],
                landing[stream][step],
                into,
                (None,) * (len(free) + 1),
                free + (width_w,),
                rows,
                block_rows,
                span,
            )
        if step == bits or (step == bits - 1 and not over_wsh):
            here = ctx_index(every)[:-1] + (mine_w,)
            for chunk in range(0, rows, block_rows):
                down = pl.ds(chunk, block_rows)
                total = held[array][here + (down, span)].astype(jnp.float32)
                for gap in range(1, width_w):
                    total = total + landing[stream][bits][gap - 1, down, :].astype(jnp.float32)
                outs[array][down, span] = total.astype(outs[array].dtype)

    steps = bits + (1 if over_wsh else 0)

    def first():
        for stream in streams:
            start(stream, 0)

    def move(slot, step):
        for stream in slot:
            finish(stream, step - 1)
            if step < steps:
                start(stream, step)

    def drain():
        for (stream, step), copies in started.items():
            for copy in copies[1:] if step == 0 else copies:
                copy.wait_send()

    return [first] + wavefront(slots, steps, move) + [drain]


def scatter_shapes(arrays, over_wsh):
    bits = len(masks_of("ctx"))
    width_w = lax.axis_size("wsh") if over_wsh else 1
    rows = [array.shape[0] // (width_w << bits) for array in arrays]
    shaped = [
        array.reshape((2,) * bits + (width_w, row, array.shape[1]))
        for array, row in zip(arrays, rows)
    ]
    return shaped, rows


def scatter_scratch(arrays, slots, over_wsh):
    bits = len(masks_of("ctx"))
    width_w = lax.axis_size("wsh") if over_wsh else 1
    rows = [array.shape[0] // (width_w << bits) for array in arrays]
    streams = [stream for slot in slots for stream in slot]
    copies = len(streams) * (width_w - 1 + bits)
    buffers = [
        pltpu.VMEM((2,) * (bits - 1) + (width_w, row, array.shape[1]), array.dtype)
        for array, row in zip(arrays, rows)
    ]
    for array, first, cols, upward in streams:
        kind = arrays[array].dtype
        for step in range(bits):
            buffers.append(
                pltpu.VMEM((2,) * (bits - 1 - step) + (width_w, rows[array], cols), kind)
            )
        if over_wsh:
            buffers.append(pltpu.VMEM((width_w - 1, rows[array], cols), kind))
    return buffers + [
        pltpu.SemaphoreType.DMA((copies,)),
        pltpu.SemaphoreType.DMA((copies,)),
        pltpu.SemaphoreType.DMA((len(streams),)),
    ]


def scatter_kernel(slots, count, over_wsh, *refs):
    greet(over_wsh)
    grads, outs, scratch = refs[:count], refs[count : 2 * count], refs[2 * count :]
    for tick in scatter_ticks(slots, grads, outs, scratch, over_wsh):
        tick()


def scatter_sums(arrays, slots, over_wsh, collective, dtype):
    count = len(arrays)
    shaped, rows = scatter_shapes(arrays, over_wsh)
    return pl.pallas_call(
        functools.partial(scatter_kernel, slots, count, over_wsh),
        out_shape=tuple(
            jax.ShapeDtypeStruct((row, array.shape[1]), dtype) for array, row in zip(arrays, rows)
        ),
        in_specs=[pl.BlockSpec(memory_space=pl.ANY)] * count,
        out_specs=(pl.BlockSpec(memory_space=pltpu.VMEM),) * count,
        scratch_shapes=scatter_scratch(arrays, slots, over_wsh),
        compiler_params=pltpu.CompilerParams(
            collective_id=collective, has_side_effects=True, vmem_limit_bytes=56 << 20
        ),
        name="scatter_sums",
    )(*shaped)


def halves(number, rows, cols):
    pieces = 2 * max(1, rows * cols // SLOT_ELEMENTS)
    while cols // pieces < 128:
        pieces = pieces - 2
    cuts = [cols * piece // pieces // 128 * 128 for piece in range(pieces)] + [cols]
    streams = [
        (number, cuts[piece], cuts[piece + 1] - cuts[piece], piece % 2 == 0)
        for piece in range(pieces)
    ]
    return [tuple(streams[piece : piece + 2]) for piece in range(0, pieces, 2)]


def slots_of(arrays, shards):
    slots = []
    for number, part in enumerate(arrays):
        rows = part.shape[0]
        if not shards:
            rows = rows // (lax.axis_size("ctx") * lax.axis_size("wsh"))
        slots = slots + halves(number, rows, part.shape[1])
    return slots


HEAD_GROUPS = 4


def groups():
    apart = lax.axis_size("ctx") // HEAD_GROUPS
    mine = lax.axis_index("ctx")
    return apart, lax.div(mine, apart), lax.rem(mine, apart)


def ctx_partner(gap):
    return place_of("ctx", lax.bitwise_xor(lax.axis_index("ctx"), gap))


def greet_ctx(gaps):
    barrier = pltpu.get_barrier_semaphore()
    for gap in gaps:
        pl.semaphore_signal(
            barrier, inc=1, device_id=ctx_partner(gap), device_id_type=pl.DeviceIdType.MESH
        )
    pl.semaphore_wait(barrier, len(gaps))


def spread_ticks(qkv_ref, q_out, kv_out, send_q, send_kv, send_sem, recv_sem, local_sem):
    apart, group, inner = groups()
    width = qkv_ref.shape[1] // 3
    cols = width // HEAD_GROUPS
    mine = lax.axis_index("ctx")
    sems = (send_sem, recv_sem)
    kv_copies, q_copies, own, passed = [], [], [], []

    def send():
        for other in range(HEAD_GROUPS):
            send_q[other] = qkv_ref[:, other * cols : (other + 1) * cols]
            for part in range(2):
                first = (part + 1) * width + other * cols
                send_kv[other, :, part * cols : (part + 1) * cols] = qkv_ref[
                    :, first : first + cols
                ]
        for gap in range(1, HEAD_GROUPS):
            other = lax.bitwise_xor(group, gap)
            partner = ctx_partner(gap * apart)
            kv_copies.append(
                remote(send_kv.at[other], kv_out.at[mine], sems, gap - 1, partner)
            )
        for gap in range(1, HEAD_GROUPS):
            other = lax.bitwise_xor(group, gap)
            partner = ctx_partner(gap * apart)
            q_copies.append(
                remote(send_q.at[other], q_out.at[group], sems, HEAD_GROUPS - 2 + gap, partner)
            )
        own.append(pltpu.make_async_copy(send_kv.at[group], kv_out.at[mine], local_sem.at[0]))
        own.append(pltpu.make_async_copy(send_q.at[group], q_out.at[group], local_sem.at[1]))
        for copy in own + kv_copies + q_copies:
            copy.start()

    def pass_on():
        own[0].wait()
        number = 2 * (HEAD_GROUPS - 1)
        for gap in range(HEAD_GROUPS):
            if gap:
                kv_copies[gap - 1].wait_recv()
            slot = lax.bitwise_xor(mine, gap * apart)
            for near in range(1, apart):
                copy = remote(kv_out.at[slot], kv_out.at[slot], sems, number, ctx_partner(near))
                copy.start()
                passed.append(copy)
                number = number + 1

    def wait():
        own[1].wait()
        for copy in q_copies + passed:
            copy.wait_recv()
        for copy in kv_copies + q_copies + passed:
            copy.wait_send()

    return send, pass_on, wait


def spread_scratch(rows, cols, dtype):
    apart = lax.axis_size("ctx") // HEAD_GROUPS
    copies = 2 * (HEAD_GROUPS - 1) + HEAD_GROUPS * (apart - 1)
    return [
        pltpu.VMEM((HEAD_GROUPS, rows, cols), dtype),
        pltpu.VMEM((HEAD_GROUPS, rows, 2 * cols), dtype),
        pltpu.SemaphoreType.DMA((copies,)),
        pltpu.SemaphoreType.DMA((copies,)),
        pltpu.SemaphoreType.DMA((2,)),
    ]


def head_rows(value, head):
    rows = lax.broadcasted_iota(jnp.int32, value.shape, 0)
    inside = (rows >= head * HEAD_DIM) & (rows < (head + 1) * HEAD_DIM)
    return jnp.where(inside, value, jnp.zeros_like(value))


def head_cols(value, head):
    cols = lax.broadcasted_iota(jnp.int32, value.shape, 1)
    inside = (cols >= head * HEAD_DIM) & (cols < (head + 1) * HEAD_DIM)
    return jnp.where(inside, value, jnp.zeros_like(value))


def turned(value):
    return jnp.transpose(value.astype(jnp.float32))


def dot32(left, right):
    return jnp.dot(left, right, preferred_element_type=jnp.float32)


def key_mask(key_block, size, spans_ref, slot):
    keys = key_block * size + lax.broadcasted_iota(jnp.int32, (size, size), 0)
    return (keys >= spans_ref[slot, 0:1, :]) & (keys < spans_ref[slot, 1:2, :])


def attend_kernel(bounds, q_ref, kv_ref, spans_ref, o_ref, exact_ref, log_ref, vt_s, qt_s, ot_s, stat_s):
    blocks, size, both = kv_ref.shape
    cols = both // 2
    heads = cols // HEAD_DIM

    def turn_values(block, carry):
        vt_s[block] = turned(kv_ref[block, :, cols:]).astype(jnp.bfloat16)
        return carry

    lax.fori_loop(0, blocks, turn_values, 0)

    def query_block(slot, carry):
        qt = (turned(q_ref[slot]) * HEAD_DIM ** (-0.5)).astype(jnp.bfloat16)
        for head in range(heads):
            qt_s[head] = head_rows(qt, head)
        ot_s[...] = jnp.zeros_like(ot_s)
        stat_s[0] = jnp.full_like(stat_s[0], masked_score)
        stat_s[1] = jnp.zeros_like(stat_s[1])

        def key_step(block, carry):
            allowed = key_mask(block, size, spans_ref, slot)
            keys = kv_ref[block, :, :cols]
            for head in range(heads):
                row = slice(head, head + 1)
                part = slice(head * HEAD_DIM, (head + 1) * HEAD_DIM)
                scores = jnp.where(allowed, dot32(keys, qt_s[head]), masked_score)
                old = stat_s[0, row, :]
                top = jnp.maximum(old, jnp.max(scores, axis=0, keepdims=True))
                factor = jnp.exp(old - top)
                weights = jnp.exp(scores - top)
                stat_s[0, row, :] = top
                stat_s[1, row, :] = stat_s[1, row, :] * factor + jnp.sum(
                    weights, axis=0, keepdims=True
                )
                ot_s[part, :] = ot_s[part, :] * factor + dot32(
                    vt_s[block, part, :], weights.astype(jnp.bfloat16)
                )
            return carry

        lax.fori_loop(bounds[slot, 0], bounds[slot, 1], key_step, 0)
        for head in range(heads):
            row = slice(head, head + 1)
            part = slice(head * HEAD_DIM, (head + 1) * HEAD_DIM)
            ot_s[part, :] = ot_s[part, :] / stat_s[1, row, :]
            log_ref[slot, row, :] = stat_s[0, row, :] + jnp.log(stat_s[1, row, :])
        exact = jnp.transpose(ot_s[...])
        exact_ref[slot] = exact
        o_ref[slot] = exact.astype(jnp.bfloat16)
        return carry

    lax.fori_loop(0, q_ref.shape[0], query_block, 0)


def attend_back_kernel(
    bounds, q_ref, kv_ref, g_ref, exact_ref, log_ref, spans_ref, dq_ref, dkv_ref, v_s, kt_s, qt_s, gt_s,
    qn_s, gn_s, dqt_s, row_s, dk_s, dv_s
):
    blocks, size, both = kv_ref.shape
    cols = both // 2
    heads = cols // HEAD_DIM
    scale = HEAD_DIM ** (-0.5)
    bf16 = jnp.bfloat16

    def turn_keys(block, carry):
        kt_s[block] = turned(kv_ref[block, :, :cols]).astype(bf16)
        v_s[block] = kv_ref[block, :, cols:]
        dk_s[block] = jnp.zeros(dk_s.shape[1:], jnp.float32)
        dv_s[block] = jnp.zeros(dv_s.shape[1:], jnp.float32)
        return carry

    lax.fori_loop(0, blocks, turn_keys, 0)

    def query_block(slot, carry):
        qn = (q_ref[slot].astype(jnp.float32) * scale).astype(bf16)
        gn = g_ref[slot]
        qt = turned(qn).astype(bf16)
        gt32 = turned(gn)
        products = gt32 * jnp.transpose(exact_ref[slot])
        gt = gt32.astype(bf16)
        for head in range(heads):
            part = slice(head * HEAD_DIM, (head + 1) * HEAD_DIM)
            qt_s[head] = head_rows(qt, head)
            gt_s[head] = head_rows(gt, head)
            qn_s[head] = head_cols(qn, head)
            gn_s[head] = head_cols(gn, head)
            row_s[head : head + 1, :] = jnp.sum(products[part], axis=0, keepdims=True)
        dqt_s[...] = jnp.zeros_like(dqt_s)

        def key_step(block, carry):
            allowed = key_mask(block, size, spans_ref, slot)
            keys = kv_ref[block, :, :cols]
            values = v_s[block]
            dk = jnp.zeros(dk_s.shape[1:], jnp.float32)
            dv = jnp.zeros(dv_s.shape[1:], jnp.float32)
            for head in range(heads):
                row = slice(head, head + 1)
                part = slice(head * HEAD_DIM, (head + 1) * HEAD_DIM)
                scores = jnp.where(allowed, dot32(keys, qt_s[head]), masked_score)
                weights = jnp.exp(scores - log_ref[slot, row, :])
                slopes = dot32(values, gt_s[head])
                ds = (weights * (slopes - row_s[row, :])).astype(bf16)
                dqt_s[part, :] = dqt_s[part, :] + dot32(kt_s[block, part, :], ds)
                dk = dk + dot32(ds, qn_s[head])
                dv = dv + dot32(weights.astype(bf16), gn_s[head])
            dk_s[block] = dk_s[block] + dk
            dv_s[block] = dv_s[block] + dv
            return carry

        lax.fori_loop(bounds[slot, 0], bounds[slot, 1], key_step, 0)
        dq_ref[slot] = (jnp.transpose(dqt_s[...]) * scale).astype(bf16)
        return carry

    lax.fori_loop(0, q_ref.shape[0], query_block, 0)

    def write(block, carry):
        dkv_ref[block, :, :cols] = dk_s[block].astype(bf16)
        dkv_ref[block, :, cols:] = dv_s[block].astype(bf16)
        return carry

    lax.fori_loop(0, blocks, write, 0)


def attend(bounds, q, kv, spans):
    slots, size, cols = q.shape
    blocks = kv.shape[0]
    heads = cols // HEAD_DIM
    whole = pl.BlockSpec(memory_space=pltpu.VMEM)
    f32, bf16 = jnp.float32, jnp.bfloat16
    return pl.pallas_call(
        attend_kernel,
        out_shape=(
            jax.ShapeDtypeStruct(q.shape, bf16),
            jax.ShapeDtypeStruct(q.shape, f32),
            jax.ShapeDtypeStruct((slots, 8, size), f32),
        ),
        in_specs=[pl.BlockSpec(memory_space=pltpu.SMEM), whole, whole, whole],
        out_specs=(whole, whole, whole),
        scratch_shapes=[
            pltpu.VMEM((blocks, cols, size), bf16),
            pltpu.VMEM((heads, cols, size), bf16),
            pltpu.VMEM((cols, size), f32),
            pltpu.VMEM((2, 8, size), f32),
        ],
        compiler_params=pltpu.CompilerParams(vmem_limit_bytes=32 << 20),
        name="attend",
    )(bounds, q, kv, spans)


def attend_back(bounds, q, kv, g, exact, log, spans):
    slots, size, cols = q.shape
    blocks = kv.shape[0]
    heads = cols // HEAD_DIM
    whole = pl.BlockSpec(memory_space=pltpu.VMEM)
    f32, bf16 = jnp.float32, jnp.bfloat16
    return pl.pallas_call(
        attend_back_kernel,
        out_shape=(
            jax.ShapeDtypeStruct(q.shape, bf16),
            jax.ShapeDtypeStruct(kv.shape, bf16),
        ),
        in_specs=[pl.BlockSpec(memory_space=pltpu.SMEM)] + [whole] * 6,
        out_specs=(whole, whole),
        scratch_shapes=[
            pltpu.VMEM((blocks, size, cols), bf16),
            pltpu.VMEM((blocks, cols, size), bf16),
            pltpu.VMEM((heads, cols, size), bf16),
            pltpu.VMEM((heads, cols, size), bf16),
            pltpu.VMEM((heads, size, cols), bf16),
            pltpu.VMEM((heads, size, cols), bf16),
            pltpu.VMEM((cols, size), f32),
            pltpu.VMEM((8, size), f32),
            pltpu.VMEM((blocks, size, cols), f32),
            pltpu.VMEM((blocks, size, cols), f32),
        ],
        compiler_params=pltpu.CompilerParams(vmem_limit_bytes=48 << 20),
        name="attend_back",
    )(bounds, q, kv, g, exact, log, spans)


def exchange_sums(sums_ref, sems, base):
    mine = lax.axis_index("ctx")
    copies = []
    for gap in range(1, lax.axis_size("ctx")):
        copy = remote(sums_ref.at[mine], sums_ref.at[mine], sems, base + gap - 1, ctx_partner(gap))
        copy.start()
        copies.append(copy)
    return copies


def total_of(sums_ref):
    total = sums_ref[0]
    for slot in range(1, sums_ref.shape[0]):
        total = total + sums_ref[slot]
    return total


def summed(value):
    return jnp.sum(jnp.sum(value, axis=0, keepdims=True), axis=1, keepdims=True)


def join_kernel(
    elements, o_ref, tokens_ref, weight_ref, attn_ref, proj_ref, resid_ref, stat_ref, land, sums, send_sem,
    recv_sem, local_sem
):
    apart, group, inner = groups()
    cols = o_ref.shape[2]
    sems = (send_sem, recv_sem)
    greet_ctx(list(range(1, lax.axis_size("ctx"))))
    copies = []
    for gap in range(1, HEAD_GROUPS):
        other = lax.bitwise_xor(group, gap)
        copy = remote(o_ref.at[other], land.at[group], sems, gap - 1, ctx_partner(gap * apart))
        copy.start()
        copies.append(copy)
    own = pltpu.make_async_copy(o_ref.at[group], land.at[group], local_sem.at[0])
    own.start()
    tokens = tokens_ref[...].astype(jnp.float32)
    square = summed(tokens * tokens)
    own.wait()
    for copy in copies:
        copy.wait_recv()
    proj = jnp.zeros(proj_ref.shape, jnp.float32)
    for other in range(HEAD_GROUPS):
        part = land[other]
        attn_ref[:, other * cols : (other + 1) * cols] = part
        proj = proj + dot32(part, weight_ref[other * cols : (other + 1) * cols, :])
    proj_ref[...] = proj
    row = lax.broadcasted_iota(jnp.int32, sums.shape[1:], 0)
    mine = lax.axis_index("ctx")
    sums[mine] = jnp.where(
        row == 0,
        summed(proj * proj),
        jnp.where(row == 1, summed(tokens * proj), jnp.where(row == 2, square, 0.0)),
    )
    small = exchange_sums(sums, sems, HEAD_GROUPS - 1)
    for copy in small:
        copy.wait_recv()
    total = total_of(sums)
    stat_ref[...] = total
    sq_proj, cross, sq_tok = total[0:1, 0:1], total[1:2, 0:1], total[2:3, 0:1]
    rms_scale = lax.rsqrt(sq_proj / elements + 1e-06)
    stream_sq = (sq_tok + 2.0 * rms_scale * cross + rms_scale * rms_scale * sq_proj) / elements
    stream_scale = lax.rsqrt(stream_sq + 1e-06)
    resid_ref[...] = (tokens + proj_ref[...] * rms_scale) * stream_scale
    for copy in copies + small:
        copy.wait_send()


def join_heads(o, tokens, weight, elements, collective):
    rows, width = tokens.shape
    count = lax.axis_size("ctx")
    copies = HEAD_GROUPS - 1 + count - 1
    whole = pl.BlockSpec(memory_space=pltpu.VMEM)
    f32, bf16 = jnp.float32, jnp.bfloat16
    return pl.pallas_call(
        functools.partial(join_kernel, elements),
        out_shape=(
            jax.ShapeDtypeStruct((rows, width), bf16),
            jax.ShapeDtypeStruct((rows, width), f32),
            jax.ShapeDtypeStruct((rows, width), f32),
            jax.ShapeDtypeStruct((8, 128), f32),
        ),
        in_specs=[whole] * 3,
        out_specs=(whole,) * 4,
        scratch_shapes=[
            pltpu.VMEM(o.shape, bf16),
            pltpu.VMEM((count, 8, 128), f32),
            pltpu.SemaphoreType.DMA((copies,)),
            pltpu.SemaphoreType.DMA((copies,)),
            pltpu.SemaphoreType.DMA((1,)),
        ],
        compiler_params=pltpu.CompilerParams(
            collective_id=collective, has_side_effects=True, vmem_limit_bytes=24 << 20
        ),
        name="join_heads",
    )(o, tokens, weight)


def part_kernel(elements, slots, *refs):
    grad_ref, resid_grad_ref, proj_ref, tokens_ref, weight_ref, stat_ref = refs[:6]
    shard_ref, stream_grad_ref, proj_grad_ref, g_out = refs[6:10]
    send, sums, send_sem, recv_sem, local_sem = refs[10:15]
    apart, group, inner = groups()
    cols = g_out.shape[2]
    sems = (send_sem, recv_sem)
    ticks = scatter_ticks(slots, [grad_ref], [shard_ref], refs[15:], True)
    greet_all()
    ticks.pop(0)()
    mine = lax.axis_index("ctx")
    sq_proj, cross, sq_tok = stat_ref[0:1, 0:1], stat_ref[1:2, 0:1], stat_ref[2:3, 0:1]
    rms_scale = lax.rsqrt(sq_proj / elements + 1e-06)
    stream_sq = (sq_tok + 2.0 * rms_scale * cross + rms_scale * rms_scale * sq_proj) / elements
    stream_scale = lax.rsqrt(stream_sq + 1e-06)
    stream = tokens_ref[...].astype(jnp.float32) + proj_ref[...] * rms_scale
    row = lax.broadcasted_iota(jnp.int32, sums.shape[1:], 0)
    sums[mine] = jnp.where(
        row == 0,
        summed(resid_grad_ref[...] * stream),
        jnp.where(row == 1, summed(resid_grad_ref[...] * proj_ref[...]), 0.0),
    )
    small = exchange_sums(sums, sems, HEAD_GROUPS - 1)
    ticks.pop(0)()
    for copy in small:
        copy.wait_recv()
    total = total_of(sums)
    mean_gs = total[0:1, 0:1] / elements
    mean_gp = total[1:2, 0:1] / elements
    mean_sp = (cross + rms_scale * sq_proj) / elements
    cubed = stream_scale * stream_scale * stream_scale
    stream_grad = stream_scale * resid_grad_ref[...] - cubed * mean_gs * stream
    stream_grad_ref[...] = stream_grad
    mean_gsp = stream_scale * mean_gp - cubed * mean_gs * mean_sp
    proj_grad = (
        rms_scale * stream_grad - rms_scale * rms_scale * rms_scale * mean_gsp * proj_ref[...]
    ).astype(jnp.bfloat16)
    proj_grad_ref[...] = proj_grad
    for other in range(HEAD_GROUPS):
        send[other] = lax.dot_general(
            proj_grad,
            weight_ref[other * cols : (other + 1) * cols, :],
            (((1,), (1,)), ((), ())),
            preferred_element_type=jnp.float32,
        ).astype(jnp.bfloat16)
    copies = []
    for gap in range(1, HEAD_GROUPS):
        other = lax.bitwise_xor(group, gap)
        copy = remote(send.at[other], g_out.at[group], sems, gap - 1, ctx_partner(gap * apart))
        copy.start()
        copies.append(copy)
    own = pltpu.make_async_copy(send.at[group], g_out.at[group], local_sem.at[0])
    own.start()
    for tick in ticks:
        tick()
    own.wait()
    for copy in copies:
        copy.wait_recv()
    for copy in copies + small:
        copy.wait_send()


def part_heads(grad, resid_grad, proj, tokens, weight, stat, elements, collective):
    rows, width = tokens.shape
    count = lax.axis_size("ctx")
    copies = HEAD_GROUPS - 1 + count - 1
    cols = width // HEAD_GROUPS
    whole = pl.BlockSpec(memory_space=pltpu.VMEM)
    f32, bf16 = jnp.float32, jnp.bfloat16
    slots = slots_of([grad], False)
    shaped, shard_rows = scatter_shapes([grad], True)
    return pl.pallas_call(
        functools.partial(part_kernel, elements, slots),
        out_shape=(
            jax.ShapeDtypeStruct((shard_rows[0], grad.shape[1]), f32),
            jax.ShapeDtypeStruct((rows, width), f32),
            jax.ShapeDtypeStruct((rows, width), bf16),
            jax.ShapeDtypeStruct((HEAD_GROUPS, rows, cols), bf16),
        ),
        in_specs=[pl.BlockSpec(memory_space=pl.ANY)] + [whole] * 5,
        out_specs=(whole, whole, whole, pl.BlockSpec(memory_space=pl.ANY)),
        scratch_shapes=[
            pltpu.VMEM((HEAD_GROUPS, rows, cols), bf16),
            pltpu.VMEM((count, 8, 128), f32),
            pltpu.SemaphoreType.DMA((copies,)),
            pltpu.SemaphoreType.DMA((copies,)),
            pltpu.SemaphoreType.DMA((1,)),
        ]
        + scatter_scratch([grad], slots, True),
        compiler_params=pltpu.CompilerParams(
            collective_id=collective, has_side_effects=True, vmem_limit_bytes=32 << 20
        ),
        name="part_heads",
    )(shaped[0], resid_grad, proj, tokens, weight, stat)


def collect_ticks(dq_ref, dkv_ref, out_ref, scratch):
    near_land, own_s, q_land, kv_land, send_sem, recv_sem, local_sem = scratch
    apart, group, inner = groups()
    cols = dq_ref.shape[2]
    rows = dq_ref.shape[1]
    width = cols * HEAD_GROUPS
    sems = (send_sem, recv_sem)
    near, far_q, far_kv, own = [], [], [], []

    def send():
        number = 0
        for gap in range(1, apart):
            other = lax.bitwise_xor(inner, gap)
            near.append(
                remote(dkv_ref.at[:, other], near_land.at[gap - 1], sems, number, ctx_partner(gap))
            )
            number = number + 1
        own.append(pltpu.make_async_copy(dkv_ref.at[:, inner], own_s, local_sem.at[0]))
        own.append(pltpu.make_async_copy(dq_ref.at[group], q_land.at[group], local_sem.at[1]))
        for gap in range(1, HEAD_GROUPS):
            other = lax.bitwise_xor(group, gap)
            far_q.append(
                remote(
                    dq_ref.at[other], q_land.at[group], sems, number, ctx_partner(gap * apart)
                )
            )
            number = number + 1
        for copy in near + own + far_q:
            copy.start()

    def add_near():
        own[0].wait()
        for copy in near:
            copy.wait_recv()
        chunk = 32

        def add(position, carry):
            slot = lax.div(position, rows // chunk)
            down = pl.ds(pl.multiple_of(lax.rem(position, rows // chunk) * chunk, chunk), chunk)
            total = own_s[slot, down, :].astype(jnp.float32)
            for gap in range(1, apart):
                total = total + near_land[gap - 1, slot, down, :].astype(jnp.float32)
            own_s[slot, down, :] = total.astype(own_s.dtype)
            return carry

        lax.fori_loop(0, HEAD_GROUPS * (rows // chunk), add, 0)
        number = apart - 1 + HEAD_GROUPS - 1
        own.append(pltpu.make_async_copy(own_s.at[group], kv_land.at[group], local_sem.at[2]))
        own[2].start()
        for gap in range(1, HEAD_GROUPS):
            other = lax.bitwise_xor(group, gap)
            copy = remote(
                own_s.at[other], kv_land.at[group], sems, number, ctx_partner(gap * apart)
            )
            copy.start()
            far_kv.append(copy)
            number = number + 1

    def write():
        own[1].wait()
        for copy in far_q:
            copy.wait_recv()
        for other in range(HEAD_GROUPS):
            out_ref[:, other * cols : (other + 1) * cols] = q_land[other]
        own[2].wait()
        for copy in far_kv:
            copy.wait_recv()
        for other in range(HEAD_GROUPS):
            for part in range(2):
                first = (part + 1) * width + other * cols
                out_ref[:, first : first + cols] = kv_land[
                    other, :, part * cols : (part + 1) * cols
                ]
        for copy in near + far_q + far_kv:
            copy.wait_send()

    return send, add_near, write


def collect_scratch(rows, cols, dtype):
    apart = lax.axis_size("ctx") // HEAD_GROUPS
    copies = apart - 1 + 2 * (HEAD_GROUPS - 1)
    return [
        pltpu.VMEM((max(apart - 1, 1), HEAD_GROUPS, rows, 2 * cols), dtype),
        pltpu.VMEM((HEAD_GROUPS, rows, 2 * cols), dtype),
        pltpu.VMEM((HEAD_GROUPS, rows, cols), dtype),
        pltpu.VMEM((HEAD_GROUPS, rows, 2 * cols), dtype),
        pltpu.SemaphoreType.DMA((copies,)),
        pltpu.SemaphoreType.DMA((copies,)),
        pltpu.SemaphoreType.DMA((3,)),
    ]


LANES = 128
SEGMENTS = 8
PAD = 8


def gate_cols(chunk, half):
    direction, inside = chunk // half, (chunk % half) * LANES
    first = direction * 2 * half * LANES + inside
    return first, first + half * LANES, inside


def read_gate(gates_ref, curve_ref, down, chunk, half):
    gate, cand, inside = gate_cols(chunk, half)
    zeta = jax.nn.sigmoid(
        gates_ref[down, pl.ds(gate, LANES)] - curve_ref[0:1, pl.ds(inside, LANES)]
    )
    return zeta, gates_ref[down, pl.ds(cand, LANES)] * curve_ref[1:2, pl.ds(inside, LANES)]


def scan_chunks(coef_s, term_s, rows, chunks, ahead, shifts, found):
    length = rows // SEGMENTS
    pitch = rows + 2 * PAD
    parts = 4

    def step(j, carry):
        states, prods = carry
        new_states, new_prods = [], []
        for chunk in range(chunks):
            place = j if ahead[chunk] else length - 1 - j
            base = chunk * pitch + PAD + place
            coef_at = pl.ds(base + shifts[chunk], SEGMENTS, stride=length)
            term_at = pl.ds(base, SEGMENTS, stride=length)
            coef = coef_s[coef_at, :]
            state = coef * states[chunk] + term_s[term_at, :]
            prod = coef * prods[chunk]
            term_s[term_at, :] = state
            coef_s[coef_at, :] = prod
            new_states.append(state)
            new_prods.append(prod)
        return (tuple(new_states), tuple(new_prods))

    zero = jnp.zeros((SEGMENTS, LANES), jnp.float32)
    one = jnp.ones((SEGMENTS, LANES), jnp.float32)
    found.append(((zero,) * chunks, (one,) * chunks))

    def part(number):
        span = length // parts
        found[0] = lax.fori_loop(number * span, (number + 1) * span, step, found[0], unroll=4)

    return [functools.partial(part, number) for number in range(parts)]


def block_totals(states, prods, chunk, ahead):
    carry = jnp.zeros((1, LANES), jnp.float32)
    prod = jnp.ones((1, LANES), jnp.float32)
    for segment in range(SEGMENTS) if ahead[chunk] else range(SEGMENTS - 1, -1, -1):
        row = slice(segment, segment + 1)
        carry = prods[chunk][row] * carry + states[chunk][row]
        prod = prods[chunk][row] * prod
    return prod, carry


def carry_of(totals_ref, forward_first):
    count = totals_ref.shape[0]
    mine = lax.axis_index("ctx")
    half = totals_ref.shape[2] // 2
    low = jnp.zeros((1, half), jnp.float32)
    high = jnp.zeros((1, half), jnp.float32)
    for position in range(count - 1):
        back = count - 1 - position
        first, second = (position, back) if forward_first else (back, position)
        low_ok = (first < mine) if forward_first else (first > mine)
        high_ok = (second > mine) if forward_first else (second < mine)
        low = jnp.where(
            low_ok, totals_ref[first, 0:1, :half] * low + totals_ref[first, 1:2, :half], low
        )
        high = jnp.where(
            high_ok, totals_ref[second, 0:1, half:] * high + totals_ref[second, 1:2, half:], high
        )
    return jnp.concatenate([low, high], axis=1)


def segment_carries(states, prods, chunk, ahead, entering):
    carry = entering[:, chunk * LANES : (chunk + 1) * LANES]
    carries = {}
    for segment in range(SEGMENTS) if ahead[chunk] else range(SEGMENTS - 1, -1, -1):
        row = slice(segment, segment + 1)
        carries[segment] = carry
        carry = prods[chunk][row] * carry + states[chunk][row]
    return carries


def ring_partner(step):
    count = lax.axis_size("ctx")
    return place_of("ctx", lax.rem(lax.axis_index("ctx") + count + step, count))


def greet_all():
    barrier = pltpu.get_barrier_semaphore()
    partners = [ctx_partner(gap) for gap in range(1, lax.axis_size("ctx"))] + [
        place_of("wsh", lax.bitwise_xor(lax.axis_index("wsh"), gap))
        for gap in range(1, lax.axis_size("wsh"))
    ]
    for partner in partners:
        pl.semaphore_signal(
            barrier, inc=1, device_id=partner, device_id_type=pl.DeviceIdType.MESH
        )
    pl.semaphore_wait(barrier, len(partners))


def front_kernel(slots, count, *refs):
    shards = refs[:count]
    qkv_ref, gates_ref, chars_ref, curve_ref, keep_ref, map_ref = refs[count : count + 6]
    refs = refs[count + 6 :]
    outs = refs[:count]
    q_out, kv_out, states_ref, chars_out, pooled_ref, edge_ref, root_ref = refs[count : count + 7]
    refs = refs[count + 7 :]
    gather_scratch, spread_refs, refs = refs[:3], refs[3:8], refs[8:]
    coef_s, term_s, mixed_s, totals_s, land_edge, send_sem, recv_sem = refs
    sems = (send_sem, recv_sem)
    rows, width = chars_ref.shape
    chunks = width // LANES
    half = chunks // 2
    length = rows // SEGMENTS
    pitch = rows + 2 * PAD
    ahead = [chunk < half for chunk in range(chunks)]
    mine = lax.axis_index("ctx")
    others = lax.axis_size("ctx") - 1
    toks = pooled_ref.shape[0]
    tail = edge_ref.shape[1]
    send, pass_on, wait = spread_ticks(qkv_ref, q_out, kv_out, *spread_refs)
    found, small, edges, kept = [], [], [], {}

    def prepare(chunk):
        direction = chunk // half

        def one(position, carry):
            down = pl.ds(pl.multiple_of(position * length, length), length)
            zeta, cand = read_gate(gates_ref, curve_ref, down, chunk, half)
            held = pl.ds(pl.multiple_of(chunk * pitch + PAD + position * length, 8), length)
            coef_s[held, :] = (1.0 - zeta) * keep_ref[down, direction : direction + 1]
            term_s[held, :] = zeta * cand
            return carry

        lax.fori_loop(0, SEGMENTS, one, 0)

    def send_totals():
        states, prods = found[0]
        for chunk in range(chunks):
            prod, carry = block_totals(states, prods, chunk, ahead)
            cols = pl.ds(chunk * LANES, LANES)
            totals_s[mine, 0:1, cols] = prod
            totals_s[mine, 1:2, cols] = carry
        small.extend(exchange_sums(totals_s, sems, 0))

    def count_chars():
        hits = lax.broadcasted_iota(jnp.int32, (toks, rows), 0) == map_ref[0:1, :]
        counts = jnp.sum(hits.astype(jnp.float32), axis=1, keepdims=True)
        root_ref[...] = jnp.broadcast_to(jnp.sqrt(counts), root_ref.shape)

    def enter():
        for copy in small:
            copy.wait_recv()
        entering = carry_of(totals_s, True)
        states_ref[PAD - 1 : PAD, :] = entering
        states_ref[PAD + rows : PAD + rows + 1, :] = entering
        kept["entering"] = entering

    def settle(chunk):
        states, prods = found[0]
        carries = segment_carries(states, prods, chunk, ahead, kept["entering"])
        cols = pl.ds(chunk * LANES, LANES)
        for segment in range(SEGMENTS):
            held = pl.ds(chunk * pitch + PAD + segment * length, length)
            down = pl.ds(segment * length, length)
            state = term_s[held, :] + coef_s[held, :] * carries[segment]
            states_ref[pl.ds(PAD + segment * length, length), cols] = state
            mixed = state.astype(jnp.bfloat16)
            mixed_s[down, cols] = mixed
            chars_out[down, cols] = (
                chars_ref[down, cols].astype(jnp.float32) + mixed.astype(jnp.float32)
            ).astype(jnp.bfloat16)

    def pool():
        hits = lax.broadcasted_iota(jnp.int32, (toks, rows), 0) == map_ref[0:1, :]
        pooled_ref[...] = (
            dot32(hits.astype(jnp.bfloat16), mixed_s[...]) / root_ref[:, 0:1]
        ).astype(jnp.bfloat16)
        last = pooled_ref.at[pl.ds(toks - tail, tail)]
        edges.append(remote(last, land_edge.at[0], sems, others, ring_partner(1)))
        head = pooled_ref.at[pl.ds(0, tail)]
        edges.append(remote(head, land_edge.at[1], sems, others + 1, ring_partner(-1)))
        for copy in edges:
            copy.start()

    def close():
        for copy in edges:
            copy.wait_recv()
        edge_ref[...] = land_edge[...]
        for copy in small + edges:
            copy.wait_send()

    pieces = [functools.partial(prepare, chunk) for chunk in range(chunks)]
    pieces.insert(chunks // 2, pass_on)
    pieces = pieces + scan_chunks(
        coef_s, term_s, rows, chunks, ahead, [0] * chunks, found
    )
    pieces = pieces + [send_totals, count_chars, wait, enter]
    pieces = pieces + [functools.partial(settle, chunk) for chunk in range(chunks)]
    pieces = pieces + [pool, close]
    greet_all()
    send()
    weave(
        gather_ticks(slots, shards, outs, gather_scratch[:2], gather_scratch[2], True), pieces, FRONT_SHARE
    )


def front(arrays, slots, qkv, gates, chars, curve, keep, char_map, collective):
    count = len(arrays)
    rows, width = chars.shape
    toks = qkv.shape[0]
    cols = width // HEAD_GROUPS
    ctx = lax.axis_size("ctx")
    f32, bf16 = jnp.float32, jnp.bfloat16
    hbm = pl.BlockSpec(memory_space=pl.ANY)
    whole = pl.BlockSpec(memory_space=pltpu.VMEM)
    held = pltpu.VMEM((width // LANES * (rows + 2 * PAD), LANES), f32)
    outs = pl.pallas_call(
        functools.partial(front_kernel, slots, count),
        out_shape=gather_shapes(arrays, True)
        + (
            jax.ShapeDtypeStruct((HEAD_GROUPS, toks, cols), bf16),
            jax.ShapeDtypeStruct((ctx, toks, 2 * cols), bf16),
            jax.ShapeDtypeStruct((rows + 2 * PAD, width), f32),
            jax.ShapeDtypeStruct((rows, width), bf16),
            jax.ShapeDtypeStruct((toks, width), bf16),
            jax.ShapeDtypeStruct((2, 16, width), bf16),
            jax.ShapeDtypeStruct((toks, LANES), f32),
        ),
        in_specs=[hbm] * count + [whole] * 6,
        out_specs=(hbm,) * (count + 2) + (whole,) * 5,
        scratch_shapes=gather_sems(slots, True)
        + spread_scratch(toks, cols, bf16)
        + [
            held,
            held,
            pltpu.VMEM((rows, width), bf16),
            pltpu.VMEM((ctx, 8, width), f32),
            pltpu.VMEM((2, 16, width), bf16),
            pltpu.SemaphoreType.DMA((ctx + 1,)),
            pltpu.SemaphoreType.DMA((ctx + 1,)),
        ],
        compiler_params=pltpu.CompilerParams(
            collective_id=collective, has_side_effects=True, vmem_limit_bytes=48 << 20
        ),
        name="front",
    )(*arrays, qkv, gates, chars, curve, keep, char_map)
    return [out.reshape((-1, out.shape[-1])) for out in outs[:count]], outs[count:]


def back_kernel(slots, late_slots, count, *refs):
    grads = refs[:count]
    dq_ref, dkv_ref, gates_ref, states_ref, cot_ref, taps_ref, curve_ref, keep_ref, root_ref, in_ref = refs[
        count : count + 10
    ]
    refs = refs[count + 10 :]
    outs, late_out = refs[:count], refs[count]
    heads_out, gates_out, late_grad = refs[count + 1 : count + 4]
    refs = refs[count + 4 :]
    collect_refs, refs = refs[:7], refs[7:]
    coef_s, term_s, edge_s, high_s, low_s, totals_s, stage_s = refs[:7]
    send_sem, recv_sem, stage_sem = refs[7:10]
    late_size = 3 + 1 + len([stream for slot in late_slots for stream in slot]) * (
        len(masks_of("ctx")) + 1
    )
    ticks = scatter_ticks(slots, grads, outs, refs[10 + late_size :], True)
    late_ticks = scatter_ticks(
        late_slots, [late_grad], [late_out], refs[10 : 10 + late_size], True
    )
    sems = (send_sem, recv_sem)
    rows, width = cot_ref.shape
    toks = root_ref.shape[0]
    chunks = width // LANES
    half = chunks // 2
    length = rows // SEGMENTS
    pitch = rows + 2 * PAD
    ahead = [chunk >= half for chunk in range(chunks)]
    shifts = [1 if chunk < half else -1 for chunk in range(chunks)]
    ctx = lax.axis_size("ctx")
    mine = lax.axis_index("ctx")
    others = ctx - 1
    bf16 = jnp.bfloat16
    send, add_near, write = collect_ticks(dq_ref, dkv_ref, heads_out, collect_refs)
    found, small, edges, kept = [], [], [], {}

    def open_edges():
        head = taps_ref.at[0, pl.ds(0, PAD)]
        edges.append(remote(head, edge_s.at[0], sems, others, ring_partner(-1)))
        last = taps_ref.at[2, pl.ds(toks - PAD, PAD)]
        edges.append(remote(last, edge_s.at[1], sems, others + 1, ring_partner(1)))
        for copy in edges:
            copy.start()

    def prepare(chunk):
        direction = chunk // half
        gate, _, inside = gate_cols(chunk, half)

        def one(position, carry):
            down = pl.ds(pl.multiple_of(position * length, length), length)
            zeta = jax.nn.sigmoid(
                gates_ref[down, pl.ds(gate, LANES)] - curve_ref[0:1, pl.ds(inside, LANES)]
            )
            held = pl.ds(pl.multiple_of(chunk * pitch + PAD + position * length, 8), length)
            coef_s[held, :] = (1.0 - zeta) * keep_ref[down, direction : direction + 1]
            return carry

        lax.fori_loop(0, SEGMENTS, one, 0)
        outside = chunk * pitch + (PAD + rows if chunk < half else 0)
        coef_s[pl.ds(outside, PAD), :] = jnp.ones((PAD, LANES), jnp.float32)

    def join_taps():
        for copy in edges:
            copy.wait_recv()
        token = lax.broadcasted_iota(jnp.int32, (toks, width), 0)
        outer = jnp.where(mine == ctx - 1, 0.0, edge_s[0, 0:1, :])
        after = jnp.where(token == toks - 1, outer, pltpu.roll(taps_ref[0], toks - 1, 0))
        outer = jnp.where(mine == 0, 0.0, edge_s[1, PAD - 1 : PAD, :])
        before = jnp.where(token == 0, outer, pltpu.roll(taps_ref[2], 1, 0))
        pooled_grad = (after + taps_ref[1] + before) / root_ref[:, 0:1]
        high = pooled_grad.astype(bf16)
        high_s[...] = high
        low_s[...] = (pooled_grad - high.astype(jnp.float32)).astype(bf16)

    def mix(first, last):
        def one(position, carry):
            down = pl.ds(pl.multiple_of(position * length, length), length)
            tokens = lax.broadcasted_iota(jnp.int32, (length, toks), 1).astype(jnp.float32)
            hits = (tokens == keep_ref[down, 2:3]).astype(bf16)
            mixed = cot_ref[down, :].astype(jnp.float32) + (
                dot32(hits, high_s[...]) + dot32(hits, low_s[...])
            )
            for chunk in range(chunks):
                held = pl.ds(pl.multiple_of(chunk * pitch + PAD + position * length, 8), length)
                term_s[held, :] = mixed[:, chunk * LANES : (chunk + 1) * LANES]
            return carry

        lax.fori_loop(first, last, one, 0)

    def send_totals():
        states, prods = found[0]
        for chunk in range(chunks):
            prod, carry = block_totals(states, prods, chunk, ahead)
            edge = chunk * pitch + PAD + (0 if chunk < half else rows - 1)
            own = coef_s[pl.ds(edge, 1), :]
            cols = pl.ds(chunk * LANES, LANES)
            totals_s[mine, 0:1, cols] = own * prod
            totals_s[mine, 1:2, cols] = own * carry
        small.extend(exchange_sums(totals_s, sems, 0))

    block = 3 * LANES
    group_rows = late_grad.shape[-2]
    groups_in = block // group_rows

    def weigh(down, across):
        cols = pl.ds(across * width, width)
        product = lax.dot_general(
            in_ref[:, down * block : (down + 1) * block],
            heads_out[:, across * width : (across + 1) * width],
            (((0,), (0,)), ((), ())),
            preferred_element_type=jnp.float32,
        ).astype(bf16)
        slot = (down * 3 + across) % 2
        if down * 3 + across >= 2:
            kept["stage", slot].wait()
        lead = stage_s.shape[1:-2]
        for group in range(groups_in):
            place, rest = [], group
            for size in reversed(lead):
                place.append(rest % size)
                rest = rest // size
            stage_s[(slot,) + tuple(place[::-1])] = product[
                group * group_rows : (group + 1) * group_rows
            ]
        copy = pltpu.make_async_copy(
            stage_s.at[slot],
            late_grad.at[(down,) + (slice(None),) * len(lead) + (slice(None), cols)],
            stage_sem.at[slot],
        )
        copy.start()
        kept["stage", slot] = copy

    def open_late():
        for slot in range(2):
            kept["stage", slot].wait()
        late_ticks.pop(0)()

    def enter():
        for copy in small:
            copy.wait_recv()
        kept["entering"] = carry_of(totals_s, False)

    def settle(chunk):
        states, prods = found[0]
        carries = segment_carries(states, prods, chunk, ahead, kept["entering"])
        gate, cand_at, inside = gate_cols(chunk, half)
        direction = chunk // half
        behind = -1 if chunk < half else 1
        cols = pl.ds(chunk * LANES, LANES)
        lift = curve_ref[1:2, pl.ds(inside, LANES)]
        for segment in range(SEGMENTS):
            base = chunk * pitch + PAD + segment * length
            down = pl.ds(segment * length, length)
            slope = (
                term_s[pl.ds(base, length), :]
                + coef_s[pl.ds(base + shifts[chunk], length), :] * carries[segment]
            )
            zeta, cand = read_gate(gates_ref, curve_ref, down, chunk, half)
            past = states_ref[pl.ds(PAD + segment * length + behind, length), cols]
            keep = keep_ref[down, direction : direction + 1]
            lifted = slope * zeta
            gates_out[down, pl.ds(gate, LANES)] = (
                lifted * (cand - keep * past) * (1.0 - zeta)
            ).astype(bf16)
            gates_out[down, pl.ds(cand_at, LANES)] = (lifted * lift).astype(bf16)

    def close():
        for copy in small + edges:
            copy.wait_send()

    prepares = [functools.partial(prepare, chunk) for chunk in range(chunks)]
    pieces = prepares[:half] + [add_near] + prepares[half:] + [join_taps]
    pieces = pieces + [functools.partial(mix, 0, 4), functools.partial(mix, 4, SEGMENTS), write]
    weighs = [
        functools.partial(weigh, down, across) for down in range(width // block) for across in range(3)
    ]
    scans = scan_chunks(coef_s, term_s, rows, chunks, ahead, shifts, found)
    pieces = pieces + weighs + [open_late] + scans + [send_totals, enter]
    pieces = pieces + [functools.partial(settle, chunk) for chunk in range(chunks)] + [close]
    greet_all()
    open_edges()
    send()
    total = len(ticks) + len(late_ticks) - 1
    ticks.pop(0)()
    done = 1
    for number, piece in enumerate(pieces):
        piece()
        while done < BACK_SHARE * total * (number + 1) / len(pieces) and len(ticks) > 4:
            ticks.pop(0)()
            done = done + 1
    while ticks or late_ticks:
        if late_ticks:
            late_ticks.pop(0)()
        if ticks:
            ticks.pop(0)()


def back(arrays, slots, dq, dkv, gates, states, cot, taps, curve, keep, roots, attn_in, collective):
    count = len(arrays)
    rows, width = cot.shape
    toks, cols = dq.shape[1:]
    ctx, wsh = lax.axis_size("ctx"), lax.axis_size("wsh")
    bits = len(masks_of("ctx"))
    apart = ctx // HEAD_GROUPS
    f32, bf16 = jnp.float32, jnp.bfloat16
    hbm = pl.BlockSpec(memory_space=pl.ANY)
    whole = pl.BlockSpec(memory_space=pltpu.VMEM)
    held = pltpu.VMEM((width // LANES * (rows + 2 * PAD), LANES), f32)
    shaped, shard_rows = scatter_shapes(arrays, True)
    late = jax.ShapeDtypeStruct((width, 3 * width), bf16)
    late_rows = width // (ctx * wsh)
    late_slots = slots_of([late], False)
    outs = pl.pallas_call(
        functools.partial(back_kernel, slots, late_slots, count),
        out_shape=tuple(
            jax.ShapeDtypeStruct((row, array.shape[1]), f32)
            for array, row in zip(arrays, shard_rows)
        )
        + (
            jax.ShapeDtypeStruct((late_rows, 3 * width), f32),
            jax.ShapeDtypeStruct((toks, 3 * width), bf16),
            jax.ShapeDtypeStruct(gates.shape, bf16),
            jax.ShapeDtypeStruct((2,) * bits + (wsh, late_rows, 3 * width), bf16),
        ),
        in_specs=[hbm] * (count + 2) + [whole] * 8,
        out_specs=(whole,) * (count + 3) + (hbm,),
        scratch_shapes=collect_scratch(toks, cols, bf16)
        + [
            held,
            held,
            pltpu.VMEM((2, PAD, width), f32),
            pltpu.VMEM((toks, width), bf16),
            pltpu.VMEM((toks, width), bf16),
            pltpu.VMEM((ctx, 8, width), f32),
            pltpu.VMEM((2,) + (2,) * (bits - 1) + (wsh, late_rows, width), bf16),
            pltpu.SemaphoreType.DMA((ctx + 1,)),
            pltpu.SemaphoreType.DMA((ctx + 1,)),
            pltpu.SemaphoreType.DMA((2,)),
        ]
        + scatter_scratch([late], late_slots, True)
        + scatter_scratch(arrays, slots, True),
        compiler_params=pltpu.CompilerParams(
            collective_id=collective, has_side_effects=True, vmem_limit_bytes=60 << 20
        ),
        name="back",
    )(
        *shaped,
        dq,
        dkv.reshape(HEAD_GROUPS, apart, toks, 2 * cols),
        gates,
        states,
        cot,
        taps,
        curve,
        keep,
        roots,
        attn_in,
    )
    return outs[:count], outs[count : count + 3]


def normed(values, scales):
    average = jnp.mean(values, axis=-1, keepdims=True)
    centred = values - average
    spread = jnp.mean(centred * centred, axis=-1, keepdims=True)
    return centred * lax.rsqrt(spread + 1e-05) * scales


def gelu_exact(values):
    return jax.nn.gelu(values, approximate=False)


def body(
    tokens,
    chars,
    char_token,
    doc_lengths,
    gain_attn,
    qkv_weight,
    out_weight,
    gain_char,
    gru_weight,
    conv_weight,
    gain_merge,
    merge_weight,
    up_weight,
    down_weight,
    cot_tokens,
    cot_chars,
):
    f32 = jnp.float32
    bf16 = jnp.bfloat16
    width = tokens.shape[2]
    lane = 128
    gain_block = jnp.stack([gain_attn, gain_char, gain_merge], axis=1)
    gain_block = jnp.pad(gain_block, ((0, 0), (0, lane - 3)))
    first_needed = [gru_weight, jnp.concatenate([qkv_weight, gain_block], axis=1)]
    gru_full, gains_and_qkv = gather_all(
        first_needed,
        slots_of(first_needed, True),
        True,
        0,
    )
    qkv_full = gains_and_qkv[:, : 3 * width]
    gains = jnp.transpose(gains_and_qkv[:, 3 * width :].astype(f32))
    attn_gain_f, char_gain_f, merge_gain_f = gains[0], gains[1], gains[2]
    tok_rows = tokens.shape[1]
    char_rows = chars.shape[1]
    half_width = width // 2
    seq_len = tok_rows * lax.axis_size("ctx")
    token_in = tokens[0].astype(f32)
    char_in = chars[0].astype(f32)
    char_map = char_token[0, 0]
    lengths = doc_lengths[0]
    starts = jnp.cumsum(lengths) - lengths
    positions = lax.axis_index("ctx") * tok_rows + jnp.arange(tok_rows, dtype=jnp.int32)
    doc_first = jnp.any(starts[None, :] == positions[:, None], axis=1)
    doc_last = jnp.any(starts[None, :] == positions[:, None] + 1, axis=1)
    onehot = char_map[None, :] == jnp.arange(tok_rows, dtype=jnp.int32)[:, None]
    boundary = char_map[1:] != char_map[:-1]
    first_char = jnp.concatenate([jnp.ones((1,), bool), boundary])
    last_char = jnp.concatenate([boundary, jnp.ones((1,), bool)])
    opens_doc = jnp.any(onehot & doc_first[:, None], axis=0)
    closes_doc = jnp.any(onehot & doc_last[:, None], axis=0)
    keep_fwd = 1.0 - (first_char & opens_doc).astype(f32)
    keep_bwd = 1.0 - (last_char & closes_doc).astype(f32)
    attn_in = normed(token_in, attn_gain_f).astype(bf16)
    qkv = jnp.dot(attn_in, qkv_full, preferred_element_type=f32).astype(bf16)
    elements = seq_len * width
    apart = lax.axis_size("ctx") // HEAD_GROUPS
    slot_blocks = jnp.arange(HEAD_GROUPS, dtype=jnp.int32) * apart + lax.rem(
        lax.axis_index("ctx"), apart
    )
    slot_positions = slot_blocks[:, None] * tok_rows + jnp.arange(tok_rows, dtype=jnp.int32)[None]
    before = starts[None, None, :] <= slot_positions[:, :, None]
    doc_begin = jnp.max(jnp.where(before, starts, 0), axis=2)
    doc_end = jnp.min(jnp.where(before, seq_len, starts), axis=2)
    spans = jnp.concatenate(
        [
            doc_begin[:, None, :],
            doc_end[:, None, :],
            jnp.zeros((HEAD_GROUPS, 6, tok_rows), jnp.int32),
        ],
        axis=1,
    )
    bounds = jnp.stack(
        [doc_begin[:, 0] // tok_rows, (doc_end[:, -1] + tok_rows - 1) // tok_rows], axis=1
    )
    char_low = normed(char_in, char_gain_f).astype(bf16)
    gates = jnp.dot(char_low, gru_full, preferred_element_type=f32)
    ramp = jnp.arange(half_width, dtype=f32) / (half_width - 1)
    shift = (1.0 + math.log(char_rows * lax.axis_size("ctx"))) * ramp
    curve = jnp.pad(jnp.stack([shift, jnp.exp(0.5 * shift)]), ((0, 6), (0, 0)))
    keep = jnp.stack([keep_fwd, keep_bwd, char_map.astype(f32)], axis=1)
    keep = jnp.pad(keep, ((0, 0), (0, lane - 3)))
    later = [conv_weight, out_weight, merge_weight, up_weight, down_weight]
    gathered, fronts = front(
        later, slots_of(later, True), qkv, gates, chars[0], curve, keep, char_map[None, :], 1
    )
    conv_full, out_full, merge_full, up_full, down_full = gathered
    q_heads, kv_heads, states, out_chars, pooled, edges, roots = fronts
    o_heads, exact_heads, log_heads = attend(bounds, q_heads, kv_heads, spans)
    attn_out, proj, resid, sums = join_heads(o_heads, tokens[0], out_full, elements, 6)
    mine = lax.axis_index("ctx")
    edge_rows = edges.shape[1]
    padded = jnp.concatenate(
        [
            jnp.where(mine == 0, 0.0, edges[0, edge_rows - 1 :]).astype(bf16),
            pooled,
            jnp.where(mine == lax.axis_size("ctx") - 1, 0.0, edges[1, :1]).astype(bf16),
        ],
        axis=0,
    )
    conv_out = jnp.zeros((tok_rows, width), f32)
    for kernel in range(3):
        conv_out = conv_out + jnp.dot(
            padded[kernel : kernel + tok_rows],
            conv_full[:, kernel * width : (kernel + 1) * width],
            preferred_element_type=f32,
        )
    merge_in = normed(resid, merge_gain_f).astype(bf16)
    merge_pre = jnp.dot(merge_in, merge_full, preferred_element_type=f32) + conv_out
    merged = gelu_exact(merge_pre).astype(bf16)
    up_pre = jnp.dot(merged, up_full, preferred_element_type=f32)
    up_act = gelu_exact(up_pre).astype(bf16)
    out_tok = (resid + jnp.dot(up_act, down_full, preferred_element_type=f32)).astype(bf16)
    cot_tok = cot_tokens[0]
    cot_tok_f = cot_tok.astype(f32)
    cot_chr_f = cot_chars[0].astype(f32)
    grad_down = jnp.einsum("tf,td->fd", up_act, cot_tok, preferred_element_type=f32)
    grad_act = jnp.einsum("td,fd->tf", cot_tok, down_full, preferred_element_type=f32)
    _, gelu_up_back = jax.vjp(gelu_exact, up_pre)
    grad_up_pre = gelu_up_back(grad_act)[0].astype(bf16)
    grad_up = jnp.einsum("tc,tf->cf", merged, grad_up_pre, preferred_element_type=f32)
    grad_merged = jnp.einsum("tf,cf->tc", grad_up_pre, up_full, preferred_element_type=f32)
    _, gelu_merge_back = jax.vjp(gelu_exact, merge_pre)
    grad_pre = gelu_merge_back(grad_merged)[0].astype(bf16)
    grad_merge = jnp.einsum("tc,te->ce", merge_in, grad_pre, preferred_element_type=f32)
    grad_merge_in = jnp.einsum("te,ce->tc", grad_pre, merge_full, preferred_element_type=f32)
    grad_conv = jnp.concatenate(
        [
            jnp.einsum(
                "tc,te->ce",
                padded[kernel : kernel + tok_rows],
                grad_pre,
                preferred_element_type=f32,
            )
            for kernel in range(3)
        ],
        axis=1,
    )
    grad_taps = jnp.stack(
        [
            jnp.einsum(
                "te,ce->tc",
                grad_pre,
                conv_full[:, kernel * width : (kernel + 1) * width],
                preferred_element_type=f32,
            )
            for kernel in range(3)
        ]
    )
    _, merge_norm_back = jax.vjp(normed, resid, merge_gain_f)
    grad_resid_norm, grad_merge_gain = merge_norm_back(grad_merge_in)
    grad_resid = cot_tok_f + grad_resid_norm
    down_shard, grad_stream, grad_proj, g_heads = part_heads(
        grad_down.astype(bf16), grad_resid, proj, tokens[0], out_full, sums, elements, 7
    )
    grad_out_proj = jnp.einsum("tc,te->ce", attn_out, grad_proj, preferred_element_type=f32)
    dq_heads, dkv_heads = attend_back(
        bounds, q_heads, kv_heads, g_heads, exact_heads, log_heads, spans
    )
    early = [grad_up, grad_conv, grad_out_proj, grad_merge]
    early = [part.astype(bf16) for part in early]
    early_shards, backs = back(
        early,
        slots_of(early, False),
        dq_heads,
        dkv_heads,
        gates,
        states,
        cot_chars[0],
        grad_taps,
        curve,
        keep,
        roots,
        attn_in,
        4,
    )
    up_shard, conv_shard, out_shard, merge_shard = early_shards
    qkv_shard, grad_qkv_low, grad_gates = backs
    grad_gru = jnp.einsum("tc,tg->cg", char_low, grad_gates, preferred_element_type=f32)
    grad_char_norm = jnp.einsum("tg,cg->tc", grad_gates, gru_full, preferred_element_type=f32)
    _, char_norm_back = jax.vjp(normed, char_in, char_gain_f)
    grad_char_in, grad_char_gain = char_norm_back(grad_char_norm)
    grad_chars_out = (cot_chr_f + grad_char_in).astype(bf16)
    grad_attn_in = jnp.einsum("tg,cg->tc", grad_qkv_low, qkv_full, preferred_element_type=f32)
    _, attn_norm_back = jax.vjp(normed, token_in, attn_gain_f)
    grad_token_in, grad_attn_gain = attn_norm_back(grad_attn_in)
    grad_tokens_out = (grad_stream + grad_token_in).astype(bf16)
    gain_grads = jnp.stack([grad_attn_gain, grad_char_gain, grad_merge_gain], axis=1)
    gain_grads = jnp.pad(gain_grads, ((0, 0), (0, lane - 3)))
    late = [jnp.concatenate([grad_gru, gain_grads], axis=1).astype(bf16)]
    gru_shard = scatter_sums(late, slots_of(late, False), True, 5, f32)[0]
    gain_shard = gru_shard[:, 2 * width :]
    shards = (
        gain_shard[:, 0],
        qkv_shard,
        out_shard,
        gain_shard[:, 1],
        gru_shard[:, : 2 * width],
        conv_shard,
        gain_shard[:, 2],
        merge_shard,
        up_shard,
        down_shard,
    )
    return (
        out_tok[None],
        out_chars[None],
        grad_tokens_out[None],
        grad_chars_out[None],
        shards[0],
        shards[1],
        shards[2],
        shards[3],
        shards[4],
        shards[5],
        shards[6],
        shards[7],
        shards[8],
        shards[9],
    )


def solution(mesh):
    in_specs = (
        P("wsh", "ctx", None),
        P("wsh", "ctx", None),
        P("wsh", "ctx", None),
        P("wsh", None),
        P(("ctx", "wsh")),
        P(("ctx", "wsh"), None),
        P(("ctx", "wsh"), None),
        P(("ctx", "wsh")),
        P(("ctx", "wsh"), None),
        P(("ctx", "wsh"), None),
        P(("ctx", "wsh")),
        P(("ctx", "wsh"), None),
        P(("ctx", "wsh"), None),
        P(("ctx", "wsh"), None),
        P("wsh", "ctx", None),
        P("wsh", "ctx", None),
    )
    out_specs = (
        P("wsh", "ctx", None),
        P("wsh", "ctx", None),
        P("wsh", "ctx", None),
        P("wsh", "ctx", None),
        P(("ctx", "wsh")),
        P(("ctx", "wsh"), None),
        P(("ctx", "wsh"), None),
        P(("ctx", "wsh")),
        P(("ctx", "wsh"), None),
        P(("ctx", "wsh"), None),
        P(("ctx", "wsh")),
        P(("ctx", "wsh"), None),
        P(("ctx", "wsh"), None),
        P(("ctx", "wsh"), None),
    )
    return jax.shard_map(body, mesh=mesh, in_specs=in_specs, out_specs=out_specs, check_vma=False)
```
